256 devices in a mesh: dp: 2 (over x_lo), ctx: 128 (over y, z, x_hi, core).
Axes of the slice: x: 4 (x_hi: 2, x_lo: 2; x = x_hi * 2 + x_lo), y: 4, z: 8, core: 2. Of those that a mesh axis runs over, the one named last changes fastest.
Arguments:
- hidden_in: bfloat16 [2, 16384, 2048], P('dp', 'ctx'), may hold values from -6 to 6
- qk_weight: bfloat16 [2048, 256], replicated, may hold values from -0.125 to 0.125
- conv_weight: float32 [3, 256], replicated, may hold values from -3 to 3
- values: bfloat16 [2, 16384, 512], P('dp', 'ctx'), may hold values from -6 to 6
- gate_in: bfloat16 [2, 16384, 512], P('dp', 'ctx'), may hold values from -6 to 6
- cotangent: bfloat16 [2, 16384, 512], P('dp', 'ctx'), may hold values from -6 to 6
Outputs:
- output: bfloat16 [2, 16384, 512], P('dp', 'ctx')
- grad_hidden: bfloat16 [2, 16384, 2048], P('dp', 'ctx')
- grad_values: bfloat16 [2, 16384, 512], P('dp', 'ctx')
- grad_gate: bfloat16 [2, 16384, 512], P('dp', 'ctx')
- grad_qk_weight: bfloat16 [2048, 256], replicated
The draws below stay inside these ranges and needn't reach their ends.
All inputs are finite; a program needn't handle non-finite values.
Results may differ from the reference program's by a relative error of at most 0.008.
Values may be sent and summed in bfloat16 or wider, within the bound.
No kernel may reach another device: no remote copies, remote signals or barrier semaphores. Data moves between devices by JAX's collectives and lax.ppermute only.
A program may use at most 192 MiB of HBM per device.

```python
import math
import jax
import jax.numpy as jnp
import numpy as np
from jax import lax

D = 2048
H = 8
F = 16
DV = 64
FT = 153
KCONV = 3
TOK_DEV = 128
SEQS = 2
LEN = 16384


def shard_levels(key, shape, split, least, high):
    def one(position, shards_of):
        steps = jax.random.uniform(jax.random.fold_in(jax.random.fold_in(key, 6), position), (shards_of,), jnp.float32, least / len(split), high / len(split))
        return jnp.repeat(jnp.exp(steps), shape[position] // shards_of).reshape((-1,) + (1,) * (len(shape) - position - 1))

    loudness = one(*split[0])
    for cut in split[1:]:
        loudness = loudness * one(*cut)
    return loudness


def bell_draw(rng, dims, spread, limit, pieces=(), held_as=jnp.bfloat16):
    level = shard_levels(rng, dims, pieces, -0.22, 0.18) if pieces else 1.0
    values = jax.random.normal(rng, dims, jnp.float32) * spread * level
    return jnp.minimum(jnp.maximum(values, -limit), limit).astype(held_as)


def setup_inputs(seed: int = 0) -> dict:
    streams_of = jax.random.split(jax.random.key(seed), 7)
    return {
        "hidden_in": bell_draw(streams_of[0], (SEQS, LEN, D), 1.0, 6.0, ((0, 2), (1, 128))),
        "qk_weight": bell_draw(streams_of[1], (D, 2 * H * F), D ** -0.5, 0.125),
        "conv_weight": bell_draw(streams_of[2], (KCONV, 2 * H * F), 0.6, 3.0, (), jnp.float32),
        "values": bell_draw(streams_of[3], (SEQS, LEN, H * DV), 1.0, 6.0, ((0, 2), (1, 128))),
        "gate_in": bell_draw(streams_of[4], (SEQS, LEN, H * DV), 1.0, 6.0, ((0, 2), (1, 128))),
        "cotangent": bell_draw(streams_of[5], (SEQS, LEN, H * DV), 1.0, 6.0, ((0, 2), (1, 128))),
    }


def pair_table(feat_width):
    table = np.zeros((feat_width * feat_width, feat_width * (feat_width + 1) // 2), np.float32)
    column = 0
    for first in range(feat_width):
        for second in range(first, feat_width):
            factor = 1.0 / math.sqrt(feat_width)
            if first == second:
                factor = factor / math.sqrt(2.0)
            table[first * feat_width + second, column] = factor
            column += 1
    return table

def taylor_map(matrix):
    feat_width = matrix.shape[-1]
    outer = (matrix[..., :, None] * matrix[..., None, :]).reshape(matrix.shape[:-1] + (feat_width * feat_width,))
    second = jnp.dot(outer, pair_table(feat_width), precision=lax.Precision.HIGHEST)
    ones = jnp.ones(matrix.shape[:-1] + (1,), matrix.dtype)
    return jnp.concatenate([ones, matrix * feat_width ** (-0.25), second], -1)

def kernel_weights(queries, keys_mat):
    length = queries.shape[0]
    scores = jnp.einsum('thf,shf->hts', queries, keys_mat, precision=lax.Precision.HIGHEST) * queries.shape[-1] ** (-0.5)
    rows_idx = lax.broadcasted_iota(jnp.int32, (length, length), 0)
    cols_idx = lax.broadcasted_iota(jnp.int32, (length, length), 1)
    causal = rows_idx >= cols_idx
    return jnp.where(causal[None], 1.0 + scores + 0.5 * scores * scores, 0.0)

def block_out(queries, keys_mat, value_matrix, incoming_numerator, norm_in):
    weights_mat = kernel_weights(queries, keys_mat)
    query_feature_rows = taylor_map(queries)
    numerator = jnp.einsum('hts,shd->thd', weights_mat, value_matrix, precision=lax.Precision.HIGHEST)
    numerator = numerator + jnp.einsum('jfn,fna->jfa', query_feature_rows, incoming_numerator, precision=lax.Precision.HIGHEST)
    denom = lax.optimization_barrier(jnp.sum(weights_mat, 2)).T + jnp.einsum('thm,hm->th', query_feature_rows, norm_in, precision=lax.Precision.HIGHEST)
    return numerator / denom[..., None]

def block_state(keys_mat, value_matrix):
    key_feature_rows = taylor_map(keys_mat)
    return (jnp.einsum('oxa,oxn->xan', key_feature_rows, value_matrix, precision=lax.Precision.HIGHEST), lax.optimization_barrier(jnp.sum(key_feature_rows, 0)))

def attention_core(queries, keys_mat, value_matrix):
    total = queries.shape[0]
    blocks = total // TOK_DEV
    query_blocks = queries.reshape(blocks, TOK_DEV, H, F)
    key_blocks = keys_mat.reshape(blocks, TOK_DEV, H, F)
    value_blocks = value_matrix.reshape(blocks, TOK_DEV, H, DV)
    start = (jnp.zeros((H, FT, DV), queries.dtype), jnp.zeros((H, FT), queries.dtype))

    def advance(carry, block):
        incoming_numerator, norm_in = carry
        query_b, key_b, value_b = block
        result = block_out(query_b, key_b, value_b, incoming_numerator, norm_in)
        numer_new, norm_new = block_state(key_b, value_b)
        return ((incoming_numerator + numer_new, norm_in + norm_new), result)
    unused, results = lax.scan(advance, start, (query_blocks, key_blocks, value_blocks))
    return results.reshape(total, H, DV)

def short_conv(projected, conv_weight):
    length = projected.shape[0]
    padded = jnp.concatenate([jnp.zeros((KCONV - 1, projected.shape[1]), projected.dtype), projected], 0)
    total = conv_weight[0] * padded[KCONV - 1:KCONV - 1 + length]
    for offset in range(1, KCONV):
        total = total + conv_weight[offset] * padded[KCONV - 1 - offset:KCONV - 1 - offset + length]
    return total

def short_conv_back(grads, conv_weight):
    length = grads.shape[0]
    padded = jnp.concatenate([grads, jnp.zeros((KCONV - 1, grads.shape[1]), grads.dtype)], 0)
    total = conv_weight[0] * padded[0:length]
    for offset in range(1, KCONV):
        total = total + conv_weight[offset] * padded[offset:offset + length]
    return total

def reference(hidden_in, qk_weight, conv_weight, values, gate_in, cotangent):
    outputs = []
    grads_hidden = []
    grads_value = []
    grads_gate = []
    weight_total = jnp.zeros((D, 2 * H * F), jnp.float32)
    for seq in range(SEQS):
        tokens = hidden_in[seq]
        projected = jnp.dot(tokens, qk_weight, preferred_element_type=jnp.float32).astype(jnp.bfloat16)
        mixed = short_conv(projected.astype(jnp.float32), conv_weight)
        queries = mixed[:, :H * F].reshape(LEN, H, F)
        keys_mat = mixed[:, H * F:].reshape(LEN, H, F)
        value_matrix = values[seq].astype(jnp.float32).reshape(LEN, H, DV)
        attended, pull = jax.vjp(attention_core, queries, keys_mat, value_matrix)
        attended = attended.reshape(LEN, H * DV)
        gate_f = gate_in[seq].astype(jnp.float32)
        sigm = jax.nn.sigmoid(gate_f)
        gate_act = gate_f * sigm
        outputs.append((attended * gate_act).astype(jnp.bfloat16))
        upstream = cotangent[seq].astype(jnp.float32)
        grads_gate.append((upstream * attended * sigm * (1.0 + gate_f * (1.0 - sigm))).astype(jnp.bfloat16))
        grad_attended = (upstream * gate_act).reshape(LEN, H, DV)
        grad_query, grad_key, value_gradient_rows = pull(grad_attended)
        grads_value.append(value_gradient_rows.reshape(LEN, H * DV).astype(jnp.bfloat16))
        grad_mixed = jnp.concatenate([grad_query.reshape(LEN, H * F), grad_key.reshape(LEN, H * F)], 1)
        grad_projected = short_conv_back(grad_mixed, conv_weight).astype(jnp.bfloat16)
        grads_hidden.append(jnp.dot(grad_projected, qk_weight.T, preferred_element_type=jnp.float32).astype(jnp.bfloat16))
        weight_total = weight_total + jnp.dot(tokens.T, grad_projected, preferred_element_type=jnp.float32)
    return (jnp.stack(outputs), jnp.stack(grads_hidden), jnp.stack(grads_value), jnp.stack(grads_gate), weight_total.astype(jnp.bfloat16))
```

```python
import math

import jax
import jax.numpy as jnp
from jax import lax
from jax.experimental import pallas as pl
from jax.experimental.pallas import tpu as pltpu
from jax.sharding import Mesh, PartitionSpec as P

H = 8
F = 16
DV = 64
KCONV = 3
TOK = 128
ROWS = 256
FEAT = 160
SENT = FEAT + 16
WIDE = 2
f32 = jnp.float32
bf16 = jnp.bfloat16
NN = ((1,), (0,))
NT = ((1,), (1,))
TN = ((0,), (0,))


def mm(a, b, dims):
    return lax.dot_general(a, b, (dims, ((), ())), preferred_element_type=f32)


def halves(x):
    high = x.astype(bf16)
    return high, (x - high.astype(f32)).astype(bf16)


def mm3(a, b, dims):
    (ah, al), (bh, bl) = a, b
    return mm(ah, bh, dims) + (mm(ah, bl, dims) + mm(al, bh, dims))


def feature_scale(d):
    return F**-0.5 * (math.sqrt(0.5) if d == 0 else 1.0)


def up(x, d):
    return x if d == 0 else jnp.concatenate([x[d:], x[:d]], 0)


def features(x):
    rows = [x * F**-0.25]
    for d in range(F // 2):
        rows.append(x * up(x, d) * feature_scale(d))
    half = F // 2
    rows.append(x[:half] * x[half:] * feature_scale(half))
    row = lax.broadcasted_iota(jnp.int32, (8, x.shape[1]), 0)
    rows.append(jnp.where(row == 0, 1.0, 0.0))
    return jnp.concatenate(rows, 0)


def features_back(x, grads):
    total = grads[:F] * F**-0.25
    half = F // 2
    for d in range(half):
        part = grads[F * (d + 1) : F * (d + 2)] * feature_scale(d)
        total = total + part * up(x, d) + up(part * x, (F - d) % F)
    part = grads[F * (half + 1) : F * (half + 1) + half] * feature_scale(half)
    return total + jnp.concatenate([part * x[half:], part * x[:half]], 0)


def pack_state(state):
    high, low = halves(state)
    high, low = high.astype(f32), low.astype(f32)
    lane = lax.broadcasted_iota(jnp.int32, (FEAT, 2 * DV), 1)
    main = jnp.where(lane < DV, high, pltpu.roll(low, DV, 1))
    small = lane[:16]
    sums = jnp.zeros((16, 2 * DV), f32)
    for i in range(FEAT // 16):
        sums = jnp.where(small == i, high[16 * i : 16 * i + 16, DV : DV + 1], sums)
        sums = jnp.where(small == i + 16, low[16 * i : 16 * i + 16, DV : DV + 1], sums)
    return jnp.concatenate([main, sums], 0).astype(bf16)


def unpack_state(total):
    main = total[:FEAT]
    main = main + pltpu.roll(main, DV, 1)
    sums = total[FEAT:]
    sums = sums + pltpu.roll(sums, 2 * DV - 16, 1)
    column = jnp.concatenate([sums[:, i : i + 1] for i in range(FEAT // 16)], 0)
    lane = lax.broadcasted_iota(jnp.int32, (FEAT, 2 * DV), 1)
    return jnp.where(lane < DV, main, jnp.where(lane == DV, column, 0.0))


def wide_values(values):
    row = lax.broadcasted_iota(jnp.int32, (DV, values.shape[1]), 0)
    return jnp.concatenate([values, jnp.where(row == 0, 1.0, 0.0).astype(bf16)], 0)


def rows_of(ref, chunk, start, size):
    return jnp.concatenate(
        [ref[WIDE * chunk + i, start : start + size] for i in range(WIDE)], 1
    )


def pack_kernel(projected, halo, conv, values, gate, cot, out):
    now = projected[...].astype(f32)
    before = halo[...].astype(f32)
    mixed = (
        conv[0:1] * now
        + conv[1:2] * jnp.concatenate([before[1:2], now[:-1]], 0)
        + conv[2:3] * jnp.concatenate([before, now[:-2]], 0)
    )
    high, low = halves(mixed.T)
    v, g, c = values[...].T, gate[...].T, cot[...].T
    width = H * F
    for h in range(H):
        q, k = slice(F * h, F * (h + 1)), slice(width + F * h, width + F * (h + 1))
        out[h, 0:16] = high[q]
        out[h, 16:32] = high[k]
        out[h, 32:48] = low[q]
        out[h, 48:64] = low[k]
        cols = slice(DV * h, DV * (h + 1))
        out[h, 64:128] = v[cols]
        out[h, 128:192] = g[cols]
        out[h, 192:256] = c[cols]


def state_kernel(data, out):
    total = jnp.zeros((FEAT, 2 * DV), f32)
    for c in range(H // WIDE):
        key = rows_of(data, c, 16, 16).astype(f32) + rows_of(data, c, 48, 16).astype(f32)
        high, low = halves(features(key))
        v = wide_values(rows_of(data, c, 64, DV))
        total = total + (mm(high, v, NT) + mm(low, v, NT))
    out[...] = pack_state(total)


def main_kernel(place, data, states, out, gq, gk, gv, parts, sent):
    here = place[0]
    length = TOK * WIDE
    total = jnp.zeros((SENT, 2 * DV), f32)
    for b in range(states.shape[0]):
        total = total + states[b].astype(f32) * (b < here).astype(f32)
    state = unpack_state(total)
    k_at = lax.broadcasted_iota(jnp.int32, (length, length), 0)
    q_at = lax.broadcasted_iota(jnp.int32, (length, length), 1)
    causal = k_at <= q_at
    whole = jnp.zeros((FEAT, 2 * DV), f32)
    for c in range(H // WIDE):
        qh, kh = rows_of(data, c, 0, 16), rows_of(data, c, 16, 16)
        ql, kl = rows_of(data, c, 32, 16), rows_of(data, c, 48, 16)
        q, k = qh.astype(f32) + ql.astype(f32), kh.astype(f32) + kl.astype(f32)
        v = wide_values(rows_of(data, c, 64, DV))
        g = rows_of(data, c, 128, DV).astype(f32)
        cot = rows_of(data, c, 192, DV).astype(f32)
        scores = mm(
            jnp.concatenate([kh, kh, kl], 0), jnp.concatenate([qh, ql, qh], 0), TN
        ) * F**-0.5
        weights = halves(jnp.where(causal, 1.0 + scores + 0.5 * scores * scores, 0.0))
        q_feat, k_feat = halves(features(q)), halves(features(k))
        split_state = halves(state)
        numer = mm(v, weights[0], NN) + mm(v, weights[1], NN) + mm3(split_state, q_feat, TN)
        inverse = 1.0 / numer[DV : DV + 1]
        attended = numer[:DV] * inverse
        sig = jax.nn.sigmoid(g)
        act = g * sig
        result = (attended * act).astype(bf16)
        g_gate = (cot * attended * sig * (1.0 + g * (1.0 - sig))).astype(bf16)
        g_att = cot * act
        g_num = g_att * inverse
        g_den = -jnp.sum(g_att * attended, 0, keepdims=True) * inverse
        row = lax.broadcasted_iota(jnp.int32, (DV, length), 0)
        grads = halves(jnp.concatenate([g_num, jnp.where(row == 0, g_den, 0.0)], 0))
        g_weights = mm(v, grads[0], TN) + mm(v, grads[1], TN)
        g_scores = halves(jnp.where(causal, g_weights * (1.0 + scores), 0.0) * F**-0.5)
        g_query = mm3((kh, kl), g_scores, NN) + features_back(q, mm3(split_state, grads, NN))
        g_key = mm3((qh, ql), g_scores, NT)
        g_value = mm3((grads[0][:DV], grads[1][:DV]), weights, NT)
        part = mm3(q_feat, grads, NT)
        whole = whole + part
        parts[c] = part
        state = state + (mm(k_feat[0], v, NT) + mm(k_feat[1], v, NT))
        for i in range(WIDE):
            cols = slice(TOK * i, TOK * (i + 1))
            out[WIDE * c + i, 0:DV] = result[:, cols]
            out[WIDE * c + i, DV : 2 * DV] = g_gate[:, cols]
        gq[c] = g_query
        gk[c] = g_key
        gv[c] = g_value
    sent[...] = pack_state(whole)


def back_kernel(place, data, states, done, gq, gk, gv, parts, out):
    here = place[0]
    total = jnp.zeros((SENT, 2 * DV), f32)
    for b in range(states.shape[0]):
        total = total + states[b].astype(f32) * (b > here).astype(f32)
    state = unpack_state(total)
    for c in reversed(range(H // WIDE)):
        k = rows_of(data, c, 16, 16).astype(f32) + rows_of(data, c, 48, 16).astype(f32)
        v = wide_values(rows_of(data, c, 64, DV))
        k_feat = halves(features(k))
        split_state = halves(state)
        g_feat = mm(split_state[0], v, NN) + mm(split_state[1], v, NN)
        g_key = halves(gk[c] + features_back(k, g_feat))
        g_query = halves(gq[c])
        g_value = (gv[c] + mm3(split_state, k_feat, TN)[:DV]).astype(bf16)
        state = state + parts[c]
        for i in range(WIDE):
            cols = slice(TOK * i, TOK * (i + 1))
            b = WIDE * c + i
            out[b, 0 : 2 * DV] = done[b]
            out[b, 128:192] = g_value[:, cols]
            out[b, 192:208] = g_query[0][:, cols]
            out[b, 208:224] = g_key[0][:, cols]
            out[b, 224:240] = g_query[1][:, cols]
            out[b, 240:256] = g_key[1][:, cols]


def unpack_kernel(data, output, g_gate, g_value, g_mixed):
    for target, start in ((output, 0), (g_gate, 64), (g_value, 128)):
        target[...] = jnp.concatenate([data[h, start : start + DV] for h in range(H)], 0).T
    rows = [
        data[h, at : at + F].astype(f32) + data[h, at + 32 : at + 32 + F].astype(f32)
        for at in (192, 208)
        for h in range(H)
    ]
    g_mixed[...] = jnp.concatenate(rows, 0).T


def call(kernel, name, out_shape, *args, scalars=0):
    specs = [pl.BlockSpec(memory_space=pltpu.SMEM)] * scalars
    specs += [pl.BlockSpec(memory_space=pltpu.VMEM)] * (len(args) - scalars)
    outs = jax.tree.map(lambda s: pl.BlockSpec(memory_space=pltpu.VMEM), out_shape)
    return pl.pallas_call(
        kernel, name=name, out_shape=out_shape, in_specs=specs, out_specs=outs
    )(*args)


def shape(dims, kind):
    return jax.ShapeDtypeStruct(dims, kind)


def everyone(x, axis):
    count = lax.axis_size(axis)
    return lax.all_to_all(jnp.broadcast_to(x[None], (count,) + x.shape), axis, 0, 0, tiled=True)


def body(hidden_in, qk_weight, conv_weight, values, gate_in, cotangent):
    tokens = hidden_in[0]
    blocks = lax.axis_size(("s", "g"))
    chunks, width = H // WIDE, TOK * WIDE
    place = lax.axis_index("s").astype(jnp.int32).reshape(1)
    projected = jnp.dot(tokens, qk_weight, preferred_element_type=f32).astype(bf16)
    halo = lax.ppermute(
        projected[TOK - (KCONV - 1) :], ("s", "g"), [(i, i + 1) for i in range(blocks - 1)]
    )
    packed = call(
        pack_kernel,
        "pack",
        shape((H, ROWS, TOK), bf16),
        projected,
        halo,
        conv_weight,
        values[0],
        gate_in[0],
        cotangent[0],
    )
    data = lax.all_to_all(packed, "g", 0, 0, tiled=True)
    own = call(state_kernel, "state", shape((SENT, 2 * DV), bf16), data)
    done, gq, gk, gv, parts, sent = call(
        main_kernel,
        "main",
        (
            shape((H, 2 * DV, TOK), bf16),
            shape((chunks, F, width), f32),
            shape((chunks, F, width), f32),
            shape((chunks, DV, width), f32),
            shape((chunks, FEAT, 2 * DV), f32),
            shape((SENT, 2 * DV), bf16),
        ),
        place,
        data,
        everyone(own, "s"),
        scalars=1,
    )
    back = call(
        back_kernel,
        "back",
        shape((H, ROWS, TOK), bf16),
        place,
        data,
        everyone(sent, "s"),
        done,
        gq,
        gk,
        gv,
        parts,
        scalars=1,
    )
    back = lax.all_to_all(back, "g", 0, 0, tiled=True)
    output, grad_gate, grad_values, grad_mixed = call(
        unpack_kernel,
        "unpack",
        (
            shape((TOK, H * DV), bf16),
            shape((TOK, H * DV), bf16),
            shape((TOK, H * DV), bf16),
            shape((TOK, 2 * H * F), f32),
        ),
        back,
    )
    later = lax.ppermute(
        grad_mixed[: KCONV - 1], ("s", "g"), [(i + 1, i) for i in range(blocks - 1)]
    )
    extended = jnp.concatenate([grad_mixed, later], 0)
    grad_projected = conv_weight[0] * extended[:TOK]
    for j in range(1, KCONV):
        grad_projected = grad_projected + conv_weight[j] * extended[j : j + TOK]
    grad_projected = grad_projected.astype(bf16)
    grad_hidden = jnp.dot(grad_projected, qk_weight.T, preferred_element_type=f32).astype(bf16)
    local_term = jnp.einsum("tr,tc->rc", tokens, grad_projected, preferred_element_type=f32)
    grad_qk_weight = lax.psum(local_term, ("dp", "s", "g")).astype(bf16)
    return output[None], grad_hidden[None], grad_values[None], grad_gate[None], grad_qk_weight


def solution(mesh):
    pairs, blocks = mesh.devices.shape
    fine = Mesh(mesh.devices.reshape(pairs, blocks // H, H), ("dp", "s", "g"))
    split = P("dp", ("s", "g"), None)
    return jax.shard_map(
        body,
        mesh=fine,
        in_specs=(split, P(), P(), split, split, split),
        out_specs=(split, split, split, split, P()),
        check_vma=False,
    )
```

```python
import math

import jax
import jax.numpy as jnp
from jax import lax
from jax.experimental import pallas as pl
from jax.experimental.pallas import tpu as pltpu
from jax.sharding import Mesh, PartitionSpec as P

H = 8
F = 16
DV = 64
KCONV = 3
TOK = 128
ROWS = 256
FEAT = 160
SENT = FEAT // 2 + 16
WIDE = 2
f32 = jnp.float32
bf16 = jnp.bfloat16
NN = ((1,), (0,))
NT = ((1,), (1,))
TN = ((0,), (0,))


def mm(a, b, dims):
    return lax.dot_general(a, b, (dims, ((), ())), preferred_element_type=f32)


def halves(x):
    high = x.astype(bf16)
    return high, (x - high.astype(f32)).astype(bf16)


def mm3(a, b, dims):
    (ah, al), (bh, bl) = a, b
    return mm(ah, bh, dims) + (mm(ah, bl, dims) + mm(al, bh, dims))


def feature_scale(d):
    return F**-0.5 * (math.sqrt(0.5) if d == 0 else 1.0)


def up(x, d):
    return x if d == 0 else jnp.concatenate([x[d:], x[:d]], 0)


def features(x):
    rows = [x * F**-0.25]
    for d in range(F // 2):
        rows.append(x * up(x, d) * feature_scale(d))
    half = F // 2
    rows.append(x[:half] * x[half:] * feature_scale(half))
    row = lax.broadcasted_iota(jnp.int32, (8, x.shape[1]), 0)
    rows.append(jnp.where(row == 0, 1.0, 0.0))
    return jnp.concatenate(rows, 0)


def features_back(x, grads):
    total = grads[:F] * F**-0.25
    half = F // 2
    for d in range(half):
        part = grads[F * (d + 1) : F * (d + 2)] * feature_scale(d)
        total = total + part * up(x, d) + up(part * x, (F - d) % F)
    part = grads[F * (half + 1) : F * (half + 1) + half] * feature_scale(half)
    return total + jnp.concatenate([part * x[half:], part * x[:half]], 0)


def pack_state(state):
    half = FEAT // 2
    lane = lax.broadcasted_iota(jnp.int32, (half, 2 * DV), 1)
    main = jnp.where(lane < DV, state[:half], pltpu.roll(state[half:], DV, 1))
    high, low = halves(state)
    high, low = high.astype(f32), low.astype(f32)
    small = lane[:16]
    sums = jnp.zeros((16, 2 * DV), f32)
    for i in range(FEAT // 16):
        sums = jnp.where(small == i, high[16 * i : 16 * i + 16, DV : DV + 1], sums)
        sums = jnp.where(small == i + 16, low[16 * i : 16 * i + 16, DV : DV + 1], sums)
    return jnp.concatenate([main, sums], 0).astype(bf16)


def unpack_state(total):
    half = FEAT // 2
    main = total[:half]
    main = jnp.concatenate([main, pltpu.roll(main, DV, 1)], 0)
    sums = total[half:]
    sums = sums + pltpu.roll(sums, 2 * DV - 16, 1)
    column = jnp.concatenate([sums[:, i : i + 1] for i in range(FEAT // 16)], 0)
    lane = lax.broadcasted_iota(jnp.int32, (FEAT, 2 * DV), 1)
    return jnp.where(lane < DV, main, jnp.where(lane == DV, column, 0.0))


def repeat_into(out, value):
    for i in range(out.shape[0]):
        out[i] = value


def wide_values(values):
    row = lax.broadcasted_iota(jnp.int32, (DV, values.shape[1]), 0)
    return jnp.concatenate([values, jnp.where(row == 0, 1.0, 0.0).astype(bf16)], 0)


def rows_of(ref, chunk, start, size):
    return jnp.concatenate(
        [ref[WIDE * chunk + i, start : start + size] for i in range(WIDE)], 1
    )


def slice_kernel(tokens, states, out):
    del states
    cols = out.shape[2]
    for h in range(H):
        out[h] = tokens[:, cols * h : cols * (h + 1)]


def sum_kernel(data, out):
    total = data[0].astype(f32)
    for i in range(1, data.shape[0]):
        total = total + data[i].astype(f32)
    repeat_into(out, total.astype(bf16))


def pack_kernel(projected, halo, conv, values, gate, cot, out):
    now = projected[...].astype(f32)
    before = halo[...].astype(f32)
    mixed = (
        conv[0:1] * now
        + conv[1:2] * jnp.concatenate([before[1:2], now[:-1]], 0)
        + conv[2:3] * jnp.concatenate([before, now[:-2]], 0)
    )
    high, low = halves(mixed.T)
    v, g, c = values[...].T, gate[...].T, cot[...].T
    width = H * F
    for h in range(H):
        q, k = slice(F * h, F * (h + 1)), slice(width + F * h, width + F * (h + 1))
        out[h, 0:16] = high[q]
        out[h, 16:32] = high[k]
        out[h, 32:48] = low[q]
        out[h, 48:64] = low[k]
        cols = slice(DV * h, DV * (h + 1))
        out[h, 64:128] = v[cols]
        out[h, 128:192] = g[cols]
        out[h, 192:256] = c[cols]


def state_kernel(data, out):
    total = jnp.zeros((FEAT, 2 * DV), f32)
    for c in range(H // WIDE):
        key = rows_of(data, c, 16, 16).astype(f32) + rows_of(data, c, 48, 16).astype(f32)
        high, low = halves(features(key))
        v = wide_values(rows_of(data, c, 64, DV))
        total = total + (mm(high, v, NT) + mm(low, v, NT))
    repeat_into(out, pack_state(total))


def main_kernel(place, data, states, out, gq, gk, gv, parts, sent):
    here = place[0]
    length = TOK * WIDE
    total = jnp.zeros((SENT, 2 * DV), f32)
    for b in range(states.shape[0]):
        total = total + states[b].astype(f32) * (b < here).astype(f32)
    state = unpack_state(total)
    k_at = lax.broadcasted_iota(jnp.int32, (length, length), 0)
    q_at = lax.broadcasted_iota(jnp.int32, (length, length), 1)
    causal = k_at <= q_at
    whole = jnp.zeros((FEAT, 2 * DV), f32)
    for c in range(H // WIDE):
        qh, kh = rows_of(data, c, 0, 16), rows_of(data, c, 16, 16)
        ql, kl = rows_of(data, c, 32, 16), rows_of(data, c, 48, 16)
        q, k = qh.astype(f32) + ql.astype(f32), kh.astype(f32) + kl.astype(f32)
        v = wide_values(rows_of(data, c, 64, DV))
        g = rows_of(data, c, 128, DV).astype(f32)
        cot = rows_of(data, c, 192, DV).astype(f32)
        scores = mm(
            jnp.concatenate([kh, kh, kl], 0), jnp.concatenate([qh, ql, qh], 0), TN
        ) * F**-0.5
        weights = halves(jnp.where(causal, 1.0 + scores + 0.5 * scores * scores, 0.0))
        q_feat, k_feat = halves(features(q)), halves(features(k))
        split_state = halves(state)
        numer = mm(v, weights[0], NN) + mm(v, weights[1], NN) + mm3(split_state, q_feat, TN)
        inverse = 1.0 / numer[DV : DV + 1]
        attended = numer[:DV] * inverse
        sig = jax.nn.sigmoid(g)
        act = g * sig
        result = (attended * act).astype(bf16)
        g_gate = (cot * attended * sig * (1.0 + g * (1.0 - sig))).astype(bf16)
        g_att = cot * act
        g_num = g_att * inverse
        g_den = -jnp.sum(g_att * attended, 0, keepdims=True) * inverse
        row = lax.broadcasted_iota(jnp.int32, (DV, length), 0)
        grads = halves(jnp.concatenate([g_num, jnp.where(row == 0, g_den, 0.0)], 0))
        g_weights = mm(v, grads[0], TN) + mm(v, grads[1], TN)
        g_scores = halves(jnp.where(causal, g_weights * (1.0 + scores), 0.0) * F**-0.5)
        g_query = mm3((kh, kl), g_scores, NN) + features_back(q, mm3(split_state, grads, NN))
        g_key = mm3((qh, ql), g_scores, NT)
        g_value = mm3((grads[0][:DV], grads[1][:DV]), weights, NT)
        part = mm3(q_feat, grads, NT)
        whole = whole + part
        parts[c] = part
        state = state + (mm(k_feat[0], v, NT) + mm(k_feat[1], v, NT))
        for i in range(WIDE):
            cols = slice(TOK * i, TOK * (i + 1))
            out[WIDE * c + i, 0:DV] = result[:, cols]
            out[WIDE * c + i, DV : 2 * DV] = g_gate[:, cols]
        gq[c] = g_query
        gk[c] = g_key
        gv[c] = g_value
    repeat_into(sent, pack_state(whole))


def back_kernel(place, data, states, done, gq, gk, gv, parts, out, mixed):
    here = place[0]
    total = jnp.zeros((SENT, 2 * DV), f32)
    for b in range(states.shape[0]):
        total = total + states[b].astype(f32) * (b > here).astype(f32)
    state = unpack_state(total)
    for c in reversed(range(H // WIDE)):
        k = rows_of(data, c, 16, 16).astype(f32) + rows_of(data, c, 48, 16).astype(f32)
        v = wide_values(rows_of(data, c, 64, DV))
        k_feat = halves(features(k))
        split_state = halves(state)
        g_feat = mm(split_state[0], v, NN) + mm(split_state[1], v, NN)
        g_key = gk[c] + features_back(k, g_feat)
        g_value = (gv[c] + mm3(split_state, k_feat, TN)[:DV]).astype(bf16)
        state = state + parts[c]
        cols = slice(TOK * WIDE * c, TOK * WIDE * (c + 1))
        mixed[0:F, cols] = gq[c]
        mixed[F : 2 * F, cols] = g_key
        for i in range(WIDE):
            b = WIDE * c + i
            out[b, 0 : 2 * DV] = done[b]
            out[b, 2 * DV : 3 * DV] = g_value[:, TOK * i : TOK * (i + 1)]


def conv_back_kernel(place, mixed, later, conv, out, columns):
    head = place[0]
    padded = jnp.concatenate([conv[...], jnp.zeros((8 - KCONV, 2 * H * F), f32)], 0)
    columns[...] = padded.T
    at = pl.multiple_of(F * head, F)
    taps = jnp.concatenate([columns[pl.ds(at, F)], columns[pl.ds(H * F + at, F)]], 0)
    now, after = mixed[...], later[...]
    total = (
        taps[:, 0:1] * now
        + taps[:, 1:2] * jnp.concatenate([now[:, 1:], after[:, 0:1]], 1)
        + taps[:, 2:3] * jnp.concatenate([now[:, 2:], after], 1)
    ).astype(bf16)
    for i in range(H):
        for b in range(H):
            out[i, b] = total[:, TOK * b : TOK * (b + 1)]


def weight_kernel(place, grads, tokens, out, own):
    here = place[0]
    total = jnp.concatenate(
        [
            jnp.concatenate(
                [grads[h, b, at : at + F] for at in (0, F) for h in range(H)], 0
            )
            for b in range(H)
        ],
        1,
    )
    own[...] = jnp.concatenate(
        [grads[h, here, at : at + F] for at in (0, F) for h in range(H)], 0
    )
    result = lax.dot_general(
        tokens[...], total, (((0,), (1,)), ((), ())), preferred_element_type=f32
    ).astype(bf16)
    count, rows = out.shape[:2]
    for i in range(count):
        out[i] = result[rows * i : rows * (i + 1)]


def unpack_kernel(data, output, g_gate, g_value):
    for target, start in ((output, 0), (g_gate, 64), (g_value, 128)):
        target[...] = jnp.concatenate([data[h, start : start + DV] for h in range(H)], 0).T


def call(kernel, name, out_shape, *args, scalars=0, waits=0, scratch=()):
    specs = [pl.BlockSpec(memory_space=pltpu.SMEM)] * scalars
    specs += [pl.BlockSpec(memory_space=pltpu.VMEM)] * (len(args) - scalars - waits)
    specs += [pl.BlockSpec(memory_space=pl.ANY)] * waits
    outs = jax.tree.map(lambda s: pl.BlockSpec(memory_space=pltpu.VMEM), out_shape)
    return pl.pallas_call(
        kernel, name=name, out_shape=out_shape, in_specs=specs, out_specs=outs,
        scratch_shapes=scratch,
    )(*args)


def shape(dims, kind):
    return jax.ShapeDtypeStruct(dims, kind)


def swap(x, axis):
    return lax.all_to_all(x, axis, 0, 0, tiled=True)


def everyone(x, axis):
    return swap(jnp.broadcast_to(x[None], (lax.axis_size(axis),) + x.shape), axis)


def body(hidden_in, qk_weight, conv_weight, values, gate_in, cotangent):
    tokens = hidden_in[0]
    supers = lax.axis_size("s")
    blocks = supers * H
    others = lax.axis_size(("dp", "s"))
    model = tokens.shape[1]
    chunks, width = H // WIDE, TOK * WIDE
    place = lax.axis_index("s").astype(jnp.int32).reshape(1)
    head = lax.axis_index("g").astype(jnp.int32).reshape(1)
    projected = jnp.dot(tokens, qk_weight, preferred_element_type=f32).astype(bf16)
    halo = lax.ppermute(
        projected[TOK - (KCONV - 1) :], ("s", "g"), [(i, i + 1) for i in range(blocks - 1)]
    )
    packed = call(
        pack_kernel,
        "pack",
        shape((H, ROWS, TOK), bf16),
        projected,
        halo,
        conv_weight,
        values[0],
        gate_in[0],
        cotangent[0],
    )
    data = swap(packed, "g")
    own = call(state_kernel, "state", shape((supers, SENT, 2 * DV), bf16), data)
    states = swap(own, "s")
    columns = swap(
        call(
            slice_kernel,
            "slices",
            shape((H, TOK, model // H), bf16),
            tokens,
            states,
            waits=1,
        ),
        "g",
    )
    done, gq, gk, gv, parts, sent = call(
        main_kernel,
        "main",
        (
            shape((H, 2 * DV, TOK), bf16),
            shape((chunks, F, width), f32),
            shape((chunks, F, width), f32),
            shape((chunks, DV, width), f32),
            shape((chunks, FEAT, 2 * DV), f32),
            shape((supers, SENT, 2 * DV), bf16),
        ),
        place,
        data,
        states,
        scalars=1,
    )
    sent, columns = lax.optimization_barrier((sent, columns))
    back, grad_mixed = call(
        back_kernel,
        "back",
        (shape((H, 3 * DV, TOK), bf16), shape((2 * F, H * TOK), f32)),
        place,
        data,
        swap(sent, "s"),
        done,
        gq,
        gk,
        gv,
        parts,
        scalars=1,
    )
    later = lax.ppermute(
        grad_mixed[:, : KCONV - 1], "s", [(i + 1, i) for i in range(supers - 1)]
    )
    grads = call(
        conv_back_kernel,
        "conv_back",
        shape((H, H, 2 * F, TOK), bf16),
        head,
        grad_mixed,
        later,
        conv_weight,
        scalars=1,
        scratch=(pltpu.VMEM((2 * H * F, 8), f32),),
    )
    partial, own_grad = call(
        weight_kernel,
        "weight",
        (shape((others, model // H // others, 2 * H * F), bf16), shape((2 * H * F, TOK), bf16)),
        head,
        swap(grads, "g"),
        columns.reshape(H * TOK, model // H),
        scalars=1,
    )
    summed = call(
        sum_kernel, "sum", shape(partial.shape, bf16), swap(partial, ("dp", "s"))
    )
    slices = swap(summed, ("dp", "s")).reshape(model // H, 2 * H * F)
    grad_qk_weight = everyone(slices, "g").reshape(model, 2 * H * F)
    output, grad_gate, grad_values = call(
        unpack_kernel,
        "unpack",
        (shape((TOK, H * DV), bf16),) * 3,
        swap(back, "g"),
    )
    grad_hidden = lax.dot_general(
        own_grad, qk_weight, (((0,), (1,)), ((), ())), preferred_element_type=f32
    ).astype(bf16)
    return output[None], grad_hidden[None], grad_values[None], grad_gate[None], grad_qk_weight


def solution(mesh):
    pairs, blocks = mesh.devices.shape
    fine = Mesh(mesh.devices.reshape(pairs, blocks // H, H), ("dp", "s", "g"))
    split = P("dp", ("s", "g"), None)
    return jax.shard_map(
        body,
        mesh=fine,
        in_specs=(split, P(), P(), split, split, split),
        out_specs=(split, split, split, split, P()),
        check_vma=False,
    )
```

```python
import math

import jax
import jax.numpy as jnp
from jax import lax
from jax.experimental import pallas as pl
from jax.experimental.pallas import tpu as pltpu
from jax.sharding import Mesh, PartitionSpec as P

H = 8
F = 16
DV = 64
KCONV = 3
TOK = 128
ROWS = 256
PAD = 16
HID = TOK + PAD
FEAT = 160
SENT = FEAT // 2 + 16
WIDE = 2
FIRST = 2 * F * (H + 1)
f32 = jnp.float32
bf16 = jnp.bfloat16
NN = ((1,), (0,))
NT = ((1,), (1,))
TN = ((0,), (0,))


def mm(a, b, dims):
    return lax.dot_general(a, b, (dims, ((), ())), preferred_element_type=f32)


def halves(x):
    high = x.astype(bf16)
    return high, (x - high.astype(f32)).astype(bf16)


def mm3(a, b, dims):
    (ah, al), (bh, bl) = a, b
    return mm(ah, bh, dims) + (mm(ah, bl, dims) + mm(al, bh, dims))


def feature_scale(d):
    return F**-0.5 * (math.sqrt(0.5) if d == 0 else 1.0)


def up(x, d):
    return x if d == 0 else jnp.concatenate([x[d:], x[:d]], 0)


def features(x):
    rows = [x * F**-0.25]
    for d in range(F // 2):
        rows.append(x * up(x, d) * feature_scale(d))
    half = F // 2
    rows.append(x[:half] * x[half:] * feature_scale(half))
    row = lax.broadcasted_iota(jnp.int32, (8, x.shape[1]), 0)
    rows.append(jnp.where(row == 0, 1.0, 0.0))
    return jnp.concatenate(rows, 0)


def features_back(x, grads):
    total = grads[:F] * F**-0.25
    half = F // 2
    for d in range(half):
        part = grads[F * (d + 1) : F * (d + 2)] * feature_scale(d)
        total = total + part * up(x, d) + up(part * x, (F - d) % F)
    part = grads[F * (half + 1) : F * (half + 1) + half] * feature_scale(half)
    return total + jnp.concatenate([part * x[half:], part * x[:half]], 0)


def pack_state(state):
    half = FEAT // 2
    lane = lax.broadcasted_iota(jnp.int32, (half, 2 * DV), 1)
    main = jnp.where(lane < DV, state[:half], pltpu.roll(state[half:], DV, 1))
    high, low = halves(state)
    high, low = high.astype(f32), low.astype(f32)
    small = lane[:16]
    sums = jnp.zeros((16, 2 * DV), f32)
    for i in range(FEAT // 16):
        sums = jnp.where(small == i, high[16 * i : 16 * i + 16, DV : DV + 1], sums)
        sums = jnp.where(small == i + 16, low[16 * i : 16 * i + 16, DV : DV + 1], sums)
    return jnp.concatenate([main, sums], 0).astype(bf16)


def unpack_state(total):
    half = FEAT // 2
    main = total[:half]
    main = jnp.concatenate([main, pltpu.roll(main, DV, 1)], 0)
    sums = total[half:]
    sums = sums + pltpu.roll(sums, 2 * DV - 16, 1)
    column = jnp.concatenate([sums[:, i : i + 1] for i in range(FEAT // 16)], 0)
    lane = lax.broadcasted_iota(jnp.int32, (FEAT, 2 * DV), 1)
    return jnp.where(lane < DV, main, jnp.where(lane == DV, column, 0.0))


def repeat_into(out, value):
    for i in range(out.shape[0]):
        out[i] = value


def wide_values(values):
    row = lax.broadcasted_iota(jnp.int32, (DV, values.shape[1]), 0)
    return jnp.concatenate([values, jnp.where(row == 0, 1.0, 0.0).astype(bf16)], 0)


def rows_of(ref, chunk, start, size):
    return jnp.concatenate(
        [ref[WIDE * chunk + i, start : start + size] for i in range(WIDE)], 1
    )


def sum_kernel(data, out):
    total = data[0].astype(f32)
    for i in range(1, data.shape[0]):
        total = total + data[i].astype(f32)
    repeat_into(out, total.astype(bf16))


def pack_kernel(tokens, halo, weight, conv, values, gate, cot, out):
    x = tokens[...]
    edge = jnp.concatenate([halo[...], jnp.zeros((PAD - (KCONV - 1), x.shape[1]), bf16)], 0)
    w = weight[...]
    now = mm(x, w, NN).astype(bf16).astype(f32)
    before = mm(edge, w, NN).astype(bf16).astype(f32)[: KCONV - 1]
    mixed = (
        conv[0:1] * now
        + conv[1:2] * jnp.concatenate([before[1:2], now[:-1]], 0)
        + conv[2:3] * jnp.concatenate([before, now[:-2]], 0)
    )
    high, low = halves(mixed.T)
    v, g, c = values[...].T, gate[...].T, cot[...].T
    width = H * F
    for h in range(H):
        q, k = slice(F * h, F * (h + 1)), slice(width + F * h, width + F * (h + 1))
        out[h, 0:16] = high[q]
        out[h, 16:32] = high[k]
        out[h, 32:48] = low[q]
        out[h, 48:64] = low[k]
        cols = slice(DV * h, DV * (h + 1))
        out[h, 64:128] = v[cols]
        out[h, 128:192] = g[cols]
        out[h, 192:256] = c[cols]
        for i in range(x.shape[1] // H // 128):
            at = ROWS + HID * i
            cols = slice(x.shape[1] // H * h + 128 * i, x.shape[1] // H * h + 128 * (i + 1))
            out[h, at : at + TOK] = x[:, cols]
            out[h, at + TOK : at + HID] = edge[:, cols]


def state_kernel(data, out):
    total = jnp.zeros((FEAT, 2 * DV), f32)
    for c in range(H // WIDE):
        key = rows_of(data, c, 16, 16).astype(f32) + rows_of(data, c, 48, 16).astype(f32)
        high, low = halves(features(key))
        v = wide_values(rows_of(data, c, 64, DV))
        total = total + (mm(high, v, NT) + mm(low, v, NT))
    repeat_into(out, pack_state(total))


def main_kernel(place, data, states, out, gq, gk, gv, parts, sent):
    here = place[0]
    length = TOK * WIDE
    total = jnp.zeros((SENT, 2 * DV), f32)
    for b in range(states.shape[0]):
        total = total + states[b].astype(f32) * (b < here).astype(f32)
    state = unpack_state(total)
    k_at = lax.broadcasted_iota(jnp.int32, (length, length), 0)
    q_at = lax.broadcasted_iota(jnp.int32, (length, length), 1)
    causal = k_at <= q_at
    whole = jnp.zeros((FEAT, 2 * DV), f32)
    for c in range(H // WIDE):
        qh, kh = rows_of(data, c, 0, 16), rows_of(data, c, 16, 16)
        ql, kl = rows_of(data, c, 32, 16), rows_of(data, c, 48, 16)
        q, k = qh.astype(f32) + ql.astype(f32), kh.astype(f32) + kl.astype(f32)
        v = wide_values(rows_of(data, c, 64, DV))
        g = rows_of(data, c, 128, DV).astype(f32)
        cot = rows_of(data, c, 192, DV).astype(f32)
        scores = mm(
            jnp.concatenate([kh, kh, kl], 0), jnp.concatenate([qh, ql, qh], 0), TN
        ) * F**-0.5
        weights = halves(jnp.where(causal, 1.0 + scores + 0.5 * scores * scores, 0.0))
        q_feat, k_feat = halves(features(q)), halves(features(k))
        split_state = halves(state)
        numer = mm(v, weights[0], NN) + mm(v, weights[1], NN) + mm3(split_state, q_feat, TN)
        inverse = 1.0 / numer[DV : DV + 1]
        attended = numer[:DV] * inverse
        sig = jax.nn.sigmoid(g)
        act = g * sig
        result = (attended * act).astype(bf16)
        g_gate = (cot * attended * sig * (1.0 + g * (1.0 - sig))).astype(bf16)
        g_att = cot * act
        g_num = g_att * inverse
        g_den = -jnp.sum(g_att * attended, 0, keepdims=True) * inverse
        row = lax.broadcasted_iota(jnp.int32, (DV, length), 0)
        grads = halves(jnp.concatenate([g_num, jnp.where(row == 0, g_den, 0.0)], 0))
        g_weights = mm(v, grads[0], TN) + mm(v, grads[1], TN)
        g_scores = halves(jnp.where(causal, g_weights * (1.0 + scores), 0.0) * F**-0.5)
        g_query = mm3((kh, kl), g_scores, NN) + features_back(q, mm3(split_state, grads, NN))
        g_key = mm3((qh, ql), g_scores, NT)
        g_value = mm3((grads[0][:DV], grads[1][:DV]), weights, NT)
        part = mm3(q_feat, grads, NT)
        whole = whole + part
        parts[c] = part
        state = state + (mm(k_feat[0], v, NT) + mm(k_feat[1], v, NT))
        for i in range(WIDE):
            cols = slice(TOK * i, TOK * (i + 1))
            out[WIDE * c + i, 0:DV] = result[:, cols]
            out[WIDE * c + i, DV : 2 * DV] = g_gate[:, cols]
        gq[c] = g_query
        gk[c] = g_key
        gv[c] = g_value
    repeat_into(sent, pack_state(whole))


def back_kernel(place, data, states, done, gq, gk, gv, parts, conv, out, columns):
    here, head = place[0], place[1]
    padded = jnp.concatenate([conv[...], jnp.zeros((8 - KCONV, 2 * H * F), f32)], 0)
    columns[...] = padded.T
    at = pl.multiple_of(F * head, F)
    taps = jnp.concatenate([columns[pl.ds(at, F)], columns[pl.ds(H * F + at, F)]], 0)
    after = jnp.zeros((2 * F, 2), f32)
    length = TOK * WIDE
    total = jnp.zeros((SENT, 2 * DV), f32)
    for b in range(states.shape[0]):
        total = total + states[b].astype(f32) * (b > here).astype(f32)
    state = unpack_state(total)
    for c in reversed(range(H // WIDE)):
        k = rows_of(data, c, 16, 16).astype(f32) + rows_of(data, c, 48, 16).astype(f32)
        v = wide_values(rows_of(data, c, 64, DV))
        k_feat = halves(features(k))
        split_state = halves(state)
        g_feat = mm(split_state[0], v, NN) + mm(split_state[1], v, NN)
        g_key = gk[c] + features_back(k, g_feat)
        g_value = (gv[c] + mm3(split_state, k_feat, TN)[:DV]).astype(bf16)
        state = state + parts[c]
        now = jnp.concatenate([gq[c], g_key], 0)
        total = (
            taps[:, 0:1] * now
            + taps[:, 1:2] * jnp.concatenate([now[:, 1:], after[:, 0:1]], 1)
            + taps[:, 2:3] * jnp.concatenate([now[:, 2:], after], 1)
        ).astype(bf16)
        after = now[:, 0:2]
        for i in range(WIDE):
            cols = slice(TOK * i, TOK * (i + 1))
            b = WIDE * c + i
            out[b, FIRST : FIRST + 2 * DV] = done[b]
            out[b, FIRST + 2 * DV : FIRST + 3 * DV] = g_value[:, cols]
            for dest in range(H):
                out[dest, 2 * F * b : 2 * F * (b + 1)] = total[:, cols]
    edge = jnp.concatenate(
        [
            taps[:, 2:3] * after[:, 0:1],
            taps[:, 1:2] * after[:, 0:1] + taps[:, 2:3] * after[:, 1:2],
            jnp.zeros((2 * F, TOK - 2), f32),
        ],
        1,
    ).astype(bf16)
    for dest in range(H):
        out[dest, 2 * F * H : FIRST] = edge


def stacked(grads, block):
    return jnp.concatenate(
        [
            grads[h, pl.ds(2 * F * block + at, F)]
            for at in (0, F)
            for h in range(H)
        ],
        0,
    )


def weight_kernel(place, grads, data, out, own, edge):
    blocks = [stacked(grads, b) for b in range(H + 1)]
    own[...] = stacked(grads, place[1])
    edge[...] = blocks[H]
    total = jnp.concatenate(blocks[:H], 1)
    count, rows = out.shape[:2]
    parts = count * rows // 128
    for i in range(parts):
        at = ROWS + HID * i
        tokens = jnp.concatenate([data[b, at : at + TOK] for b in range(H)], 0)
        before = data[0, at + TOK : at + HID]
        result = (
            mm(tokens, total.T, TN) + mm(before, blocks[H].T[:PAD], TN)
        ).astype(bf16)
        for j in range(count // parts):
            out[i * (count // parts) + j] = result[rows * j : rows * (j + 1)]


def hidden_kernel(place, own, edge, weight, out):
    last = (place[1] == H - 1).astype(f32)
    later = pltpu.roll(edge[...].astype(f32), TOK - (KCONV - 1), 1) * last
    grads = (own[...].astype(f32) + later).astype(bf16)
    out[...] = mm(grads.T, weight[...], NT).astype(bf16)


def unpack_kernel(data, output, g_gate, g_value):
    for i, target in enumerate((output, g_gate, g_value)):
        at = FIRST + DV * i
        target[...] = jnp.concatenate([data[h, at : at + DV] for h in range(H)], 0).T


def call(kernel, name, out_shape, *args, scalars=0, waits=0, scratch=()):
    specs = [pl.BlockSpec(memory_space=pltpu.SMEM)] * scalars
    specs += [pl.BlockSpec(memory_space=pltpu.VMEM)] * (len(args) - scalars - waits)
    specs += [pl.BlockSpec(memory_space=pl.ANY)] * waits
    outs = jax.tree.map(lambda s: pl.BlockSpec(memory_space=pltpu.VMEM), out_shape)
    return pl.pallas_call(
        kernel, name=name, out_shape=out_shape, in_specs=specs, out_specs=outs,
        scratch_shapes=scratch,
    )(*args)


def shape(dims, kind):
    return jax.ShapeDtypeStruct(dims, kind)


def swap(x, axis):
    return lax.all_to_all(x, axis, 0, 0, tiled=True)


def everyone(x, axis):
    return swap(jnp.broadcast_to(x[None], (lax.axis_size(axis),) + x.shape), axis)


def body(hidden_in, qk_weight, conv_weight, values, gate_in, cotangent):
    tokens = hidden_in[0]
    supers = lax.axis_size("s")
    blocks = supers * H
    others = lax.axis_size(("dp", "s"))
    model = tokens.shape[1]
    chunks, width = H // WIDE, TOK * WIDE
    place = jnp.stack([lax.axis_index("s"), lax.axis_index("g")]).astype(jnp.int32)
    halo = lax.ppermute(
        tokens[TOK - (KCONV - 1) :], ("s", "g"), [(i, i + 1) for i in range(blocks - 1)]
    )
    packed = call(
        pack_kernel,
        "pack",
        shape((H, ROWS + HID * (model // H // 128), TOK), bf16),
        tokens,
        halo,
        qk_weight,
        conv_weight,
        values[0],
        gate_in[0],
        cotangent[0],
    )
    data = swap(packed, "g")
    own = call(state_kernel, "state", shape((supers, SENT, 2 * DV), bf16), data)
    done, gq, gk, gv, parts, sent = call(
        main_kernel,
        "main",
        (
            shape((H, 2 * DV, TOK), bf16),
            shape((chunks, F, width), f32),
            shape((chunks, F, width), f32),
            shape((chunks, DV, width), f32),
            shape((chunks, FEAT, 2 * DV), f32),
            shape((supers, SENT, 2 * DV), bf16),
        ),
        place,
        data,
        swap(own, "s"),
        scalars=1,
    )
    back = call(
        back_kernel,
        "back",
        shape((H, FIRST + 3 * DV, TOK), bf16),
        place,
        data,
        swap(sent, "s"),
        done,
        gq,
        gk,
        gv,
        parts,
        conv_weight,
        scalars=1,
        scratch=(pltpu.VMEM((2 * H * F, 8), f32),),
    )
    back = swap(back, "g")
    partial, own_grad, edge = call(
        weight_kernel,
        "weight",
        (
            shape((others, model // H // others, 2 * H * F), bf16),
            shape((2 * H * F, TOK), bf16),
            shape((2 * H * F, TOK), bf16),
        ),
        place,
        back,
        data,
        scalars=1,
    )
    summed = call(
        sum_kernel, "sum", shape(partial.shape, bf16), swap(partial, ("dp", "s"))
    )
    slices = swap(summed, ("dp", "s")).reshape(model // H, 2 * H * F)
    grad_qk_weight = everyone(slices, "g").reshape(model, 2 * H * F)
    output, grad_gate, grad_values = call(
        unpack_kernel, "unpack", (shape((TOK, H * DV), bf16),) * 3, back
    )
    later = lax.ppermute(edge, "s", [(i + 1, i) for i in range(supers - 1)])
    grad_hidden = call(
        hidden_kernel,
        "hidden",
        shape((TOK, model), bf16),
        place,
        own_grad,
        later,
        qk_weight,
        scalars=1,
    )
    return output[None], grad_hidden[None], grad_values[None], grad_gate[None], grad_qk_weight


def solution(mesh):
    pairs, blocks = mesh.devices.shape
    fine = Mesh(mesh.devices.reshape(pairs, blocks // H, H), ("dp", "s", "g"))
    split = P("dp", ("s", "g"), None)
    return jax.shard_map(
        body,
        mesh=fine,
        in_specs=(split, P(), P(), split, split, split),
        out_specs=(split, split, split, split, P()),
        check_vma=False,
    )
```

```python
import math

import jax
import jax.numpy as jnp
from jax import lax
from jax.experimental import pallas as pl
from jax.experimental.pallas import tpu as pltpu
from jax.sharding import Mesh, PartitionSpec as P

H = 8
F = 16
DV = 64
KCONV = 3
TOK = 128
ROWS = 2 * F + 3 * DV
AT_V, AT_G, AT_C = 2 * F, 2 * F + DV, 2 * F + 2 * DV
FEAT = 160
SENT = FEAT // 2 + 16
WIDE = 2
FIRST = 2 * F * H
SPARE = 32
f32 = jnp.float32
bf16 = jnp.bfloat16
NN = ((1,), (0,))
NT = ((1,), (1,))
TN = ((0,), (0,))


def mm(a, b, dims):
    return lax.dot_general(a, b, (dims, ((), ())), preferred_element_type=f32)


def halves(x):
    high = x.astype(bf16)
    return high, (x - high.astype(f32)).astype(bf16)


def mm3(a, b, dims):
    (ah, al), (bh, bl) = a, b
    return mm(ah, bh, dims) + (mm(ah, bl, dims) + mm(al, bh, dims))


def feature_scale(d):
    return F**-0.5 * (math.sqrt(0.5) if d == 0 else 1.0)


def up(x, d):
    return x if d == 0 else jnp.concatenate([x[d:], x[:d]], 0)


def features(x):
    rows = [x * F**-0.25]
    for d in range(F // 2):
        rows.append(x * up(x, d) * feature_scale(d))
    half = F // 2
    rows.append(x[:half] * x[half:] * feature_scale(half))
    row = lax.broadcasted_iota(jnp.int32, (8, x.shape[1]), 0)
    rows.append(jnp.where(row == 0, 1.0, 0.0))
    return jnp.concatenate(rows, 0)


def features_back(x, grads):
    total = grads[:F] * F**-0.25
    half = F // 2
    for d in range(half):
        part = grads[F * (d + 1) : F * (d + 2)] * feature_scale(d)
        total = total + part * up(x, d) + up(part * x, (F - d) % F)
    part = grads[F * (half + 1) : F * (half + 1) + half] * feature_scale(half)
    return total + jnp.concatenate([part * x[half:], part * x[:half]], 0)


def pack_state(state, extra):
    half = FEAT // 2
    lane = lax.broadcasted_iota(jnp.int32, (half, 2 * DV), 1)
    main = jnp.where(lane < DV, state[:half], pltpu.roll(state[half:], DV, 1))
    high, low = halves(state)
    high, low = high.astype(f32), low.astype(f32)
    small = lane[:16]
    sums = jnp.zeros((16, 2 * DV), f32)
    for i in range(FEAT // 16):
        sums = jnp.where(small == i, high[16 * i : 16 * i + 16, DV : DV + 1], sums)
        sums = jnp.where(small == i + 16, low[16 * i : 16 * i + 16, DV : DV + 1], sums)
    for i, column in enumerate(extra):
        sums = jnp.where(small == SPARE + i, column.astype(f32), sums)
    return jnp.concatenate([main, sums], 0).astype(bf16)


def unpack_state(total):
    half = FEAT // 2
    main = total[:half]
    main = jnp.concatenate([main, pltpu.roll(main, DV, 1)], 0)
    sums = total[half:]
    sums = sums + pltpu.roll(sums, 2 * DV - 16, 1)
    column = jnp.concatenate([sums[:, i : i + 1] for i in range(FEAT // 16)], 0)
    lane = lax.broadcasted_iota(jnp.int32, (FEAT, 2 * DV), 1)
    return jnp.where(lane < DV, main, jnp.where(lane == DV, column, 0.0))


def repeat_into(out, value):
    for i in range(out.shape[0]):
        out[i] = value


def wide_values(values):
    row = lax.broadcasted_iota(jnp.int32, (DV, values.shape[1]), 0)
    return jnp.concatenate([values, jnp.where(row == 0, 1.0, 0.0).astype(bf16)], 0)


def rows_of(ref, chunk, start, size):
    return jnp.concatenate(
        [ref[WIDE * chunk + i, start : start + size] for i in range(WIDE)], 1
    )


def head_taps(conv, columns, head):
    padded = jnp.concatenate([conv[...], jnp.zeros((8 - KCONV, 2 * H * F), f32)], 0)
    columns[...] = padded.T
    at = pl.multiple_of(F * head, F)
    return jnp.concatenate([columns[pl.ds(at, F)], columns[pl.ds(H * F + at, F)]], 0)


def convolve(now, before, taps):
    return (
        taps[:, 0:1] * now
        + taps[:, 1:2] * jnp.concatenate([before[:, 1:2], now[:, :-1]], 1)
        + taps[:, 2:3] * jnp.concatenate([before, now[:, :-2]], 1)
    )


def first_tokens(states, taps):
    rows, lanes = F, 2 * DV
    lane = lax.broadcasted_iota(jnp.int32, (rows, lanes), 1)
    raw, vals = jnp.zeros((rows, lanes), f32), jnp.zeros((rows, lanes), f32)
    for b in range(states.shape[0]):
        tile = states[b, FEAT // 2 : SENT].astype(f32)
        here = (lane >= 8 * b) & (lane < 8 * (b + 1))
        raw = jnp.where(here, pltpu.roll(tile, (8 * b - SPARE) % lanes, 1), raw)
        vals = jnp.where(here, pltpu.roll(tile, (8 * b - SPARE - 8) % lanes, 1), vals)
    prev = jnp.where(lane < 8, 0.0, pltpu.roll(raw, 8, 1))
    one = jnp.where(
        lane % 4 == 0, pltpu.roll(prev, lanes - 3, 1), pltpu.roll(raw, 1, 1)
    )
    two = pltpu.roll(prev, lanes - 2, 1)
    q, k = (
        t[:, 0:1] * raw + t[:, 1:2] * one + t[:, 2:3] * two for t in (taps[:F], taps[F:])
    )
    v = jnp.concatenate(
        [vals if j == 0 else pltpu.roll(vals, lanes - 2 * j, 1) for j in range(DV // F)], 0
    )
    return q, k, v


def sum_kernel(data, out):
    total = data[0].astype(f32)
    for i in range(1, data.shape[0]):
        total = total + data[i].astype(f32)
    repeat_into(out, total.astype(bf16))


def pack_kernel(tokens, weight, values, gate, cot, out):
    x = tokens[...]
    projected = mm(x, weight[...], NN).T.astype(bf16)
    v, g, c = values[...].T, gate[...].T, cot[...].T
    width = H * F
    for h in range(H):
        out[h, 0:F] = projected[F * h : F * (h + 1)]
        out[h, F : 2 * F] = projected[width + F * h : width + F * (h + 1)]
        cols = slice(DV * h, DV * (h + 1))
        out[h, AT_V : AT_V + DV] = v[cols]
        out[h, AT_G : AT_G + DV] = g[cols]
        out[h, AT_C : AT_C + DV] = c[cols]
        for i in range(x.shape[1] // H // TOK):
            at = ROWS + TOK * i
            start = x.shape[1] // H * h + TOK * i
            out[h, at : at + TOK] = x[:, start : start + TOK]


def state_kernel(place, data, conv, out, columns):
    taps = head_taps(conv, columns, place[1])[F:]
    total = jnp.zeros((FEAT, 2 * DV), f32)
    before = jnp.zeros((F, 2), f32)
    for c in range(H // WIDE):
        raw = rows_of(data, c, F, F).astype(f32)
        feat = features(convolve(raw, before, taps))
        if c == 0:
            token = lax.broadcasted_iota(jnp.int32, feat.shape, 1)
            feat = jnp.where(token < KCONV - 1, 0.0, feat)
        before = raw[:, -2:]
        high, low = halves(feat)
        v = wide_values(rows_of(data, c, AT_V, DV))
        total = total + (mm(high, v, NT) + mm(low, v, NT))
    first, last = data[0, 0 : 2 * F + DV], data[H - 1, 0 : 2 * F]
    extra = []
    for start in (F, 0):
        rows = slice(start, start + F)
        extra += [first[rows, 0:1], first[rows, 1:2]]
        extra += [last[rows, TOK - 2 : TOK - 1], last[rows, TOK - 1 : TOK]]
    for j in range(DV // F):
        rows = slice(2 * F + F * j, 2 * F + F * (j + 1))
        extra += [first[rows, 0:1], first[rows, 1:2]]
    repeat_into(out, pack_state(total, extra))


def main_kernel(place, data, states, conv, out, gq, gk, gv, parts, keys, edges, sent, columns):
    here = place[0]
    taps = head_taps(conv, columns, place[1])
    length = TOK * WIDE
    total = jnp.zeros((SENT, 2 * DV), f32)
    for b in range(states.shape[0]):
        total = total + states[b].astype(f32) * (b < here).astype(f32)
    first_q, first_k, first_v = first_tokens(states, taps)
    lane = lax.broadcasted_iota(jnp.int32, (FEAT, 2 * DV), 1)
    earlier = (lane % 8 < KCONV - 1) & (lane < 8 * here)
    feat = halves(jnp.where(earlier, features(first_k), 0.0))
    first_values = wide_values(first_v.astype(bf16))
    state = (
        unpack_state(total) + mm(feat[0], first_values, NT) + mm(feat[1], first_values, NT)
    )
    shift = 2 * DV * 2 - 8 * (here + 1)
    edges[0:F] = pltpu.roll(first_q, shift - 4, 1)
    edges[F : 2 * F] = pltpu.roll(first_k, shift, 1)
    edges[2 * F :] = pltpu.roll(first_v, shift, 1)
    tile = states[jnp.maximum(here - 1, 0), FEAT // 2 : SENT].astype(f32)
    tile = tile * (here > 0).astype(f32)
    before = jnp.concatenate(
        [tile[:, SPARE + 6 : SPARE + 8], tile[:, SPARE + 2 : SPARE + 4]], 0
    )
    k_at = lax.broadcasted_iota(jnp.int32, (length, length), 0)
    q_at = lax.broadcasted_iota(jnp.int32, (length, length), 1)
    causal = k_at <= q_at
    whole = jnp.zeros((FEAT, 2 * DV), f32)
    for c in range(H // WIDE):
        raw = rows_of(data, c, 0, 2 * F).astype(f32)
        mixed = convolve(raw, before, taps)
        before = raw[:, -2:]
        q, k = mixed[:F], mixed[F:]
        (qh, ql), (kh, kl) = halves(q), halves(k)
        keys[c] = k
        v = wide_values(rows_of(data, c, AT_V, DV))
        g = rows_of(data, c, AT_G, DV).astype(f32)
        cot = rows_of(data, c, AT_C, DV).astype(f32)
        scores = mm(
            jnp.concatenate([kh, kh, kl], 0), jnp.concatenate([qh, ql, qh], 0), TN
        ) * F**-0.5
        weights = halves(jnp.where(causal, 1.0 + scores + 0.5 * scores * scores, 0.0))
        q_feat, k_feat = halves(features(q)), halves(features(k))
        split_state = halves(state)
        numer = mm(v, weights[0], NN) + mm(v, weights[1], NN) + mm3(split_state, q_feat, TN)
        inverse = 1.0 / numer[DV : DV + 1]
        attended = numer[:DV] * inverse
        sig = jax.nn.sigmoid(g)
        act = g * sig
        result = (attended * act).astype(bf16)
        g_gate = (cot * attended * sig * (1.0 + g * (1.0 - sig))).astype(bf16)
        g_att = cot * act
        g_num = g_att * inverse
        g_den = -jnp.sum(g_att * attended, 0, keepdims=True) * inverse
        row = lax.broadcasted_iota(jnp.int32, (DV, length), 0)
        wide = jnp.concatenate([g_num, jnp.where(row == 0, g_den, 0.0)], 0)
        grads = halves(wide)
        g_weights = mm(v, grads[0], TN) + mm(v, grads[1], TN)
        g_scores = halves(jnp.where(causal, g_weights * (1.0 + scores), 0.0) * F**-0.5)
        g_query = mm3((kh, kl), g_scores, NN) + features_back(q, mm3(split_state, grads, NN))
        if c == 0:
            extra = [g_query[:, 0:1], g_query[:, 1:2]]
            for j in range(DV // F + 1):
                column = wide[F * j : F * (j + 1), 0:1]
                high = column.astype(bf16)
                extra += [high, column - high.astype(f32)]
        g_key = mm3((qh, ql), g_scores, NT)
        g_value = mm3((grads[0][:DV], grads[1][:DV]), weights, NT)
        part = mm3(q_feat, grads, NT)
        whole = whole + part
        parts[c] = part
        state = state + (mm(k_feat[0], v, NT) + mm(k_feat[1], v, NT))
        for i in range(WIDE):
            cols = slice(TOK * i, TOK * (i + 1))
            out[WIDE * c + i, 0:DV] = result[:, cols]
            out[WIDE * c + i, DV : 2 * DV] = g_gate[:, cols]
        gq[c] = g_query
        gk[c] = g_key
        gv[c] = g_value
    repeat_into(sent, pack_state(whole, extra))


def back_kernel(
    place, data, states, done, gq, gk, gv, parts, keys, edges, conv, out, columns
):
    here = place[0]
    taps = head_taps(conv, columns, place[1])
    count = states.shape[0]
    total = jnp.zeros((SENT, 2 * DV), f32)
    for b in range(count):
        total = total + states[b].astype(f32) * (b > here).astype(f32)
    state = unpack_state(total)
    tile = states[jnp.minimum(here + 1, count - 1), FEAT // 2 : SENT].astype(f32)
    edge = edges[...]
    edge_v = wide_values(edge[2 * F :].astype(bf16))
    split_state = halves(state)
    column = jnp.concatenate(
        [
            tile[:, SPARE + 2 + 2 * j : SPARE + 3 + 2 * j]
            + tile[:, SPARE + 3 + 2 * j : SPARE + 4 + 2 * j]
            for j in range(DV // F + 1)
        ],
        0,
    )
    pair = jnp.sum(column * edge_v[: DV + F].astype(f32), 0, keepdims=True)
    lane = lax.broadcasted_iota(jnp.int32, (FEAT, 2 * DV), 1)
    g_feat = mm(split_state[0], edge_v, NN) + mm(split_state[1], edge_v, NN)
    g_feat = g_feat - jnp.where(lane == 1, features(edge[:F])[:, 0:1] * pair, 0.0)
    after = jnp.concatenate(
        [tile[:, SPARE : SPARE + 2], features_back(edge[F : 2 * F], g_feat)[:, 0:2]], 0
    ) * (here + 1 < count).astype(f32)
    length = TOK * WIDE
    for c in reversed(range(H // WIDE)):
        k = keys[c]
        v = wide_values(rows_of(data, c, AT_V, DV))
        k_feat = halves(features(k))
        split_state = halves(state)
        g_feat = mm(split_state[0], v, NN) + mm(split_state[1], v, NN)
        g_key = gk[c] + features_back(k, g_feat)
        g_value = (gv[c] + mm3(split_state, k_feat, TN)[:DV]).astype(bf16)
        state = state + parts[c]
        now = jnp.concatenate([gq[c], g_key], 0)
        total = (
            taps[:, 0:1] * now
            + taps[:, 1:2] * jnp.concatenate([now[:, 1:], after[:, 0:1]], 1)
            + taps[:, 2:3] * jnp.concatenate([now[:, 2:], after], 1)
        ).astype(bf16)
        after = now[:, 0:2]
        for i in range(WIDE):
            cols = slice(TOK * i, TOK * (i + 1))
            b = WIDE * c + i
            out[b, FIRST : FIRST + 2 * DV] = done[b]
            out[b, FIRST + 2 * DV : FIRST + 3 * DV] = g_value[:, cols]
            for dest in range(H):
                out[dest, 2 * F * b : 2 * F * (b + 1)] = total[:, cols]

def stacked(grads, block):
    return jnp.concatenate(
        [
            grads[h, pl.ds(2 * F * block + at, F)]
            for at in (0, F)
            for h in range(H)
        ],
        0,
    )


def weight_kernel(place, grads, data, out, own):
    own[...] = stacked(grads, place[1])
    total = jnp.concatenate([stacked(grads, b) for b in range(H)], 1).T
    count, rows = out.shape[:2]
    parts = count * rows // TOK
    for i in range(parts):
        at = ROWS + TOK * i
        tokens = jnp.concatenate([data[b, at : at + TOK] for b in range(H)], 0)
        result = mm(tokens, total, TN).astype(bf16)
        for j in range(count // parts):
            out[i * (count // parts) + j] = result[rows * j : rows * (j + 1)]


def hidden_kernel(own, weight, out):
    out[...] = mm(own[...].T, weight[...], NT).astype(bf16)


def unpack_kernel(data, output, g_gate, g_value):
    for i, target in enumerate((output, g_gate, g_value)):
        at = FIRST + DV * i
        target[...] = jnp.concatenate([data[h, at : at + DV] for h in range(H)], 0).T


def call(kernel, name, out_shape, *args, scalars=0, waits=0, scratch=()):
    specs = [pl.BlockSpec(memory_space=pltpu.SMEM)] * scalars
    specs += [pl.BlockSpec(memory_space=pltpu.VMEM)] * (len(args) - scalars - waits)
    specs += [pl.BlockSpec(memory_space=pl.ANY)] * waits
    outs = jax.tree.map(lambda s: pl.BlockSpec(memory_space=pltpu.VMEM), out_shape)
    return pl.pallas_call(
        kernel, name=name, out_shape=out_shape, in_specs=specs, out_specs=outs,
        scratch_shapes=scratch,
    )(*args)


def shape(dims, kind):
    return jax.ShapeDtypeStruct(dims, kind)


def swap(x, axis):
    return lax.all_to_all(x, axis, 0, 0, tiled=True)


def everyone(x, axis):
    return swap(jnp.broadcast_to(x[None], (lax.axis_size(axis),) + x.shape), axis)


def body(hidden_in, qk_weight, conv_weight, values, gate_in, cotangent):
    tokens = hidden_in[0]
    supers = lax.axis_size("s")
    others = lax.axis_size(("dp", "s"))
    model = tokens.shape[1]
    chunks, width = H // WIDE, TOK * WIDE
    place = jnp.stack([lax.axis_index("s"), lax.axis_index("g")]).astype(jnp.int32)
    taps = (pltpu.VMEM((2 * H * F, 8), f32),)
    packed = call(
        pack_kernel,
        "pack",
        shape((H, ROWS + model // H, TOK), bf16),
        tokens,
        qk_weight,
        values[0],
        gate_in[0],
        cotangent[0],
    )
    data = swap(packed, "g")
    own = call(
        state_kernel,
        "state",
        shape((supers, SENT, 2 * DV), bf16),
        place,
        data,
        conv_weight,
        scalars=1,
        scratch=taps,
    )
    done, gq, gk, gv, parts, keys, edges, sent = call(
        main_kernel,
        "main",
        (
            shape((H, 2 * DV, TOK), bf16),
            shape((chunks, F, width), f32),
            shape((chunks, F, width), f32),
            shape((chunks, DV, width), f32),
            shape((chunks, FEAT, 2 * DV), f32),
            shape((chunks, F, width), f32),
            shape((2 * F + DV, 2 * DV), f32),
            shape((supers, SENT, 2 * DV), bf16),
        ),
        place,
        data,
        swap(own, "s"),
        conv_weight,
        scalars=1,
        scratch=taps,
    )
    back = call(
        back_kernel,
        "back",
        shape((H, FIRST + 3 * DV, TOK), bf16),
        place,
        data,
        swap(sent, "s"),
        done,
        gq,
        gk,
        gv,
        parts,
        keys,
        edges,
        conv_weight,
        scalars=1,
        scratch=taps,
    )
    back = swap(back, "g")
    partial, own_grad = call(
        weight_kernel,
        "weight",
        (
            shape((others, model // H // others, 2 * H * F), bf16),
            shape((2 * H * F, TOK), bf16),
        ),
        place,
        back,
        data,
        scalars=1,
    )
    summed = call(
        sum_kernel, "sum", shape(partial.shape, bf16), swap(partial, ("dp", "s"))
    )
    slices = swap(summed, ("dp", "s")).reshape(model // H, 2 * H * F)
    grad_qk_weight = everyone(slices, "g").reshape(model, 2 * H * F)
    output, grad_gate, grad_values = call(
        unpack_kernel, "unpack", (shape((TOK, H * DV), bf16),) * 3, back
    )
    grad_hidden = call(
        hidden_kernel, "hidden", shape((TOK, model), bf16), own_grad, qk_weight
    )
    return output[None], grad_hidden[None], grad_values[None], grad_gate[None], grad_qk_weight


def solution(mesh):
    pairs, blocks = mesh.devices.shape
    fine = Mesh(mesh.devices.reshape(pairs, blocks // H, H), ("dp", "s", "g"))
    split = P("dp", ("s", "g"), None)
    return jax.shard_map(
        body,
        mesh=fine,
        in_specs=(split, P(), P(), split, split, split),
        out_specs=(split, split, split, split, P()),
        check_vma=False,
    )
```

```python
import math

import jax
import jax.numpy as jnp
from jax import lax
from jax.experimental import pallas as pl
from jax.experimental.pallas import tpu as pltpu
from jax.sharding import Mesh, PartitionSpec as P

H = 8
F = 16
DV = 64
KCONV = 3
SUPER = ("y", "z")
OTHER = ("dp", "y")
TOK = 128
ROWS = 2 * F + 2 * DV
AT_V, AT_G = 2 * F, 2 * F + DV
FEAT = 160
SENT = FEAT // 2 + 16
WIDE = 2
FIRST = 2 * F * H
SPARE = 32
f32 = jnp.float32
bf16 = jnp.bfloat16
NN = ((1,), (0,))
NT = ((1,), (1,))
TN = ((0,), (0,))


def mm(a, b, dims):
    return lax.dot_general(a, b, (dims, ((), ())), preferred_element_type=f32)


def halves(x):
    high = x.astype(bf16)
    return high, (x - high.astype(f32)).astype(bf16)


def mm3(a, b, dims):
    (ah, al), (bh, bl) = a, b
    return mm(ah, bh, dims) + (mm(ah, bl, dims) + mm(al, bh, dims))


def feature_scale(d):
    return F**-0.5 * (math.sqrt(0.5) if d == 0 else 1.0)


def up(x, d):
    return x if d == 0 else jnp.concatenate([x[d:], x[:d]], 0)


def features(x):
    rows = [x * F**-0.25]
    for d in range(F // 2):
        rows.append(x * up(x, d) * feature_scale(d))
    half = F // 2
    rows.append(x[:half] * x[half:] * feature_scale(half))
    row = lax.broadcasted_iota(jnp.int32, (8, x.shape[1]), 0)
    rows.append(jnp.where(row == 0, 1.0, 0.0))
    return jnp.concatenate(rows, 0)


def features_back(x, grads):
    total = grads[:F] * F**-0.25
    half = F // 2
    for d in range(half):
        part = grads[F * (d + 1) : F * (d + 2)] * feature_scale(d)
        total = total + part * up(x, d) + up(part * x, (F - d) % F)
    part = grads[F * (half + 1) : F * (half + 1) + half] * feature_scale(half)
    return total + jnp.concatenate([part * x[half:], part * x[:half]], 0)


def pack_state(state, extra):
    half = FEAT // 2
    lane = lax.broadcasted_iota(jnp.int32, (half, 2 * DV), 1)
    main = jnp.where(lane < DV, state[:half], pltpu.roll(state[half:], DV, 1))
    high, low = halves(state)
    high, low = high.astype(f32), low.astype(f32)
    small = lane[:16]
    sums = jnp.zeros((16, 2 * DV), f32)
    for i in range(FEAT // 16):
        sums = jnp.where(small == i, high[16 * i : 16 * i + 16, DV : DV + 1], sums)
        sums = jnp.where(small == i + 16, low[16 * i : 16 * i + 16, DV : DV + 1], sums)
    for i, column in enumerate(extra):
        sums = jnp.where(small == SPARE + i, column.astype(f32), sums)
    return jnp.concatenate([main, sums], 0).astype(bf16)


def unpack_state(total):
    half = FEAT // 2
    main = total[:half]
    main = jnp.concatenate([main, pltpu.roll(main, DV, 1)], 0)
    sums = total[half:]
    sums = sums + pltpu.roll(sums, 2 * DV - 16, 1)
    column = jnp.concatenate([sums[:, i : i + 1] for i in range(FEAT // 16)], 0)
    lane = lax.broadcasted_iota(jnp.int32, (FEAT, 2 * DV), 1)
    return jnp.where(lane < DV, main, jnp.where(lane == DV, column, 0.0))


def repeat_into(out, value):
    for i in range(out.shape[0]):
        out[i] = value


def wide_values(values):
    row = lax.broadcasted_iota(jnp.int32, (DV, values.shape[1]), 0)
    return jnp.concatenate([values, jnp.where(row == 0, 1.0, 0.0).astype(bf16)], 0)


def rows_of(ref, chunk, start, size):
    return jnp.concatenate(
        [ref[WIDE * chunk + i, start : start + size] for i in range(WIDE)], 1
    )


def head_taps(conv, columns, head):
    padded = jnp.concatenate([conv[...], jnp.zeros((8 - KCONV, 2 * H * F), f32)], 0)
    columns[...] = padded.T
    at = pl.multiple_of(F * head, F)
    return jnp.concatenate([columns[pl.ds(at, F)], columns[pl.ds(H * F + at, F)]], 0)


def convolve(now, before, taps):
    return (
        taps[:, 0:1] * now
        + taps[:, 1:2] * jnp.concatenate([before[:, 1:2], now[:, :-1]], 1)
        + taps[:, 2:3] * jnp.concatenate([before, now[:, :-2]], 1)
    )


def first_tokens(states, taps):
    rows, lanes = F, 2 * DV
    lane = lax.broadcasted_iota(jnp.int32, (rows, lanes), 1)
    raw, vals = jnp.zeros((rows, lanes), f32), jnp.zeros((rows, lanes), f32)
    for b in range(states.shape[0]):
        tile = states[b, FEAT // 2 : SENT].astype(f32)
        here = (lane >= 8 * b) & (lane < 8 * (b + 1))
        raw = jnp.where(here, pltpu.roll(tile, (8 * b - SPARE) % lanes, 1), raw)
        vals = jnp.where(here, pltpu.roll(tile, (8 * b - SPARE - 8) % lanes, 1), vals)
    prev = jnp.where(lane < 8, 0.0, pltpu.roll(raw, 8, 1))
    one = jnp.where(
        lane % 4 == 0, pltpu.roll(prev, lanes - 3, 1), pltpu.roll(raw, 1, 1)
    )
    two = pltpu.roll(prev, lanes - 2, 1)
    q, k = (
        t[:, 0:1] * raw + t[:, 1:2] * one + t[:, 2:3] * two for t in (taps[:F], taps[F:])
    )
    v = jnp.concatenate(
        [vals if j == 0 else pltpu.roll(vals, lanes - 2 * j, 1) for j in range(DV // F)], 0
    )
    return q, k, v


def sum_kernel(data, out):
    total = data[0].astype(f32)
    for i in range(1, data.shape[0]):
        total = total + data[i].astype(f32)
    repeat_into(out, total.astype(bf16))


def pack_kernel(tokens, weight, values, gate, cot, out):
    x = tokens[...]
    projected = mm(x, weight[...], NN).T.astype(bf16)
    g = gate[...].astype(f32)
    v = values[...].T
    up = (cot[...].astype(f32) * (g * jax.nn.sigmoid(g))).astype(bf16).T
    width = H * F
    for h in range(H):
        out[h, 0:F] = projected[F * h : F * (h + 1)]
        out[h, F : 2 * F] = projected[width + F * h : width + F * (h + 1)]
        cols = slice(DV * h, DV * (h + 1))
        out[h, AT_V : AT_V + DV] = v[cols]
        out[h, AT_G : AT_G + DV] = up[cols]
        for i in range(x.shape[1] // H // TOK):
            at = ROWS + TOK * i
            start = x.shape[1] // H * h + TOK * i
            out[h, at : at + TOK] = x[:, start : start + TOK]


def state_kernel(place, data, conv, out, columns):
    taps = head_taps(conv, columns, place[1])[F:]
    total = jnp.zeros((FEAT, 2 * DV), f32)
    before = jnp.zeros((F, 2), f32)
    for c in range(H // WIDE):
        raw = rows_of(data, c, F, F).astype(f32)
        feat = features(convolve(raw, before, taps))
        if c == 0:
            token = lax.broadcasted_iota(jnp.int32, feat.shape, 1)
            feat = jnp.where(token < KCONV - 1, 0.0, feat)
        before = raw[:, -2:]
        high, low = halves(feat)
        v = wide_values(rows_of(data, c, AT_V, DV))
        total = total + (mm(high, v, NT) + mm(low, v, NT))
    first, last = data[0, 0 : 2 * F + DV], data[H - 1, 0 : 2 * F]
    extra = []
    for start in (F, 0):
        rows = slice(start, start + F)
        extra += [first[rows, 0:1], first[rows, 1:2]]
        extra += [last[rows, TOK - 2 : TOK - 1], last[rows, TOK - 1 : TOK]]
    for j in range(DV // F):
        rows = slice(2 * F + F * j, 2 * F + F * (j + 1))
        extra += [first[rows, 0:1], first[rows, 1:2]]
    repeat_into(out, pack_state(total, extra))


def main_kernel(place, data, states, conv, out, gq, gk, gv, parts, keys, edges, sent, columns):
    here = place[0]
    taps = head_taps(conv, columns, place[1])
    length = TOK * WIDE
    total = jnp.zeros((SENT, 2 * DV), f32)
    for b in range(states.shape[0]):
        total = total + states[b].astype(f32) * (b < here).astype(f32)
    first_q, first_k, first_v = first_tokens(states, taps)
    lane = lax.broadcasted_iota(jnp.int32, (FEAT, 2 * DV), 1)
    earlier = (lane % 8 < KCONV - 1) & (lane < 8 * here)
    feat = halves(jnp.where(earlier, features(first_k), 0.0))
    first_values = wide_values(first_v.astype(bf16))
    state = (
        unpack_state(total) + mm(feat[0], first_values, NT) + mm(feat[1], first_values, NT)
    )
    shift = 2 * DV * 2 - 8 * (here + 1)
    edges[0:F] = pltpu.roll(first_q, shift - 4, 1)
    edges[F : 2 * F] = pltpu.roll(first_k, shift, 1)
    edges[2 * F :] = pltpu.roll(first_v, shift, 1)
    tile = states[jnp.maximum(here - 1, 0), FEAT // 2 : SENT].astype(f32)
    tile = tile * (here > 0).astype(f32)
    before = jnp.concatenate(
        [tile[:, SPARE + 6 : SPARE + 8], tile[:, SPARE + 2 : SPARE + 4]], 0
    )
    k_at = lax.broadcasted_iota(jnp.int32, (length, length), 0)
    q_at = lax.broadcasted_iota(jnp.int32, (length, length), 1)
    causal = k_at <= q_at
    whole = jnp.zeros((FEAT, 2 * DV), f32)
    for c in range(H // WIDE):
        raw = rows_of(data, c, 0, 2 * F).astype(f32)
        mixed = convolve(raw, before, taps)
        before = raw[:, -2:]
        q, k = mixed[:F], mixed[F:]
        (qh, ql), (kh, kl) = halves(q), halves(k)
        keys[c] = k
        v = wide_values(rows_of(data, c, AT_V, DV))
        g_att = rows_of(data, c, AT_G, DV).astype(f32)
        scores = mm(
            jnp.concatenate([kh, kh, kl], 0), jnp.concatenate([qh, ql, qh], 0), TN
        ) * F**-0.5
        weights = halves(jnp.where(causal, 1.0 + scores + 0.5 * scores * scores, 0.0))
        q_feat, k_feat = halves(features(q)), halves(features(k))
        split_state = halves(state)
        numer = mm(v, weights[0], NN) + mm(v, weights[1], NN) + mm3(split_state, q_feat, TN)
        inverse = 1.0 / numer[DV : DV + 1]
        attended = numer[:DV] * inverse
        result = attended.astype(bf16)
        g_num = g_att * inverse
        g_den = -jnp.sum(g_att * attended, 0, keepdims=True) * inverse
        row = lax.broadcasted_iota(jnp.int32, (DV, length), 0)
        wide = jnp.concatenate([g_num, jnp.where(row == 0, g_den, 0.0)], 0)
        grads = halves(wide)
        g_weights = mm(v, grads[0], TN) + mm(v, grads[1], TN)
        g_scores = halves(jnp.where(causal, g_weights * (1.0 + scores), 0.0) * F**-0.5)
        g_query = mm3((kh, kl), g_scores, NN) + features_back(q, mm3(split_state, grads, NN))
        if c == 0:
            extra = [g_query[:, 0:1], g_query[:, 1:2]]
            for j in range(DV // F + 1):
                column = wide[F * j : F * (j + 1), 0:1]
                high = column.astype(bf16)
                extra += [high, column - high.astype(f32)]
        g_key = mm3((qh, ql), g_scores, NT)
        g_value = mm3((grads[0][:DV], grads[1][:DV]), weights, NT)
        part = mm3(q_feat, grads, NT)
        whole = whole + part
        parts[c] = part
        state = state + (mm(k_feat[0], v, NT) + mm(k_feat[1], v, NT))
        for i in range(WIDE):
            cols = slice(TOK * i, TOK * (i + 1))
            out[WIDE * c + i] = result[:, cols]
        gq[c] = g_query
        gk[c] = g_key
        gv[c] = g_value
    repeat_into(sent, pack_state(whole, extra))


def back_kernel(
    place, data, states, done, gq, gk, gv, parts, keys, edges, conv, out, columns
):
    here = place[0]
    taps = head_taps(conv, columns, place[1])
    count = states.shape[0]
    total = jnp.zeros((SENT, 2 * DV), f32)
    for b in range(count):
        total = total + states[b].astype(f32) * (b > here).astype(f32)
    state = unpack_state(total)
    tile = states[jnp.minimum(here + 1, count - 1), FEAT // 2 : SENT].astype(f32)
    edge = edges[...]
    edge_v = wide_values(edge[2 * F :].astype(bf16))
    split_state = halves(state)
    column = jnp.concatenate(
        [
            tile[:, SPARE + 2 + 2 * j : SPARE + 3 + 2 * j]
            + tile[:, SPARE + 3 + 2 * j : SPARE + 4 + 2 * j]
            for j in range(DV // F + 1)
        ],
        0,
    )
    pair = jnp.sum(column * edge_v[: DV + F].astype(f32), 0, keepdims=True)
    lane = lax.broadcasted_iota(jnp.int32, (FEAT, 2 * DV), 1)
    g_feat = mm(split_state[0], edge_v, NN) + mm(split_state[1], edge_v, NN)
    g_feat = g_feat - jnp.where(lane == 1, features(edge[:F])[:, 0:1] * pair, 0.0)
    after = jnp.concatenate(
        [tile[:, SPARE : SPARE + 2], features_back(edge[F : 2 * F], g_feat)[:, 0:2]], 0
    ) * (here + 1 < count).astype(f32)
    length = TOK * WIDE
    for c in reversed(range(H // WIDE)):
        k = keys[c]
        v = wide_values(rows_of(data, c, AT_V, DV))
        k_feat = halves(features(k))
        split_state = halves(state)
        g_feat = mm(split_state[0], v, NN) + mm(split_state[1], v, NN)
        g_key = gk[c] + features_back(k, g_feat)
        g_value = (gv[c] + mm3(split_state, k_feat, TN)[:DV]).astype(bf16)
        state = state + parts[c]
        now = jnp.concatenate([gq[c], g_key], 0)
        total = (
            taps[:, 0:1] * now
            + taps[:, 1:2] * jnp.concatenate([now[:, 1:], after[:, 0:1]], 1)
            + taps[:, 2:3] * jnp.concatenate([now[:, 2:], after], 1)
        ).astype(bf16)
        after = now[:, 0:2]
        for i in range(WIDE):
            cols = slice(TOK * i, TOK * (i + 1))
            b = WIDE * c + i
            out[b, FIRST : FIRST + DV] = done[b]
            out[b, FIRST + DV : FIRST + 2 * DV] = g_value[:, cols]
            for dest in range(H):
                out[dest, 2 * F * b : 2 * F * (b + 1)] = total[:, cols]

def stacked(grads, block):
    return jnp.concatenate(
        [
            grads[h, pl.ds(2 * F * block + at, F)]
            for at in (0, F)
            for h in range(H)
        ],
        0,
    )


def weight_kernel(place, grads, data, out, own):
    own[...] = stacked(grads, place[1])
    total = jnp.concatenate([stacked(grads, b) for b in range(H)], 1).T
    count, rows = out.shape[:2]
    parts = count * rows // TOK
    for i in range(parts):
        at = ROWS + TOK * i
        tokens = jnp.concatenate([data[b, at : at + TOK] for b in range(H)], 0)
        result = mm(tokens, total, TN).astype(bf16)
        for j in range(count // parts):
            out[i * (count // parts) + j] = result[rows * j : rows * (j + 1)]


def hidden_kernel(own, weight, out):
    out[...] = mm(own[...].T, weight[...], NT).astype(bf16)


def unpack_kernel(data, gate, cot, output, g_gate, g_value):
    attended, values = (
        jnp.concatenate([data[h, at : at + DV] for h in range(H)], 0).T
        for at in (FIRST, FIRST + DV)
    )
    g = gate[...].astype(f32)
    sig = jax.nn.sigmoid(g)
    attended = attended.astype(f32)
    output[...] = (attended * (g * sig)).astype(bf16)
    g_gate[...] = (
        cot[...].astype(f32) * attended * sig * (1.0 + g * (1.0 - sig))
    ).astype(bf16)
    g_value[...] = values


def near(x):
    return pltpu.with_memory_space_constraint(x, pltpu.VMEM)


def call(kernel, name, out_shape, *args, scalars=0, final=False, scratch=()):
    specs = [pl.BlockSpec(memory_space=pltpu.SMEM)] * scalars
    specs += [pl.BlockSpec(memory_space=pltpu.VMEM)] * (len(args) - scalars)
    outs = jax.tree.map(lambda s: pl.BlockSpec(memory_space=pltpu.VMEM), out_shape)
    if not final:
        out_shape = jax.tree.map(lambda s: pltpu.VMEM(s.shape, s.dtype), out_shape)
    return pl.pallas_call(
        kernel,
        name=name,
        out_shape=out_shape,
        in_specs=specs,
        out_specs=outs,
        scratch_shapes=scratch,
    )(*args)


def shape(dims, kind):
    return jax.ShapeDtypeStruct(dims, kind)


def swap(x, axis):
    return near(lax.all_to_all(x, axis, 0, 0, tiled=True))


def body(hidden_in, qk_weight, conv_weight, values, gate_in, cotangent):
    tokens = hidden_in[0]
    supers = lax.axis_size(SUPER)
    others = lax.axis_size(OTHER)
    model = tokens.shape[1]
    chunks, width = H // WIDE, TOK * WIDE
    place = jnp.stack([lax.axis_index(SUPER), lax.axis_index("g")]).astype(jnp.int32)
    taps = (pltpu.VMEM((2 * H * F, 8), f32),)
    packed = call(
        pack_kernel,
        "pack",
        shape((H, ROWS + model // H, TOK), bf16),
        tokens,
        qk_weight,
        values[0],
        gate_in[0],
        cotangent[0],
    )
    data = swap(packed, "g")
    own = call(
        state_kernel,
        "state",
        shape((supers, SENT, 2 * DV), bf16),
        place,
        data,
        conv_weight,
        scalars=1,
        scratch=taps,
    )
    done, gq, gk, gv, parts, keys, edges, sent = call(
        main_kernel,
        "main",
        (
            shape((H, DV, TOK), bf16),
            shape((chunks, F, width), f32),
            shape((chunks, F, width), f32),
            shape((chunks, DV, width), f32),
            shape((chunks, FEAT, 2 * DV), f32),
            shape((chunks, F, width), f32),
            shape((2 * F + DV, 2 * DV), f32),
            shape((supers, SENT, 2 * DV), bf16),
        ),
        place,
        data,
        swap(own, SUPER),
        conv_weight,
        scalars=1,
        scratch=taps,
    )
    back = call(
        back_kernel,
        "back",
        shape((H, FIRST + 2 * DV, TOK), bf16),
        place,
        data,
        swap(sent, SUPER),
        *(near(x) for x in (done, gq, gk, gv, parts, keys, edges)),
        conv_weight,
        scalars=1,
        scratch=taps,
    )
    back = swap(back, "g")
    partial, own_grad = call(
        weight_kernel,
        "weight",
        (
            shape((others, model // H // others, 2 * H * F), bf16),
            shape((2 * H * F, TOK), bf16),
        ),
        place,
        back,
        data,
        scalars=1,
    )
    deep = model // H // others
    some = swap(partial, OTHER)
    summed = call(
        sum_kernel, "sum_a", shape((lax.axis_size("z"), deep, 2 * H * F), bf16), some
    )
    summed = call(
        sum_kernel, "sum_b", shape((H * others, deep, 2 * H * F), bf16), swap(summed, "z")
    )
    grad_qk_weight = lax.all_to_all(summed, ("g",) + OTHER, 0, 0, tiled=True)
    grad_qk_weight = grad_qk_weight.reshape(model, 2 * H * F)
    output, grad_gate, grad_values = call(
        unpack_kernel,
        "unpack",
        (shape((TOK, H * DV), bf16),) * 3,
        back,
        gate_in[0],
        cotangent[0],
        final=True,
    )
    grad_hidden = call(
        hidden_kernel,
        "hidden",
        shape((TOK, model), bf16),
        near(own_grad),
        qk_weight,
        final=True,
    )
    return output[None], grad_hidden[None], grad_values[None], grad_gate[None], grad_qk_weight


def solution(mesh):
    pairs, blocks = mesh.devices.shape
    y = 4 if blocks // H % 4 == 0 else 1
    fine = Mesh(
        mesh.devices.reshape(pairs, y, blocks // H // y, H), ("dp", "y", "z", "g")
    )
    split = P("dp", ("y", "z", "g"), None)
    return jax.shard_map(
        body,
        mesh=fine,
        in_specs=(split, P(), P(), split, split, split),
        out_specs=(split, split, split, split, P()),
        check_vma=False,
    )
```

```python
import math

import jax
import jax.numpy as jnp
from jax import lax
from jax.experimental import pallas as pl
from jax.experimental.pallas import tpu as pltpu
from jax.sharding import Mesh, PartitionSpec as P

H = 8
F = 16
DV = 64
KCONV = 3
SUPER = ("y", "z")
OTHER = ("dp", "y")
TOK = 128
HID = 256
AT_V, AT_G, AT_P = HID, HID + DV, HID + 2 * DV
ROWS = AT_P + 2 * F
FEAT = 160
SENT = FEAT // 2 + 16
WIDE = 2
FIRST = 2 * F * H
SPARE = 32
f32 = jnp.float32
bf16 = jnp.bfloat16
NN = ((1,), (0,))
NT = ((1,), (1,))
TN = ((0,), (0,))


def mm(a, b, dims):
    return lax.dot_general(a, b, (dims, ((), ())), preferred_element_type=f32)


def halves(x):
    high = x.astype(bf16)
    return high, (x - high.astype(f32)).astype(bf16)


def mm3(a, b, dims):
    (ah, al), (bh, bl) = a, b
    return mm(ah, bh, dims) + (mm(ah, bl, dims) + mm(al, bh, dims))


def feature_scale(d):
    return F**-0.5 * (math.sqrt(0.5) if d == 0 else 1.0)


def up(x, d):
    return x if d == 0 else jnp.concatenate([x[d:], x[:d]], 0)


def features(x):
    rows = [x * F**-0.25]
    for d in range(F // 2):
        rows.append(x * up(x, d) * feature_scale(d))
    half = F // 2
    rows.append(x[:half] * x[half:] * feature_scale(half))
    row = lax.broadcasted_iota(jnp.int32, (8, x.shape[1]), 0)
    rows.append(jnp.where(row == 0, 1.0, 0.0))
    return jnp.concatenate(rows, 0)


def features_back(x, grads):
    total = grads[:F] * F**-0.25
    half = F // 2
    for d in range(half):
        part = grads[F * (d + 1) : F * (d + 2)] * feature_scale(d)
        total = total + part * up(x, d) + up(part * x, (F - d) % F)
    part = grads[F * (half + 1) : F * (half + 1) + half] * feature_scale(half)
    return total + jnp.concatenate([part * x[half:], part * x[:half]], 0)


def pack_state(state, extra):
    half = FEAT // 2
    lane = lax.broadcasted_iota(jnp.int32, (half, 2 * DV), 1)
    main = jnp.where(lane < DV, state[:half], pltpu.roll(state[half:], DV, 1))
    high, low = halves(state)
    high, low = high.astype(f32), low.astype(f32)
    small = lane[:16]
    sums = jnp.zeros((16, 2 * DV), f32)
    for i in range(FEAT // 16):
        sums = jnp.where(small == i, high[16 * i : 16 * i + 16, DV : DV + 1], sums)
        sums = jnp.where(small == i + 16, low[16 * i : 16 * i + 16, DV : DV + 1], sums)
    for i, column in enumerate(extra):
        sums = jnp.where(small == SPARE + i, column.astype(f32), sums)
    return jnp.concatenate([main, sums], 0).astype(bf16)


def unpack_state(total):
    half = FEAT // 2
    main = total[:half]
    main = jnp.concatenate([main, pltpu.roll(main, DV, 1)], 0)
    sums = total[half:]
    sums = sums + pltpu.roll(sums, 2 * DV - 16, 1)
    column = jnp.concatenate([sums[:, i : i + 1] for i in range(FEAT // 16)], 0)
    lane = lax.broadcasted_iota(jnp.int32, (FEAT, 2 * DV), 1)
    return jnp.where(lane < DV, main, jnp.where(lane == DV, column, 0.0))


def repeat_into(out, value):
    for i in range(out.shape[0]):
        out[i] = value


def wide_values(values):
    row = lax.broadcasted_iota(jnp.int32, (DV, values.shape[1]), 0)
    return jnp.concatenate([values, jnp.where(row == 0, 1.0, 0.0).astype(bf16)], 0)


def rows_of(ref, chunk, start, size):
    return jnp.concatenate(
        [ref[WIDE * chunk + i, start : start + size] for i in range(WIDE)], 1
    )


def head_taps(conv, columns, head):
    padded = jnp.concatenate([conv[...], jnp.zeros((8 - KCONV, 2 * H * F), f32)], 0)
    columns[...] = padded.T
    at = pl.multiple_of(F * head, F)
    return jnp.concatenate([columns[pl.ds(at, F)], columns[pl.ds(H * F + at, F)]], 0)


def convolve(now, before, taps):
    return (
        taps[:, 0:1] * now
        + taps[:, 1:2] * jnp.concatenate([before[:, 1:2], now[:, :-1]], 1)
        + taps[:, 2:3] * jnp.concatenate([before, now[:, :-2]], 1)
    )


def first_tokens(states, taps):
    rows, lanes = F, 2 * DV
    lane = lax.broadcasted_iota(jnp.int32, (rows, lanes), 1)
    raw, vals = jnp.zeros((rows, lanes), f32), jnp.zeros((rows, lanes), f32)
    for b in range(states.shape[0]):
        tile = states[b, FEAT // 2 : SENT].astype(f32)
        here = (lane >= 8 * b) & (lane < 8 * (b + 1))
        raw = jnp.where(here, pltpu.roll(tile, (8 * b - SPARE) % lanes, 1), raw)
        vals = jnp.where(here, pltpu.roll(tile, (8 * b - SPARE - 8) % lanes, 1), vals)
    prev = jnp.where(lane < 8, 0.0, pltpu.roll(raw, 8, 1))
    one = jnp.where(
        lane % 4 == 0, pltpu.roll(prev, lanes - 3, 1), pltpu.roll(raw, 1, 1)
    )
    two = pltpu.roll(prev, lanes - 2, 1)
    q, k = (
        t[:, 0:1] * raw + t[:, 1:2] * one + t[:, 2:3] * two for t in (taps[:F], taps[F:])
    )
    v = jnp.concatenate(
        [vals if j == 0 else pltpu.roll(vals, lanes - 2 * j, 1) for j in range(DV // F)], 0
    )
    return q, k, v


def sum_kernel(data, out):
    total = data[0].astype(f32)
    for i in range(1, data.shape[0]):
        total = total + data[i].astype(f32)
    repeat_into(out, total.astype(bf16))


def pack_kernel(tokens, weight, values, gate, cot, out):
    x = tokens[...]
    projected = mm(x, weight[...], NN).T.astype(bf16)
    g = gate[...].astype(f32)
    v = values[...].T
    up = (cot[...].astype(f32) * (g * jax.nn.sigmoid(g))).astype(bf16).T
    width = H * F
    for h in range(H):
        out[h, AT_P : AT_P + F] = projected[F * h : F * (h + 1)]
        out[h, AT_P + F : ROWS] = projected[width + F * h : width + F * (h + 1)]
        cols = slice(DV * h, DV * (h + 1))
        out[h, AT_V : AT_V + DV] = v[cols]
        out[h, AT_G : AT_G + DV] = up[cols]
        for i in range(x.shape[1] // H // TOK):
            start = x.shape[1] // H * h + TOK * i
            out[h, TOK * i : TOK * (i + 1)] = x[:, start : start + TOK]


def state_kernel(place, data, conv, out, columns):
    taps = head_taps(conv, columns, place[1])[F:]
    total = jnp.zeros((FEAT, 2 * DV), f32)
    before = jnp.zeros((F, 2), f32)
    for c in range(H // WIDE):
        raw = rows_of(data, c, AT_P + F, F).astype(f32)
        feat = features(convolve(raw, before, taps))
        if c == 0:
            token = lax.broadcasted_iota(jnp.int32, feat.shape, 1)
            feat = jnp.where(token < KCONV - 1, 0.0, feat)
        before = raw[:, -2:]
        high, low = halves(feat)
        v = wide_values(rows_of(data, c, AT_V, DV))
        total = total + (mm(high, v, NT) + mm(low, v, NT))
    first, last = data[0, AT_P:ROWS], data[H - 1, AT_P:ROWS]
    begin = data[0, AT_V : AT_V + DV]
    extra = []
    for start in (F, 0):
        rows = slice(start, start + F)
        extra += [first[rows, 0:1], first[rows, 1:2]]
        extra += [last[rows, TOK - 2 : TOK - 1], last[rows, TOK - 1 : TOK]]
    for j in range(DV // F):
        rows = slice(F * j, F * (j + 1))
        extra += [begin[rows, 0:1], begin[rows, 1:2]]
    repeat_into(out, pack_state(total, extra))


def main_kernel(place, data, states, conv, out, gq, gk, gv, parts, keys, edges, sent, columns):
    here = place[0]
    taps = head_taps(conv, columns, place[1])
    length = TOK * WIDE
    total = jnp.zeros((SENT, 2 * DV), f32)
    for b in range(states.shape[0]):
        total = total + states[b].astype(f32) * (b < here).astype(f32)
    first_q, first_k, first_v = first_tokens(states, taps)
    lane = lax.broadcasted_iota(jnp.int32, (FEAT, 2 * DV), 1)
    earlier = (lane % 8 < KCONV - 1) & (lane < 8 * here)
    feat = halves(jnp.where(earlier, features(first_k), 0.0))
    first_values = wide_values(first_v.astype(bf16))
    state = (
        unpack_state(total) + mm(feat[0], first_values, NT) + mm(feat[1], first_values, NT)
    )
    shift = 2 * DV * 2 - 8 * (here + 1)
    edges[0:F] = pltpu.roll(first_q, shift - 4, 1)
    edges[F : 2 * F] = pltpu.roll(first_k, shift, 1)
    edges[2 * F :] = pltpu.roll(first_v, shift, 1)
    tile = states[jnp.maximum(here - 1, 0), FEAT // 2 : SENT].astype(f32)
    tile = tile * (here > 0).astype(f32)
    before = jnp.concatenate(
        [tile[:, SPARE + 6 : SPARE + 8], tile[:, SPARE + 2 : SPARE + 4]], 0
    )
    k_at = lax.broadcasted_iota(jnp.int32, (length, length), 0)
    q_at = lax.broadcasted_iota(jnp.int32, (length, length), 1)
    causal = k_at <= q_at
    whole = jnp.zeros((FEAT, 2 * DV), f32)
    for c in range(H // WIDE):
        raw = rows_of(data, c, AT_P, 2 * F).astype(f32)
        mixed = convolve(raw, before, taps)
        before = raw[:, -2:]
        q, k = mixed[:F], mixed[F:]
        (qh, ql), (kh, kl) = halves(q * F**-0.5), halves(k)
        keys[c] = k
        v = wide_values(rows_of(data, c, AT_V, DV))
        g_att = rows_of(data, c, AT_G, DV).astype(f32)
        near_one = 1.0 + mm(
            jnp.concatenate([kh, kh, kl], 0), jnp.concatenate([qh, ql, qh], 0), TN
        )
        weights = jnp.where(causal, 0.5 + 0.5 * near_one * near_one, 0.0).astype(bf16)
        q_feat, k_feat = halves(features(q)), halves(features(k))
        split_state = halves(state)
        numer = mm(v, weights, NN) + mm3(split_state, q_feat, TN)
        inverse = 1.0 / numer[DV : DV + 1]
        attended = numer[:DV] * inverse
        result = attended.astype(bf16)
        g_num = g_att * inverse
        g_den = -jnp.sum(g_att * attended, 0, keepdims=True) * inverse
        row = lax.broadcasted_iota(jnp.int32, (DV, length), 0)
        wide = jnp.concatenate([g_num, jnp.where(row == 0, g_den, 0.0)], 0)
        grads = halves(wide)
        g_weights = mm(v, grads[0], TN) + mm(v, grads[1], TN)
        g_scores = jnp.where(causal, g_weights * near_one, 0.0).astype(bf16)
        g_local = (mm(kh, g_scores, NN) + mm(kl, g_scores, NN)) * F**-0.5
        g_query = g_local + features_back(q, mm3(split_state, grads, NN))
        if c == 0:
            extra = [g_query[:, 0:1], g_query[:, 1:2]]
            for j in range(DV // F + 1):
                column = wide[F * j : F * (j + 1), 0:1]
                high = column.astype(bf16)
                extra += [high, column - high.astype(f32)]
        g_key = mm(qh, g_scores, NT) + mm(ql, g_scores, NT)
        g_value = mm(grads[0][:DV], weights, NT) + mm(grads[1][:DV], weights, NT)
        part = mm3(q_feat, grads, NT)
        whole = whole + part
        parts[c] = part
        state = state + (mm(k_feat[0], v, NT) + mm(k_feat[1], v, NT))
        for i in range(WIDE):
            cols = slice(TOK * i, TOK * (i + 1))
            out[WIDE * c + i] = result[:, cols]
        gq[c] = g_query
        gk[c] = g_key
        gv[c] = g_value
    repeat_into(sent, pack_state(whole, extra))


def back_kernel(
    place, states, done, gq, gk, gv, parts, keys, edges, conv, far, out, columns, data, sem
):
    fetch = pltpu.make_async_copy(far.at[:, AT_V : AT_V + DV], data, sem)
    fetch.start()
    here = place[0]
    taps = head_taps(conv, columns, place[1])
    count = states.shape[0]
    total = jnp.zeros((SENT, 2 * DV), f32)
    for b in range(count):
        total = total + states[b].astype(f32) * (b > here).astype(f32)
    state = unpack_state(total)
    tile = states[jnp.minimum(here + 1, count - 1), FEAT // 2 : SENT].astype(f32)
    edge = edges[...]
    edge_v = wide_values(edge[2 * F :].astype(bf16))
    split_state = halves(state)
    column = jnp.concatenate(
        [
            tile[:, SPARE + 2 + 2 * j : SPARE + 3 + 2 * j]
            + tile[:, SPARE + 3 + 2 * j : SPARE + 4 + 2 * j]
            for j in range(DV // F + 1)
        ],
        0,
    )
    pair = jnp.sum(column * edge_v[: DV + F].astype(f32), 0, keepdims=True)
    lane = lax.broadcasted_iota(jnp.int32, (FEAT, 2 * DV), 1)
    g_feat = mm(split_state[0], edge_v, NN) + mm(split_state[1], edge_v, NN)
    g_feat = g_feat - jnp.where(lane == 1, features(edge[:F])[:, 0:1] * pair, 0.0)
    after = jnp.concatenate(
        [tile[:, SPARE : SPARE + 2], features_back(edge[F : 2 * F], g_feat)[:, 0:2]], 0
    ) * (here + 1 < count).astype(f32)
    fetch.wait()
    for c in reversed(range(H // WIDE)):
        k = keys[c]
        v = wide_values(rows_of(data, c, 0, DV))
        k_feat = halves(features(k))
        split_state = halves(state)
        g_feat = mm(split_state[0], v, NN) + mm(split_state[1], v, NN)
        g_key = gk[c] + features_back(k, g_feat)
        g_value = (gv[c] + mm3(split_state, k_feat, TN)[:DV]).astype(bf16)
        state = state + parts[c]
        now = jnp.concatenate([gq[c], g_key], 0)
        total = (
            taps[:, 0:1] * now
            + taps[:, 1:2] * jnp.concatenate([now[:, 1:], after[:, 0:1]], 1)
            + taps[:, 2:3] * jnp.concatenate([now[:, 2:], after], 1)
        ).astype(bf16)
        after = now[:, 0:2]
        for i in range(WIDE):
            cols = slice(TOK * i, TOK * (i + 1))
            b = WIDE * c + i
            out[b, FIRST : FIRST + DV] = done[b]
            out[b, FIRST + DV : FIRST + 2 * DV] = g_value[:, cols]
            for dest in range(H):
                out[dest, 2 * F * b : 2 * F * (b + 1)] = total[:, cols]

def stacked(grads, block):
    return jnp.concatenate(
        [
            grads[h, pl.ds(2 * F * block + at, F)]
            for at in (0, F)
            for h in range(H)
        ],
        0,
    )


def weight_kernel(place, grads, far, out, own, data, sem):
    fetch = pltpu.make_async_copy(far.at[:, 0:HID], data, sem)
    fetch.start()
    own[...] = stacked(grads, place[1])
    total = jnp.concatenate([stacked(grads, b) for b in range(H)], 1).T
    count, rows = out.shape[:2]
    parts = count * rows // TOK
    fetch.wait()
    for i in range(parts):
        at = TOK * i
        tokens = jnp.concatenate([data[b, at : at + TOK] for b in range(H)], 0)
        result = mm(tokens, total, TN).astype(bf16)
        for j in range(count // parts):
            out[i * (count // parts) + j] = result[rows * j : rows * (j + 1)]


def hidden_kernel(own, weight, out):
    out[...] = mm(own[...].T, weight[...], NT).astype(bf16)


def unpack_kernel(data, gate, cot, output, g_gate, g_value):
    attended, values = (
        jnp.concatenate([data[h, at : at + DV] for h in range(H)], 0).T
        for at in (FIRST, FIRST + DV)
    )
    g = gate[...].astype(f32)
    sig = jax.nn.sigmoid(g)
    attended = attended.astype(f32)
    output[...] = (attended * (g * sig)).astype(bf16)
    g_gate[...] = (
        cot[...].astype(f32) * attended * sig * (1.0 + g * (1.0 - sig))
    ).astype(bf16)
    g_value[...] = values


def near(x):
    return pltpu.with_memory_space_constraint(x, pltpu.VMEM)


def call(kernel, name, out_shape, *args, scalars=0, lazy=0, far=False, scratch=()):
    whole = pl.BlockSpec(memory_space=pltpu.VMEM)
    specs = [pl.BlockSpec(memory_space=pltpu.SMEM)] * scalars
    specs += [whole] * (len(args) - scalars - lazy)
    specs += [pl.BlockSpec(memory_space=pl.ANY)] * lazy
    outs = jax.tree.map(lambda s: whole, out_shape)
    if not far:
        out_shape = jax.tree.map(lambda s: pltpu.VMEM(s.shape, s.dtype), out_shape)
    return pl.pallas_call(
        kernel,
        name=name,
        out_shape=out_shape,
        in_specs=specs,
        out_specs=outs,
        scratch_shapes=scratch,
    )(*args)


def window(size):
    return pltpu.VMEM((H, size, TOK), bf16), pltpu.SemaphoreType.DMA(())


def shape(dims, kind):
    return jax.ShapeDtypeStruct(dims, kind)


def swap(x, axis):
    return near(lax.all_to_all(x, axis, 0, 0, tiled=True))


def body(hidden_in, qk_weight, conv_weight, values, gate_in, cotangent):
    tokens = hidden_in[0]
    supers = lax.axis_size(SUPER)
    others = lax.axis_size(OTHER)
    model = tokens.shape[1]
    chunks, width = H // WIDE, TOK * WIDE
    place = jnp.stack([lax.axis_index(SUPER), lax.axis_index("g")]).astype(jnp.int32)
    taps = (pltpu.VMEM((2 * H * F, 8), f32),)
    packed = call(
        pack_kernel,
        "pack",
        shape((H, ROWS, TOK), bf16),
        tokens,
        qk_weight,
        values[0],
        gate_in[0],
        cotangent[0],
    )
    data = lax.all_to_all(packed, "g", 0, 0, tiled=True)
    own = call(
        state_kernel,
        "state",
        shape((supers, SENT, 2 * DV), bf16),
        place,
        near(data),
        conv_weight,
        scalars=1,
        scratch=taps,
    )
    done, gq, gk, gv, parts, keys, edges, sent = call(
        main_kernel,
        "main",
        (
            shape((H, DV, TOK), bf16),
            shape((chunks, F, width), f32),
            shape((chunks, F, width), f32),
            shape((chunks, DV, width), f32),
            shape((chunks, FEAT, 2 * DV), f32),
            shape((chunks, F, width), f32),
            shape((2 * F + DV, 2 * DV), f32),
            shape((supers, SENT, 2 * DV), bf16),
        ),
        place,
        near(data),
        swap(own, SUPER),
        conv_weight,
        scalars=1,
        far=True,
        scratch=taps,
    )
    back = call(
        back_kernel,
        "back",
        shape((H, FIRST + 2 * DV, TOK), bf16),
        place,
        swap(sent, SUPER),
        done,
        gq,
        gk,
        gv,
        parts,
        keys,
        edges,
        conv_weight,
        data,
        scalars=1,
        lazy=1,
        scratch=taps + window(DV),
    )
    back = swap(back, "g")
    partial, own_grad = call(
        weight_kernel,
        "weight",
        (
            shape((others, model // H // others, 2 * H * F), bf16),
            shape((2 * H * F, TOK), bf16),
        ),
        place,
        back,
        data,
        scalars=1,
        lazy=1,
        scratch=window(HID),
    )
    deep = model // H // others
    some = swap(partial, OTHER)
    summed = call(
        sum_kernel, "sum_a", shape((lax.axis_size("z"), deep, 2 * H * F), bf16), some
    )
    summed = call(
        sum_kernel, "sum_b", shape((H * others, deep, 2 * H * F), bf16), swap(summed, "z")
    )
    grad_qk_weight = lax.all_to_all(summed, ("g",) + OTHER, 0, 0, tiled=True)
    grad_qk_weight = grad_qk_weight.reshape(model, 2 * H * F)
    output, grad_gate, grad_values = call(
        unpack_kernel,
        "unpack",
        (shape((TOK, H * DV), bf16),) * 3,
        back,
        gate_in[0],
        cotangent[0],
        far=True,
    )
    grad_hidden = call(
        hidden_kernel,
        "hidden",
        shape((TOK, model), bf16),
        near(own_grad),
        qk_weight,
        far=True,
    )
    return output[None], grad_hidden[None], grad_values[None], grad_gate[None], grad_qk_weight


def solution(mesh):
    pairs, blocks = mesh.devices.shape
    y = 4 if blocks // H % 4 == 0 else 1
    fine = Mesh(
        mesh.devices.reshape(pairs, y, blocks // H // y, H), ("dp", "y", "z", "g")
    )
    split = P("dp", ("y", "z", "g"), None)
    return jax.shard_map(
        body,
        mesh=fine,
        in_specs=(split, P(), P(), split, split, split),
        out_specs=(split, split, split, split, P()),
        check_vma=False,
    )
```

```python
import math

import jax
import jax.numpy as jnp
from jax import lax
from jax.experimental import pallas as pl
from jax.experimental.pallas import tpu as pltpu
from jax.sharding import Mesh, PartitionSpec as P

H = 8
F = 16
DV = 64
KCONV = 3
SUPER = ("y", "z")
OTHER = ("dp", "y")
GROUP = ("h", "core")
TOK = 128
HID = 256
AT_V, AT_G, AT_P = HID, HID + DV, HID + 2 * DV
ROWS = AT_P + 2 * F
FEAT = 160
SENT = FEAT // 2 + 16
WIDE = 2
FIRST = 2 * F * H
SPARE = 32
f32 = jnp.float32
bf16 = jnp.bfloat16
NN = ((1,), (0,))
NT = ((1,), (1,))
TN = ((0,), (0,))


def mm(a, b, dims):
    return lax.dot_general(a, b, (dims, ((), ())), preferred_element_type=f32)


def halves(x):
    high = x.astype(bf16)
    return high, (x - high.astype(f32)).astype(bf16)


def mm3(a, b, dims):
    (ah, al), (bh, bl) = a, b
    return mm(ah, bh, dims) + (mm(ah, bl, dims) + mm(al, bh, dims))


def feature_scale(d):
    return F**-0.5 * (math.sqrt(0.5) if d == 0 else 1.0)


def up(x, d):
    return x if d == 0 else jnp.concatenate([x[d:], x[:d]], 0)


def features(x):
    rows = [x * F**-0.25]
    for d in range(F // 2):
        rows.append(x * up(x, d) * feature_scale(d))
    half = F // 2
    rows.append(x[:half] * x[half:] * feature_scale(half))
    row = lax.broadcasted_iota(jnp.int32, (8, x.shape[1]), 0)
    rows.append(jnp.where(row == 0, 1.0, 0.0))
    return jnp.concatenate(rows, 0)


def features_back(x, grads):
    total = grads[:F] * F**-0.25
    half = F // 2
    for d in range(half):
        part = grads[F * (d + 1) : F * (d + 2)] * feature_scale(d)
        total = total + part * up(x, d) + up(part * x, (F - d) % F)
    part = grads[F * (half + 1) : F * (half + 1) + half] * feature_scale(half)
    return total + jnp.concatenate([part * x[half:], part * x[:half]], 0)


def pack_state(state, extra):
    half = FEAT // 2
    lane = lax.broadcasted_iota(jnp.int32, (half, 2 * DV), 1)
    main = jnp.where(lane < DV, state[:half], pltpu.roll(state[half:], DV, 1))
    high, low = halves(state)
    high, low = high.astype(f32), low.astype(f32)
    small = lane[:16]
    sums = jnp.zeros((16, 2 * DV), f32)
    for i in range(FEAT // 16):
        sums = jnp.where(small == i, high[16 * i : 16 * i + 16, DV : DV + 1], sums)
        sums = jnp.where(small == i + 16, low[16 * i : 16 * i + 16, DV : DV + 1], sums)
    for i, column in enumerate(extra):
        sums = jnp.where(small == SPARE + i, column.astype(f32), sums)
    return jnp.concatenate([main, sums], 0).astype(bf16)


def unpack_state(total):
    half = FEAT // 2
    main = total[:half]
    main = jnp.concatenate([main, pltpu.roll(main, DV, 1)], 0)
    sums = total[half:]
    sums = sums + pltpu.roll(sums, 2 * DV - 16, 1)
    column = jnp.concatenate([sums[:, i : i + 1] for i in range(FEAT // 16)], 0)
    lane = lax.broadcasted_iota(jnp.int32, (FEAT, 2 * DV), 1)
    return jnp.where(lane < DV, main, jnp.where(lane == DV, column, 0.0))


def repeat_into(out, value):
    for i in range(out.shape[0]):
        out[i] = value


def wide_values(values):
    row = lax.broadcasted_iota(jnp.int32, (DV, values.shape[1]), 0)
    return jnp.concatenate([values, jnp.where(row == 0, 1.0, 0.0).astype(bf16)], 0)


def rows_of(ref, chunk, start, size):
    return jnp.concatenate(
        [ref[WIDE * chunk + i, start : start + size] for i in range(WIDE)], 1
    )


def head_taps(conv, columns, head):
    padded = jnp.concatenate([conv[...], jnp.zeros((8 - KCONV, 2 * H * F), f32)], 0)
    columns[...] = padded.T
    at = pl.multiple_of(F * head, F)
    return jnp.concatenate([columns[pl.ds(at, F)], columns[pl.ds(H * F + at, F)]], 0)


def convolve(now, before, taps):
    return (
        taps[:, 0:1] * now
        + taps[:, 1:2] * jnp.concatenate([before[:, 1:2], now[:, :-1]], 1)
        + taps[:, 2:3] * jnp.concatenate([before, now[:, :-2]], 1)
    )


def first_tokens(states, taps):
    rows, lanes = F, 2 * DV
    lane = lax.broadcasted_iota(jnp.int32, (rows, lanes), 1)
    raw, vals = jnp.zeros((rows, lanes), f32), jnp.zeros((rows, lanes), f32)
    for b in range(states.shape[0]):
        tile = states[b, FEAT // 2 : SENT].astype(f32)
        here = (lane >= 8 * b) & (lane < 8 * (b + 1))
        raw = jnp.where(here, pltpu.roll(tile, (8 * b - SPARE) % lanes, 1), raw)
        vals = jnp.where(here, pltpu.roll(tile, (8 * b - SPARE - 8) % lanes, 1), vals)
    prev = jnp.where(lane < 8, 0.0, pltpu.roll(raw, 8, 1))
    one = jnp.where(
        lane % 4 == 0, pltpu.roll(prev, lanes - 3, 1), pltpu.roll(raw, 1, 1)
    )
    two = pltpu.roll(prev, lanes - 2, 1)
    q, k = (
        t[:, 0:1] * raw + t[:, 1:2] * one + t[:, 2:3] * two for t in (taps[:F], taps[F:])
    )
    v = jnp.concatenate(
        [vals if j == 0 else pltpu.roll(vals, lanes - 2 * j, 1) for j in range(DV // F)], 0
    )
    return q, k, v


def sum_kernel(data, out):
    total = data[0].astype(f32)
    for i in range(1, data.shape[0]):
        total = total + data[i].astype(f32)
    repeat_into(out, total.astype(bf16))


def pack_kernel(tokens, weight, values, gate, cot, out):
    x = tokens[...]
    projected = mm(x, weight[...], NN).T.astype(bf16)
    g = gate[...].astype(f32)
    v = values[...].T
    up = (cot[...].astype(f32) * (g * jax.nn.sigmoid(g))).astype(bf16).T
    width = H * F
    for h in range(H):
        out[h, AT_P : AT_P + F] = projected[F * h : F * (h + 1)]
        out[h, AT_P + F : ROWS] = projected[width + F * h : width + F * (h + 1)]
        cols = slice(DV * h, DV * (h + 1))
        out[h, AT_V : AT_V + DV] = v[cols]
        out[h, AT_G : AT_G + DV] = up[cols]
        for i in range(x.shape[1] // H // TOK):
            start = x.shape[1] // H * h + TOK * i
            out[h, TOK * i : TOK * (i + 1)] = x[:, start : start + TOK]


def state_kernel(place, data, conv, out, columns):
    taps = head_taps(conv, columns, place[1])[F:]
    total = jnp.zeros((FEAT, 2 * DV), f32)
    before = jnp.zeros((F, 2), f32)
    for c in range(H // WIDE):
        raw = rows_of(data, c, AT_P + F, F).astype(f32)
        feat = features(convolve(raw, before, taps))
        if c == 0:
            token = lax.broadcasted_iota(jnp.int32, feat.shape, 1)
            feat = jnp.where(token < KCONV - 1, 0.0, feat)
        before = raw[:, -2:]
        high, low = halves(feat)
        v = wide_values(rows_of(data, c, AT_V, DV))
        total = total + (mm(high, v, NT) + mm(low, v, NT))
    first, last = data[0, AT_P:ROWS], data[H - 1, AT_P:ROWS]
    begin = data[0, AT_V : AT_V + DV]
    extra = []
    for start in (F, 0):
        rows = slice(start, start + F)
        extra += [first[rows, 0:1], first[rows, 1:2]]
        extra += [last[rows, TOK - 2 : TOK - 1], last[rows, TOK - 1 : TOK]]
    for j in range(DV // F):
        rows = slice(F * j, F * (j + 1))
        extra += [begin[rows, 0:1], begin[rows, 1:2]]
    repeat_into(out, pack_state(total, extra))


def main_kernel(place, data, states, conv, out, gq, gk, gv, parts, keys, edges, sent, columns):
    here = place[0]
    taps = head_taps(conv, columns, place[1])
    length = TOK * WIDE
    total = jnp.zeros((SENT, 2 * DV), f32)
    for b in range(states.shape[0]):
        total = total + states[b].astype(f32) * (b < here).astype(f32)
    first_q, first_k, first_v = first_tokens(states, taps)
    lane = lax.broadcasted_iota(jnp.int32, (FEAT, 2 * DV), 1)
    earlier = (lane % 8 < KCONV - 1) & (lane < 8 * here)
    feat = halves(jnp.where(earlier, features(first_k), 0.0))
    first_values = wide_values(first_v.astype(bf16))
    state = (
        unpack_state(total) + mm(feat[0], first_values, NT) + mm(feat[1], first_values, NT)
    )
    shift = 2 * DV * 2 - 8 * (here + 1)
    edges[0:F] = pltpu.roll(first_q, shift - 4, 1)
    edges[F : 2 * F] = pltpu.roll(first_k, shift, 1)
    edges[2 * F :] = pltpu.roll(first_v, shift, 1)
    tile = states[jnp.maximum(here - 1, 0), FEAT // 2 : SENT].astype(f32)
    tile = tile * (here > 0).astype(f32)
    before = jnp.concatenate(
        [tile[:, SPARE + 6 : SPARE + 8], tile[:, SPARE + 2 : SPARE + 4]], 0
    )
    k_at = lax.broadcasted_iota(jnp.int32, (length, length), 0)
    q_at = lax.broadcasted_iota(jnp.int32, (length, length), 1)
    causal = k_at <= q_at
    whole = jnp.zeros((FEAT, 2 * DV), f32)
    for c in range(H // WIDE):
        raw = rows_of(data, c, AT_P, 2 * F).astype(f32)
        mixed = convolve(raw, before, taps)
        before = raw[:, -2:]
        q, k = mixed[:F], mixed[F:]
        (qh, ql), (kh, kl) = halves(q * F**-0.5), halves(k)
        keys[c] = k
        v = wide_values(rows_of(data, c, AT_V, DV))
        g_att = rows_of(data, c, AT_G, DV).astype(f32)
        near_one = 1.0 + mm(
            jnp.concatenate([kh, kh, kl], 0), jnp.concatenate([qh, ql, qh], 0), TN
        )
        weights = jnp.where(causal, 0.5 + 0.5 * near_one * near_one, 0.0).astype(bf16)
        q_feat, k_feat = halves(features(q)), halves(features(k))
        split_state = halves(state)
        numer = mm(v, weights, NN) + mm3(split_state, q_feat, TN)
        inverse = 1.0 / numer[DV : DV + 1]
        attended = numer[:DV] * inverse
        result = attended.astype(bf16)
        g_num = g_att * inverse
        g_den = -jnp.sum(g_att * attended, 0, keepdims=True) * inverse
        row = lax.broadcasted_iota(jnp.int32, (DV, length), 0)
        wide = jnp.concatenate([g_num, jnp.where(row == 0, g_den, 0.0)], 0)
        grads = halves(wide)
        g_weights = mm(v, grads[0], TN) + mm(v, grads[1], TN)
        g_scores = jnp.where(causal, g_weights * near_one, 0.0).astype(bf16)
        g_local = (mm(kh, g_scores, NN) + mm(kl, g_scores, NN)) * F**-0.5
        g_query = g_local + features_back(q, mm3(split_state, grads, NN))
        if c == 0:
            extra = [g_query[:, 0:1], g_query[:, 1:2]]
            for j in range(DV // F + 1):
                column = wide[F * j : F * (j + 1), 0:1]
                high = column.astype(bf16)
                extra += [high, column - high.astype(f32)]
        g_key = mm(qh, g_scores, NT) + mm(ql, g_scores, NT)
        g_value = mm(grads[0][:DV], weights, NT) + mm(grads[1][:DV], weights, NT)
        part = mm3(q_feat, grads, NT)
        whole = whole + part
        parts[c] = part
        state = state + (mm(k_feat[0], v, NT) + mm(k_feat[1], v, NT))
        for i in range(WIDE):
            cols = slice(TOK * i, TOK * (i + 1))
            out[WIDE * c + i] = result[:, cols]
        gq[c] = g_query
        gk[c] = g_key
        gv[c] = g_value
    repeat_into(sent, pack_state(whole, extra))


def back_kernel(
    place, states, done, gq, gk, gv, parts, keys, edges, conv, far, out, columns, data, sem
):
    fetch = pltpu.make_async_copy(far.at[:, AT_V : AT_V + DV], data, sem)
    fetch.start()
    here = place[0]
    taps = head_taps(conv, columns, place[1])
    count = states.shape[0]
    total = jnp.zeros((SENT, 2 * DV), f32)
    for b in range(count):
        total = total + states[b].astype(f32) * (b > here).astype(f32)
    state = unpack_state(total)
    tile = states[jnp.minimum(here + 1, count - 1), FEAT // 2 : SENT].astype(f32)
    edge = edges[...]
    edge_v = wide_values(edge[2 * F :].astype(bf16))
    split_state = halves(state)
    column = jnp.concatenate(
        [
            tile[:, SPARE + 2 + 2 * j : SPARE + 3 + 2 * j]
            + tile[:, SPARE + 3 + 2 * j : SPARE + 4 + 2 * j]
            for j in range(DV // F + 1)
        ],
        0,
    )
    pair = jnp.sum(column * edge_v[: DV + F].astype(f32), 0, keepdims=True)
    lane = lax.broadcasted_iota(jnp.int32, (FEAT, 2 * DV), 1)
    g_feat = mm(split_state[0], edge_v, NN) + mm(split_state[1], edge_v, NN)
    g_feat = g_feat - jnp.where(lane == 1, features(edge[:F])[:, 0:1] * pair, 0.0)
    after = jnp.concatenate(
        [tile[:, SPARE : SPARE + 2], features_back(edge[F : 2 * F], g_feat)[:, 0:2]], 0
    ) * (here + 1 < count).astype(f32)
    fetch.wait()
    for c in reversed(range(H // WIDE)):
        k = keys[c]
        v = wide_values(rows_of(data, c, 0, DV))
        k_feat = halves(features(k))
        split_state = halves(state)
        g_feat = mm(split_state[0], v, NN) + mm(split_state[1], v, NN)
        g_key = gk[c] + features_back(k, g_feat)
        g_value = (gv[c] + mm3(split_state, k_feat, TN)[:DV]).astype(bf16)
        state = state + parts[c]
        now = jnp.concatenate([gq[c], g_key], 0)
        total = (
            taps[:, 0:1] * now
            + taps[:, 1:2] * jnp.concatenate([now[:, 1:], after[:, 0:1]], 1)
            + taps[:, 2:3] * jnp.concatenate([now[:, 2:], after], 1)
        ).astype(bf16)
        after = now[:, 0:2]
        for i in range(WIDE):
            cols = slice(TOK * i, TOK * (i + 1))
            b = WIDE * c + i
            out[b, FIRST : FIRST + DV] = done[b]
            out[b, FIRST + DV : FIRST + 2 * DV] = g_value[:, cols]
            for dest in range(H):
                out[dest, 2 * F * b : 2 * F * (b + 1)] = total[:, cols]

def stacked(grads, block):
    return jnp.concatenate(
        [
            grads[h, pl.ds(2 * F * block + at, F)]
            for at in (0, F)
            for h in range(H)
        ],
        0,
    )


def weight_kernel(place, grads, far, out, own, data, sem):
    fetch = pltpu.make_async_copy(far.at[:, 0:HID], data, sem)
    fetch.start()
    own[...] = stacked(grads, place[1])
    total = jnp.concatenate([stacked(grads, b) for b in range(H)], 1).T
    count, rows = out.shape[:2]
    parts = count * rows // TOK
    fetch.wait()
    for i in range(parts):
        at = TOK * i
        tokens = jnp.concatenate([data[b, at : at + TOK] for b in range(H)], 0)
        result = mm(tokens, total, TN).astype(bf16)
        for j in range(count // parts):
            out[i * (count // parts) + j] = result[rows * j : rows * (j + 1)]


def join_kernel(place, mine, theirs, out, sems):
    core = place[1] % 2
    copies = []
    for h in range(H // 2):
        for i, (part, at) in enumerate(((mine, core), (theirs, 1 - core))):
            copies.append(
                pltpu.make_async_copy(part.at[h], out.at[2 * h + at], sems.at[2 * h + i])
            )
    for copy in copies:
        copy.start()
    for copy in copies:
        copy.wait()


def hidden_kernel(own, weight, out):
    out[...] = mm(own[...].T, weight[...], NT).astype(bf16)


def unpack_kernel(data, gate, cot, output, g_gate, g_value):
    attended, values = (
        jnp.concatenate([data[h, at : at + DV] for h in range(H)], 0).T
        for at in (FIRST, FIRST + DV)
    )
    g = gate[...].astype(f32)
    sig = jax.nn.sigmoid(g)
    attended = attended.astype(f32)
    output[...] = (attended * (g * sig)).astype(bf16)
    g_gate[...] = (
        cot[...].astype(f32) * attended * sig * (1.0 + g * (1.0 - sig))
    ).astype(bf16)
    g_value[...] = values


def near(x):
    return pltpu.with_memory_space_constraint(x, pltpu.VMEM)


def call(kernel, name, out_shape, *args, scalars=0, lazy=0, far=False, results=pltpu.VMEM, scratch=()):
    whole = pl.BlockSpec(memory_space=pltpu.VMEM)
    specs = [pl.BlockSpec(memory_space=pltpu.SMEM)] * scalars
    specs += [whole] * (len(args) - scalars - lazy)
    specs += [pl.BlockSpec(memory_space=pl.ANY)] * lazy
    outs = jax.tree.map(lambda s: pl.BlockSpec(memory_space=results), out_shape)
    if not far:
        out_shape = jax.tree.map(lambda s: pltpu.VMEM(s.shape, s.dtype), out_shape)
    return pl.pallas_call(
        kernel,
        name=name,
        out_shape=out_shape,
        in_specs=specs,
        out_specs=outs,
        scratch_shapes=scratch,
    )(*args)


def window(size):
    return pltpu.VMEM((H, size, TOK), bf16), pltpu.SemaphoreType.DMA(())


def shape(dims, kind):
    return jax.ShapeDtypeStruct(dims, kind)


def swap(x, axis):
    return near(lax.all_to_all(x, axis, 0, 0, tiled=True))


def body(hidden_in, qk_weight, conv_weight, values, gate_in, cotangent):
    tokens = hidden_in[0]
    supers = lax.axis_size(SUPER)
    others = lax.axis_size(OTHER)
    model = tokens.shape[1]
    chunks, width = H // WIDE, TOK * WIDE
    place = jnp.stack([lax.axis_index(SUPER), lax.axis_index(GROUP)]).astype(jnp.int32)
    taps = (pltpu.VMEM((2 * H * F, 8), f32),)
    packed = call(
        pack_kernel,
        "pack",
        shape((H, ROWS, TOK), bf16),
        tokens,
        qk_weight,
        values[0],
        gate_in[0],
        cotangent[0],
    )
    data = lax.all_to_all(packed, GROUP, 0, 0, tiled=True)
    own = call(
        state_kernel,
        "state",
        shape((supers, SENT, 2 * DV), bf16),
        place,
        near(data),
        conv_weight,
        scalars=1,
        scratch=taps,
    )
    done, gq, gk, gv, parts, keys, edges, sent = call(
        main_kernel,
        "main",
        (
            shape((H, DV, TOK), bf16),
            shape((chunks, F, width), f32),
            shape((chunks, F, width), f32),
            shape((chunks, DV, width), f32),
            shape((chunks, FEAT, 2 * DV), f32),
            shape((chunks, F, width), f32),
            shape((2 * F + DV, 2 * DV), f32),
            shape((supers, SENT, 2 * DV), bf16),
        ),
        place,
        near(data),
        swap(own, SUPER),
        conv_weight,
        scalars=1,
        far=True,
        scratch=taps,
    )
    back = call(
        back_kernel,
        "back",
        shape((H, FIRST + 2 * DV, TOK), bf16),
        place,
        swap(sent, SUPER),
        done,
        gq,
        gk,
        gv,
        parts,
        keys,
        edges,
        conv_weight,
        data,
        scalars=1,
        lazy=1,
        scratch=taps + window(DV),
    )
    back = swap(back, GROUP)
    partial, own_grad = call(
        weight_kernel,
        "weight",
        (
            shape((others, model // H // others, 2 * H * F), bf16),
            shape((2 * H * F, TOK), bf16),
        ),
        place,
        back,
        data,
        scalars=1,
        lazy=1,
        scratch=window(HID),
    )
    deep = model // H // others
    some = swap(partial, OTHER)
    summed = call(
        sum_kernel, "sum_a", shape((lax.axis_size("z"), deep, 2 * H * F), bf16), some
    )
    summed = call(
        sum_kernel, "sum_b", shape((H // 2 * others, deep, 2 * H * F), bf16), swap(summed, "z")
    )
    mine = lax.all_to_all(summed, ("h",) + OTHER, 0, 0, tiled=True)
    mine = mine.reshape(H // 2, model // H, 2 * H * F)
    output, grad_gate, grad_values = call(
        unpack_kernel,
        "unpack",
        (shape((TOK, H * DV), bf16),) * 3,
        back,
        gate_in[0],
        cotangent[0],
        far=True,
    )
    grad_hidden = call(
        hidden_kernel,
        "hidden",
        shape((TOK, model), bf16),
        near(own_grad),
        qk_weight,
        far=True,
    )
    mine, output, grad_hidden = lax.optimization_barrier((mine, output, grad_hidden))
    theirs = lax.ppermute(mine, "core", [(0, 1), (1, 0)])
    grad_qk_weight = call(
        join_kernel,
        "join",
        shape((H, model // H, 2 * H * F), bf16),
        place,
        near(mine),
        near(theirs),
        scalars=1,
        lazy=2,
        far=True,
        results=pl.ANY,
        scratch=(pltpu.SemaphoreType.DMA((H,)),),
    ).reshape(model, 2 * H * F)
    return output[None], grad_hidden[None], grad_values[None], grad_gate[None], grad_qk_weight


def solution(mesh):
    pairs, blocks = mesh.devices.shape
    y = 4 if blocks // H % 4 == 0 else 1
    fine = Mesh(
        mesh.devices.reshape(pairs, y, blocks // H // y, H // 2, 2),
        ("dp", "y", "z", "h", "core"),
    )
    split = P("dp", SUPER + GROUP, None)
    return jax.shard_map(
        body,
        mesh=fine,
        in_specs=(split, P(), P(), split, split, split),
        out_specs=(split, split, split, split, P()),
        check_vma=False,
    )
```

```python
import math

import jax
import jax.numpy as jnp
from jax import lax
from jax.experimental import pallas as pl
from jax.experimental.pallas import tpu as pltpu
from jax.sharding import Mesh, PartitionSpec as P

H = 8
F = 16
DV = 64
KCONV = 3
SUPER = ("y", "z")
OTHER = ("dp", "y")
GROUP = ("h", "core")
TOK = 128
HID = 256
AT_V, AT_G, AT_P = HID, HID + DV, HID + 2 * DV
ROWS = AT_P + 2 * F
FEAT = 160
SENT = FEAT // 2 + 16
WIDE = 2
FIRST = 2 * F * H
SPARE = 32
f32 = jnp.float32
bf16 = jnp.bfloat16
NN = ((1,), (0,))
NT = ((1,), (1,))
TN = ((0,), (0,))


def mm(a, b, dims):
    return lax.dot_general(a, b, (dims, ((), ())), preferred_element_type=f32)


def halves(x):
    high = x.astype(bf16)
    return high, (x - high.astype(f32)).astype(bf16)


def feature_scale(d):
    return F**-0.5 * (math.sqrt(0.5) if d == 0 else 1.0)


def up(x, d):
    return x if d == 0 else jnp.concatenate([x[d:], x[:d]], 0)


def features(x):
    rows = [x * F**-0.25]
    for d in range(F // 2):
        rows.append(x * up(x, d) * feature_scale(d))
    half = F // 2
    rows.append(x[:half] * x[half:] * feature_scale(half))
    row = lax.broadcasted_iota(jnp.int32, (8, x.shape[1]), 0)
    rows.append(jnp.where(row == 0, 1.0, 0.0))
    return jnp.concatenate(rows, 0)


def features_back(x, grads):
    total = grads[:F] * F**-0.25
    half = F // 2
    for d in range(half):
        part = grads[F * (d + 1) : F * (d + 2)] * feature_scale(d)
        total = total + part * up(x, d) + up(part * x, (F - d) % F)
    part = grads[F * (half + 1) : F * (half + 1) + half] * feature_scale(half)
    return total + jnp.concatenate([part * x[half:], part * x[:half]], 0)


def pack_state(state, extra):
    half = FEAT // 2
    lane = lax.broadcasted_iota(jnp.int32, (half, 2 * DV), 1)
    main = jnp.where(lane < DV, state[:half], pltpu.roll(state[half:], DV, 1))
    high, low = halves(state)
    high, low = high.astype(f32), low.astype(f32)
    small = lane[:16]
    sums = jnp.zeros((16, 2 * DV), f32)
    for i in range(FEAT // 16):
        sums = jnp.where(small == i, high[16 * i : 16 * i + 16, DV : DV + 1], sums)
        sums = jnp.where(small == i + 16, low[16 * i : 16 * i + 16, DV : DV + 1], sums)
    for i, column in enumerate(extra):
        sums = jnp.where(small == SPARE + i, column.astype(f32), sums)
    return jnp.concatenate([main, sums], 0).astype(bf16)


def unpack_state(total):
    half = FEAT // 2
    main = total[:half]
    main = jnp.concatenate([main, pltpu.roll(main, DV, 1)], 0)
    sums = total[half:]
    sums = sums + pltpu.roll(sums, 2 * DV - 16, 1)
    column = jnp.concatenate([sums[:, i : i + 1] for i in range(FEAT // 16)], 0)
    lane = lax.broadcasted_iota(jnp.int32, (FEAT, 2 * DV), 1)
    return jnp.where(lane < DV, main, jnp.where(lane == DV, column, 0.0))


def repeat_into(out, value):
    for i in range(out.shape[0]):
        out[i] = value


def wide_values(values):
    row = lax.broadcasted_iota(jnp.int32, (DV, values.shape[1]), 0)
    return jnp.concatenate([values, jnp.where(row == 0, 1.0, 0.0).astype(bf16)], 0)


def rows_of(ref, chunk, start, size):
    return jnp.concatenate(
        [ref[WIDE * chunk + i, start : start + size] for i in range(WIDE)], 1
    )


def head_taps(conv, columns, head):
    padded = jnp.concatenate([conv[...], jnp.zeros((8 - KCONV, 2 * H * F), f32)], 0)
    columns[...] = padded.T
    at = pl.multiple_of(F * head, F)
    return jnp.concatenate([columns[pl.ds(at, F)], columns[pl.ds(H * F + at, F)]], 0)


def convolve(now, before, taps):
    return (
        taps[:, 0:1] * now
        + taps[:, 1:2] * jnp.concatenate([before[:, 1:2], now[:, :-1]], 1)
        + taps[:, 2:3] * jnp.concatenate([before, now[:, :-2]], 1)
    )


def first_tokens(states, taps):
    rows, lanes = F, 2 * DV
    lane = lax.broadcasted_iota(jnp.int32, (rows, lanes), 1)
    raw, vals = jnp.zeros((rows, lanes), f32), jnp.zeros((rows, lanes), f32)
    for b in range(states.shape[0]):
        tile = states[b, FEAT // 2 : SENT].astype(f32)
        here = (lane >= 8 * b) & (lane < 8 * (b + 1))
        raw = jnp.where(here, pltpu.roll(tile, (8 * b - SPARE) % lanes, 1), raw)
        vals = jnp.where(here, pltpu.roll(tile, (8 * b - SPARE - 8) % lanes, 1), vals)
    prev = jnp.where(lane < 8, 0.0, pltpu.roll(raw, 8, 1))
    one = jnp.where(
        lane % 4 == 0, pltpu.roll(prev, lanes - 3, 1), pltpu.roll(raw, 1, 1)
    )
    two = pltpu.roll(prev, lanes - 2, 1)
    q, k = (
        t[:, 0:1] * raw + t[:, 1:2] * one + t[:, 2:3] * two for t in (taps[:F], taps[F:])
    )
    v = jnp.concatenate(
        [vals if j == 0 else pltpu.roll(vals, lanes - 2 * j, 1) for j in range(DV // F)], 0
    )
    return q, k, v


def sum_kernel(data, out):
    total = data[0].astype(f32)
    for i in range(1, data.shape[0]):
        total = total + data[i].astype(f32)
    repeat_into(out, total.astype(bf16))


def pack_kernel(tokens, weight, values, gate, cot, out):
    x = tokens[...]
    projected = mm(x, weight[...], NN).T.astype(bf16)
    g = gate[...].astype(f32)
    v = values[...].T
    up = (cot[...].astype(f32) * (g * jax.nn.sigmoid(g))).astype(bf16).T
    width = H * F
    for h in range(H):
        out[h, AT_P : AT_P + F] = projected[F * h : F * (h + 1)]
        out[h, AT_P + F : ROWS] = projected[width + F * h : width + F * (h + 1)]
        cols = slice(DV * h, DV * (h + 1))
        out[h, AT_V : AT_V + DV] = v[cols]
        out[h, AT_G : AT_G + DV] = up[cols]
        for i in range(x.shape[1] // H // TOK):
            start = x.shape[1] // H * h + TOK * i
            out[h, TOK * i : TOK * (i + 1)] = x[:, start : start + TOK]


def state_kernel(place, data, conv, out, columns):
    taps = head_taps(conv, columns, place[1])[F:]
    total = jnp.zeros((FEAT, 2 * DV), f32)
    before = jnp.zeros((F, 2), f32)
    for c in range(H // WIDE):
        raw = rows_of(data, c, AT_P + F, F).astype(f32)
        feat = features(convolve(raw, before, taps))
        if c == 0:
            token = lax.broadcasted_iota(jnp.int32, feat.shape, 1)
            feat = jnp.where(token < KCONV - 1, 0.0, feat)
        before = raw[:, -2:]
        high, low = halves(feat)
        v = wide_values(rows_of(data, c, AT_V, DV))
        total = total + (mm(high, v, NT) + mm(low, v, NT))
    first, last = data[0, AT_P:ROWS], data[H - 1, AT_P:ROWS]
    begin = data[0, AT_V : AT_V + DV]
    extra = []
    for start in (F, 0):
        rows = slice(start, start + F)
        extra += [first[rows, 0:1], first[rows, 1:2]]
        extra += [last[rows, TOK - 2 : TOK - 1], last[rows, TOK - 1 : TOK]]
    for j in range(DV // F):
        rows = slice(F * j, F * (j + 1))
        extra += [begin[rows, 0:1], begin[rows, 1:2]]
    repeat_into(out, pack_state(total, extra))


def main_kernel(place, data, states, conv, out, saved, parts, edges, sent, columns):
    here = place[0]
    taps = head_taps(conv, columns, place[1])
    length = TOK * WIDE
    total = jnp.zeros((SENT, 2 * DV), f32)
    for b in range(states.shape[0]):
        total = total + states[b].astype(f32) * (b < here).astype(f32)
    first_q, first_k, first_v = first_tokens(states, taps)
    lane = lax.broadcasted_iota(jnp.int32, (FEAT, 2 * DV), 1)
    earlier = (lane % 8 < KCONV - 1) & (lane < 8 * here)
    feat = halves(jnp.where(earlier, features(first_k), 0.0))
    first_values = wide_values(first_v.astype(bf16))
    state = (
        unpack_state(total) + mm(feat[0], first_values, NT) + mm(feat[1], first_values, NT)
    )
    shift = 2 * DV * 2 - 8 * (here + 1)
    edges[0:F] = pltpu.roll(first_q, shift - 4, 1)
    edges[F : 2 * F] = pltpu.roll(first_k, shift, 1)
    edges[2 * F :] = pltpu.roll(first_v, shift, 1)
    tile = states[jnp.maximum(here - 1, 0), FEAT // 2 : SENT].astype(f32)
    tile = tile * (here > 0).astype(f32)
    before = jnp.concatenate(
        [tile[:, SPARE + 6 : SPARE + 8], tile[:, SPARE + 2 : SPARE + 4]], 0
    )
    k_at = lax.broadcasted_iota(jnp.int32, (length, length), 0)
    q_at = lax.broadcasted_iota(jnp.int32, (length, length), 1)
    causal = k_at <= q_at
    whole = jnp.zeros((FEAT, 2 * DV), f32)
    for c in range(H // WIDE):
        raw = rows_of(data, c, AT_P, 2 * F).astype(f32)
        mixed = convolve(raw, before, taps)
        before = raw[:, -2:]
        q, k = mixed[:F], mixed[F:]
        (qh, ql), (kh, kl) = halves(q * F**-0.5), halves(k)
        saved[c, 2 * F : 3 * F] = k
        v = wide_values(rows_of(data, c, AT_V, DV))
        g_att = rows_of(data, c, AT_G, DV).astype(f32)
        near_one = 1.0 + mm(
            jnp.concatenate([kh, kh, kl], 0), jnp.concatenate([qh, ql, qh], 0), TN
        )
        weights = jnp.where(causal, 0.5 + 0.5 * near_one * near_one, 0.0).astype(bf16)
        q_feat, k_feat = features(q).astype(bf16), features(k).astype(bf16)
        held = state.astype(bf16)
        numer = mm(v, weights, NN) + mm(held, q_feat, TN)
        inverse = 1.0 / numer[DV : DV + 1]
        attended = numer[:DV] * inverse
        result = attended.astype(bf16)
        g_num = g_att * inverse
        g_den = -jnp.sum(g_att * attended, 0, keepdims=True) * inverse
        row = lax.broadcasted_iota(jnp.int32, (DV, length), 0)
        wide = jnp.concatenate([g_num, jnp.where(row == 0, g_den, 0.0)], 0)
        grads = halves(wide)
        g_weights = mm(v, grads[0], TN) + mm(v, grads[1], TN)
        g_scores = jnp.where(causal, g_weights * near_one, 0.0).astype(bf16)
        g_local = (mm(kh, g_scores, NN) + mm(kl, g_scores, NN)) * F**-0.5
        g_query = g_local + features_back(q, mm(held, grads[0], NN))
        if c == 0:
            extra = [g_query[:, 0:1], g_query[:, 1:2]]
            for j in range(DV // F + 1):
                column = wide[F * j : F * (j + 1), 0:1]
                high = column.astype(bf16)
                extra += [high, column - high.astype(f32)]
        g_key = mm(qh, g_scores, NT) + mm(ql, g_scores, NT)
        g_value = mm(grads[0][:DV], weights, NT) + mm(grads[1][:DV], weights, NT)
        part = mm(q_feat, grads[0], NT)
        whole = whole + part
        parts[c] = part.astype(bf16)
        state = state + mm(k_feat, v, NT)
        for i in range(WIDE):
            cols = slice(TOK * i, TOK * (i + 1))
            out[WIDE * c + i] = result[:, cols]
        saved[c, 0:F] = g_query
        saved[c, F : 2 * F] = g_key
        saved[c, 3 * F :] = g_value
    repeat_into(sent, pack_state(whole, extra))


def back_kernel(
    place, states, done, saved, parts, edges, conv, far, out, columns, data, sem
):
    fetch = pltpu.make_async_copy(far.at[:, AT_V : AT_V + DV], data, sem)
    fetch.start()
    here = place[0]
    taps = head_taps(conv, columns, place[1])
    count = states.shape[0]
    total = jnp.zeros((SENT, 2 * DV), f32)
    for b in range(count):
        total = total + states[b].astype(f32) * (b > here).astype(f32)
    state = unpack_state(total)
    tile = states[jnp.minimum(here + 1, count - 1), FEAT // 2 : SENT].astype(f32)
    edge = edges[...]
    edge_v = wide_values(edge[2 * F :].astype(bf16))
    split_state = halves(state)
    column = jnp.concatenate(
        [
            tile[:, SPARE + 2 + 2 * j : SPARE + 3 + 2 * j]
            + tile[:, SPARE + 3 + 2 * j : SPARE + 4 + 2 * j]
            for j in range(DV // F + 1)
        ],
        0,
    )
    pair = jnp.sum(column * edge_v[: DV + F].astype(f32), 0, keepdims=True)
    lane = lax.broadcasted_iota(jnp.int32, (FEAT, 2 * DV), 1)
    g_feat = mm(split_state[0], edge_v, NN) + mm(split_state[1], edge_v, NN)
    g_feat = g_feat - jnp.where(lane == 1, features(edge[:F])[:, 0:1] * pair, 0.0)
    after = jnp.concatenate(
        [tile[:, SPARE : SPARE + 2], features_back(edge[F : 2 * F], g_feat)[:, 0:2]], 0
    ) * (here + 1 < count).astype(f32)
    fetch.wait()
    for c in reversed(range(H // WIDE)):
        k = saved[c, 2 * F : 3 * F]
        v = wide_values(rows_of(data, c, 0, DV))
        k_feat = features(k).astype(bf16)
        held = state.astype(bf16)
        g_key = saved[c, F : 2 * F] + features_back(k, mm(held, v, NN))
        g_value = (saved[c, 3 * F :] + mm(held, k_feat, TN)[:DV]).astype(bf16)
        state = state + parts[c].astype(f32)
        now = jnp.concatenate([saved[c, 0:F], g_key], 0)
        total = (
            taps[:, 0:1] * now
            + taps[:, 1:2] * jnp.concatenate([now[:, 1:], after[:, 0:1]], 1)
            + taps[:, 2:3] * jnp.concatenate([now[:, 2:], after], 1)
        ).astype(bf16)
        after = now[:, 0:2]
        for i in range(WIDE):
            cols = slice(TOK * i, TOK * (i + 1))
            b = WIDE * c + i
            out[b, FIRST : FIRST + DV] = done[b]
            out[b, FIRST + DV : FIRST + 2 * DV] = g_value[:, cols]
            for dest in range(H):
                out[dest, 2 * F * b : 2 * F * (b + 1)] = total[:, cols]

def stacked(grads, block):
    return jnp.concatenate(
        [
            grads[h, pl.ds(2 * F * block + at, F)]
            for at in (0, F)
            for h in range(H)
        ],
        0,
    )


def weight_kernel(place, grads, far, out, own, data, sem):
    fetch = pltpu.make_async_copy(far.at[:, 0:HID], data, sem)
    fetch.start()
    own[...] = stacked(grads, place[1])
    total = jnp.concatenate([stacked(grads, b) for b in range(H)], 1).T
    count, rows = out.shape[:2]
    parts = count * rows // TOK
    fetch.wait()
    for i in range(parts):
        at = TOK * i
        tokens = jnp.concatenate([data[b, at : at + TOK] for b in range(H)], 0)
        result = mm(tokens, total, TN).astype(bf16)
        for j in range(count // parts):
            out[i * (count // parts) + j] = result[rows * j : rows * (j + 1)]


def join_kernel(place, mine, theirs, out, sems):
    core = place[1] % 2
    copies = []
    for h in range(H // 2):
        for i, (part, at) in enumerate(((mine, core), (theirs, 1 - core))):
            copies.append(
                pltpu.make_async_copy(part.at[h], out.at[2 * h + at], sems.at[2 * h + i])
            )
    for copy in copies:
        copy.start()
    for copy in copies:
        copy.wait()


def hidden_kernel(own, weight, out):
    out[...] = mm(own[...].T, weight[...], NT).astype(bf16)


def unpack_kernel(data, gate, cot, output, g_gate, g_value):
    attended, values = (
        jnp.concatenate([data[h, at : at + DV] for h in range(H)], 0).T
        for at in (FIRST, FIRST + DV)
    )
    g = gate[...].astype(f32)
    sig = jax.nn.sigmoid(g)
    attended = attended.astype(f32)
    output[...] = (attended * (g * sig)).astype(bf16)
    g_gate[...] = (
        cot[...].astype(f32) * attended * sig * (1.0 + g * (1.0 - sig))
    ).astype(bf16)
    g_value[...] = values


def near(x):
    return pltpu.with_memory_space_constraint(x, pltpu.VMEM)


def call(kernel, name, out_shape, *args, scalars=0, lazy=0, far=False, results=pltpu.VMEM, scratch=()):
    whole = pl.BlockSpec(memory_space=pltpu.VMEM)
    specs = [pl.BlockSpec(memory_space=pltpu.SMEM)] * scalars
    specs += [whole] * (len(args) - scalars - lazy)
    specs += [pl.BlockSpec(memory_space=pl.ANY)] * lazy
    outs = jax.tree.map(lambda s: pl.BlockSpec(memory_space=results), out_shape)
    if not far:
        out_shape = jax.tree.map(lambda s: pltpu.VMEM(s.shape, s.dtype), out_shape)
    return pl.pallas_call(
        kernel,
        name=name,
        out_shape=out_shape,
        in_specs=specs,
        out_specs=outs,
        scratch_shapes=scratch,
    )(*args)


def window(size):
    return pltpu.VMEM((H, size, TOK), bf16), pltpu.SemaphoreType.DMA(())


def shape(dims, kind):
    return jax.ShapeDtypeStruct(dims, kind)


def swap(x, axis):
    return near(lax.all_to_all(x, axis, 0, 0, tiled=True))


def body(hidden_in, qk_weight, conv_weight, values, gate_in, cotangent):
    tokens = hidden_in[0]
    supers = lax.axis_size(SUPER)
    others = lax.axis_size(OTHER)
    model = tokens.shape[1]
    chunks, width = H // WIDE, TOK * WIDE
    place = jnp.stack([lax.axis_index(SUPER), lax.axis_index(GROUP)]).astype(jnp.int32)
    taps = (pltpu.VMEM((2 * H * F, 8), f32),)
    packed = call(
        pack_kernel,
        "pack",
        shape((H, ROWS, TOK), bf16),
        tokens,
        qk_weight,
        values[0],
        gate_in[0],
        cotangent[0],
    )
    data = lax.all_to_all(packed, GROUP, 0, 0, tiled=True)
    own = call(
        state_kernel,
        "state",
        shape((supers, SENT, 2 * DV), bf16),
        place,
        near(data),
        conv_weight,
        scalars=1,
        scratch=taps,
    )
    done, saved, parts, edges, sent = call(
        main_kernel,
        "main",
        (
            shape((H, DV, TOK), bf16),
            shape((chunks, 3 * F + DV, width), f32),
            shape((chunks, FEAT, 2 * DV), bf16),
            shape((2 * F + DV, 2 * DV), f32),
            pltpu.VMEM((supers, SENT, 2 * DV), bf16),
        ),
        place,
        near(data),
        swap(own, SUPER),
        conv_weight,
        scalars=1,
        far=True,
        scratch=taps,
    )
    back = call(
        back_kernel,
        "back",
        shape((H, FIRST + 2 * DV, TOK), bf16),
        place,
        swap(sent, SUPER),
        done,
        saved,
        parts,
        edges,
        conv_weight,
        data,
        scalars=1,
        lazy=1,
        scratch=taps + window(DV),
    )
    back = swap(back, GROUP)
    partial, own_grad = call(
        weight_kernel,
        "weight",
        (
            shape((others, model // H // others, 2 * H * F), bf16),
            shape((2 * H * F, TOK), bf16),
        ),
        place,
        back,
        data,
        scalars=1,
        lazy=1,
        scratch=window(HID),
    )
    deep = model // H // others
    some = swap(partial, OTHER)
    summed = call(
        sum_kernel, "sum_a", shape((lax.axis_size("z"), deep, 2 * H * F), bf16), some
    )
    summed = call(
        sum_kernel, "sum_b", shape((H // 2 * others, deep, 2 * H * F), bf16), swap(summed, "z")
    )
    mine = lax.all_to_all(summed, ("h",) + OTHER, 0, 0, tiled=True)
    mine = mine.reshape(H // 2, model // H, 2 * H * F)
    output, grad_gate, grad_values = call(
        unpack_kernel,
        "unpack",
        (shape((TOK, H * DV), bf16),) * 3,
        back,
        gate_in[0],
        cotangent[0],
        far=True,
    )
    grad_hidden = call(
        hidden_kernel,
        "hidden",
        shape((TOK, model), bf16),
        near(own_grad),
        qk_weight,
        far=True,
    )
    mine, output, grad_hidden = lax.optimization_barrier((mine, output, grad_hidden))
    theirs = lax.ppermute(mine, "core", [(0, 1), (1, 0)])
    grad_qk_weight = call(
        join_kernel,
        "join",
        shape((H, model // H, 2 * H * F), bf16),
        place,
        near(mine),
        near(theirs),
        scalars=1,
        lazy=2,
        far=True,
        results=pl.ANY,
        scratch=(pltpu.SemaphoreType.DMA((H,)),),
    ).reshape(model, 2 * H * F)
    return output[None], grad_hidden[None], grad_values[None], grad_gate[None], grad_qk_weight


def solution(mesh):
    pairs, blocks = mesh.devices.shape
    y = 4 if blocks // H % 4 == 0 else 1
    fine = Mesh(
        mesh.devices.reshape(pairs, y, blocks // H // y, H // 2, 2),
        ("dp", "y", "z", "h", "core"),
    )
    split = P("dp", SUPER + GROUP, None)
    return jax.shard_map(
        body,
        mesh=fine,
        in_specs=(split, P(), P(), split, split, split),
        out_specs=(split, split, split, split, P()),
        check_vma=False,
    )
```

```python
import functools
import math

import jax
import jax.numpy as jnp
from jax import lax
from jax.experimental import pallas as pl
from jax.experimental.pallas import tpu as pltpu
from jax.sharding import Mesh, PartitionSpec as P

H = 8
F = 16
DV = 64
KCONV = 3
SUPER = ("y", "z")
OTHER = ("dp", "y")
GROUP = ("h", "core")
TOK = 128
HID = 256
AT_V, AT_G, AT_P = HID, HID + DV, HID + 2 * DV
ROWS = AT_P + 2 * F
FEAT = 160
SENT = FEAT // 2 + 16
WIDE = 2
FIRST = 2 * F * H
SPARE = 32
f32 = jnp.float32
bf16 = jnp.bfloat16
NN = ((1,), (0,))
NT = ((1,), (1,))
TN = ((0,), (0,))


def mm(a, b, dims):
    return lax.dot_general(a, b, (dims, ((), ())), preferred_element_type=f32)


def halves(x):
    high = x.astype(bf16)
    return high, (x - high.astype(f32)).astype(bf16)


def feature_scale(d):
    return F**-0.5 * (math.sqrt(0.5) if d == 0 else 1.0)


def up(x, d):
    return x if d == 0 else jnp.concatenate([x[d:], x[:d]], 0)


def features(x):
    rows = [x * F**-0.25]
    for d in range(F // 2):
        rows.append(x * up(x, d) * feature_scale(d))
    half = F // 2
    rows.append(x[:half] * x[half:] * feature_scale(half))
    row = lax.broadcasted_iota(jnp.int32, (8, x.shape[1]), 0)
    rows.append(jnp.where(row == 0, 1.0, 0.0))
    return jnp.concatenate(rows, 0)


def features_back(x, grads):
    total = grads[:F] * F**-0.25
    half = F // 2
    for d in range(half):
        part = grads[F * (d + 1) : F * (d + 2)] * feature_scale(d)
        total = total + part * up(x, d) + up(part * x, (F - d) % F)
    part = grads[F * (half + 1) : F * (half + 1) + half] * feature_scale(half)
    return total + jnp.concatenate([part * x[half:], part * x[:half]], 0)


def pack_state(state, extra):
    half = FEAT // 2
    lane = lax.broadcasted_iota(jnp.int32, (half, 2 * DV), 1)
    main = jnp.where(lane < DV, state[:half], pltpu.roll(state[half:], DV, 1))
    high, low = halves(state)
    high, low = high.astype(f32), low.astype(f32)
    small = lane[:16]
    sums = jnp.zeros((16, 2 * DV), f32)
    for i in range(FEAT // 16):
        sums = jnp.where(small == i, high[16 * i : 16 * i + 16, DV : DV + 1], sums)
        sums = jnp.where(small == i + 16, low[16 * i : 16 * i + 16, DV : DV + 1], sums)
    for i, column in enumerate(extra):
        sums = jnp.where(small == SPARE + i, column.astype(f32), sums)
    return jnp.concatenate([main, sums], 0).astype(bf16)


def unpack_state(total):
    half = FEAT // 2
    main = total[:half]
    main = jnp.concatenate([main, pltpu.roll(main, DV, 1)], 0)
    sums = total[half:]
    sums = sums + pltpu.roll(sums, 2 * DV - 16, 1)
    column = jnp.concatenate([sums[:, i : i + 1] for i in range(FEAT // 16)], 0)
    lane = lax.broadcasted_iota(jnp.int32, (FEAT, 2 * DV), 1)
    return jnp.where(lane < DV, main, jnp.where(lane == DV, column, 0.0))


def repeat_into(out, value):
    for i in range(out.shape[0]):
        out[i] = value


def wide_values(values):
    row = lax.broadcasted_iota(jnp.int32, (DV, values.shape[1]), 0)
    return jnp.concatenate([values, jnp.where(row == 0, 1.0, 0.0).astype(bf16)], 0)


def rows_of(ref, chunk, start, size):
    return jnp.concatenate(
        [ref[WIDE * chunk + i, start : start + size] for i in range(WIDE)], 1
    )


def head_taps(conv, columns, head):
    padded = jnp.concatenate([conv[...], jnp.zeros((8 - KCONV, 2 * H * F), f32)], 0)
    columns[...] = padded.T
    at = pl.multiple_of(F * head, F)
    return jnp.concatenate([columns[pl.ds(at, F)], columns[pl.ds(H * F + at, F)]], 0)


def convolve(now, before, taps):
    return (
        taps[:, 0:1] * now
        + taps[:, 1:2] * jnp.concatenate([before[:, 1:2], now[:, :-1]], 1)
        + taps[:, 2:3] * jnp.concatenate([before, now[:, :-2]], 1)
    )


def first_tokens(states, taps):
    rows, lanes = F, 2 * DV
    lane = lax.broadcasted_iota(jnp.int32, (rows, lanes), 1)
    raw, vals = jnp.zeros((rows, lanes), f32), jnp.zeros((rows, lanes), f32)
    for b in range(states.shape[0]):
        tile = states[b, FEAT // 2 : SENT].astype(f32)
        here = (lane >= 8 * b) & (lane < 8 * (b + 1))
        raw = jnp.where(here, pltpu.roll(tile, (8 * b - SPARE) % lanes, 1), raw)
        vals = jnp.where(here, pltpu.roll(tile, (8 * b - SPARE - 8) % lanes, 1), vals)
    prev = jnp.where(lane < 8, 0.0, pltpu.roll(raw, 8, 1))
    one = jnp.where(
        lane % 4 == 0, pltpu.roll(prev, lanes - 3, 1), pltpu.roll(raw, 1, 1)
    )
    two = pltpu.roll(prev, lanes - 2, 1)
    q, k = (
        t[:, 0:1] * raw + t[:, 1:2] * one + t[:, 2:3] * two for t in (taps[:F], taps[F:])
    )
    v = jnp.concatenate(
        [vals if j == 0 else pltpu.roll(vals, lanes - 2 * j, 1) for j in range(DV // F)], 0
    )
    return q, k, v


def sum_kernel(data, out):
    total = data[0].astype(f32)
    for i in range(1, data.shape[0]):
        total = total + data[i].astype(f32)
    repeat_into(out, total.astype(bf16))


def fetch(sources, targets, sems):
    copies = [
        pltpu.make_async_copy(source, target, sems.at[i])
        for i, (source, target) in enumerate(zip(sources, targets))
    ]
    for copy in copies:
        copy.start()
    return copies


def pack_kernel(*refs):
    out, gate, cot, values, weight, tokens, sems = refs[5:]
    far_tokens, far_weight, far_values, far_gate, far_cot = refs[:5]
    copies = fetch(
        (far_gate, far_cot, far_values, far_weight, far_tokens),
        (gate, cot, values, weight, tokens),
        sems,
    )
    for copy in copies[:3]:
        copy.wait()
    g = gate[...].astype(f32)
    v = values[...].T
    up = (cot[...].astype(f32) * (g * jax.nn.sigmoid(g))).astype(bf16).T
    for h in range(H):
        cols = slice(DV * h, DV * (h + 1))
        out[h, AT_V : AT_V + DV] = v[cols]
        out[h, AT_G : AT_G + DV] = up[cols]
    for copy in copies[3:]:
        copy.wait()
    x = tokens[...]
    projected = mm(x, weight[...], NN).T.astype(bf16)
    width = H * F
    for h in range(H):
        out[h, AT_P : AT_P + F] = projected[F * h : F * (h + 1)]
        out[h, AT_P + F : ROWS] = projected[width + F * h : width + F * (h + 1)]
        for i in range(x.shape[1] // H // TOK):
            start = x.shape[1] // H * h + TOK * i
            out[h, TOK * i : TOK * (i + 1)] = x[:, start : start + TOK]


def state_kernel(place, data, conv, out, columns):
    taps = head_taps(conv, columns, place[1])[F:]
    total = jnp.zeros((FEAT, 2 * DV), f32)
    before = jnp.zeros((F, 2), f32)
    for c in range(H // WIDE):
        raw = rows_of(data, c, AT_P + F, F).astype(f32)
        feat = features(convolve(raw, before, taps))
        if c == 0:
            token = lax.broadcasted_iota(jnp.int32, feat.shape, 1)
            feat = jnp.where(token < KCONV - 1, 0.0, feat)
        before = raw[:, -2:]
        high, low = halves(feat)
        v = wide_values(rows_of(data, c, AT_V, DV))
        total = total + (mm(high, v, NT) + mm(low, v, NT))
    first, last = data[0, AT_P:ROWS], data[H - 1, AT_P:ROWS]
    begin = data[0, AT_V : AT_V + DV]
    extra = []
    for start in (F, 0):
        rows = slice(start, start + F)
        extra += [first[rows, 0:1], first[rows, 1:2]]
        extra += [last[rows, TOK - 2 : TOK - 1], last[rows, TOK - 1 : TOK]]
    for j in range(DV // F):
        rows = slice(F * j, F * (j + 1))
        extra += [begin[rows, 0:1], begin[rows, 1:2]]
    repeat_into(out, pack_state(total, extra))


def main_kernel(
    place, data, states, conv, far_out, far_saved, far_parts, far_edges, sent,
    columns, out, saved, parts, edges, sems,
):
    here = place[0]
    copies = []
    taps = head_taps(conv, columns, place[1])
    length = TOK * WIDE
    total = jnp.zeros((SENT, 2 * DV), f32)
    for b in range(states.shape[0]):
        total = total + states[b].astype(f32) * (b < here).astype(f32)
    first_q, first_k, first_v = first_tokens(states, taps)
    lane = lax.broadcasted_iota(jnp.int32, (FEAT, 2 * DV), 1)
    earlier = (lane % 8 < KCONV - 1) & (lane < 8 * here)
    feat = halves(jnp.where(earlier, features(first_k), 0.0))
    first_values = wide_values(first_v.astype(bf16))
    state = (
        unpack_state(total) + mm(feat[0], first_values, NT) + mm(feat[1], first_values, NT)
    )
    shift = 2 * DV * 2 - 8 * (here + 1)
    edges[0:F] = pltpu.roll(first_q, shift - 4, 1)
    edges[F : 2 * F] = pltpu.roll(first_k, shift, 1)
    edges[2 * F :] = pltpu.roll(first_v, shift, 1)
    copies += fetch((edges,), (far_edges,), sems.at[pl.ds(0, 1)])
    tile = states[jnp.maximum(here - 1, 0), FEAT // 2 : SENT].astype(f32)
    tile = tile * (here > 0).astype(f32)
    before = jnp.concatenate(
        [tile[:, SPARE + 6 : SPARE + 8], tile[:, SPARE + 2 : SPARE + 4]], 0
    )
    k_at = lax.broadcasted_iota(jnp.int32, (length, length), 0)
    q_at = lax.broadcasted_iota(jnp.int32, (length, length), 1)
    causal = k_at <= q_at
    whole = jnp.zeros((FEAT, 2 * DV), f32)
    for c in range(H // WIDE):
        raw = rows_of(data, c, AT_P, 2 * F).astype(f32)
        mixed = convolve(raw, before, taps)
        before = raw[:, -2:]
        q, k = mixed[:F], mixed[F:]
        (qh, ql), (kh, kl) = halves(q * F**-0.5), halves(k)
        saved[c, 2 * F : 3 * F] = k
        v = wide_values(rows_of(data, c, AT_V, DV))
        g_att = rows_of(data, c, AT_G, DV).astype(f32)
        near_one = 1.0 + mm(
            jnp.concatenate([kh, kh, kl], 0), jnp.concatenate([qh, ql, qh], 0), TN
        )
        weights = jnp.where(causal, 0.5 + 0.5 * near_one * near_one, 0.0).astype(bf16)
        q_feat, k_feat = features(q).astype(bf16), features(k).astype(bf16)
        held = state.astype(bf16)
        numer = mm(v, weights, NN) + mm(held, q_feat, TN)
        inverse = 1.0 / numer[DV : DV + 1]
        attended = numer[:DV] * inverse
        result = attended.astype(bf16)
        g_num = g_att * inverse
        g_den = -jnp.sum(g_att * attended, 0, keepdims=True) * inverse
        row = lax.broadcasted_iota(jnp.int32, (DV, length), 0)
        wide = jnp.concatenate([g_num, jnp.where(row == 0, g_den, 0.0)], 0)
        grads = halves(wide)
        g_weights = mm(v, grads[0], TN) + mm(v, grads[1], TN)
        g_scores = jnp.where(causal, g_weights * near_one, 0.0).astype(bf16)
        g_local = (mm(kh, g_scores, NN) + mm(kl, g_scores, NN)) * F**-0.5
        g_query = g_local + features_back(q, mm(held, grads[0], NN))
        if c == 0:
            extra = [g_query[:, 0:1], g_query[:, 1:2]]
            for j in range(DV // F + 1):
                column = wide[F * j : F * (j + 1), 0:1]
                high = column.astype(bf16)
                extra += [high, column - high.astype(f32)]
        g_key = mm(qh, g_scores, NT) + mm(ql, g_scores, NT)
        g_value = mm(grads[0][:DV], weights, NT) + mm(grads[1][:DV], weights, NT)
        part = mm(q_feat, grads[0], NT)
        whole = whole + part
        parts[c] = part.astype(bf16)
        state = state + mm(k_feat, v, NT)
        for i in range(WIDE):
            cols = slice(TOK * i, TOK * (i + 1))
            out[WIDE * c + i] = result[:, cols]
        saved[c, 0:F] = g_query
        saved[c, F : 2 * F] = g_key
        saved[c, 3 * F :] = g_value
        some = slice(WIDE * c, WIDE * (c + 1))
        copies += fetch(
            (out.at[some], saved.at[c], parts.at[c]),
            (far_out.at[some], far_saved.at[c], far_parts.at[c]),
            sems.at[pl.ds(1 + 3 * c, 3)],
        )
    repeat_into(sent, pack_state(whole, extra))
    for copy in copies:
        copy.wait()


def back_kernel(
    place, states, conv, far_done, far_saved, far_parts, far_edges, far, out,
    columns, edges, data, done, saved, parts, sems,
):
    copies = fetch(
        (far_edges, far.at[:, AT_V : AT_V + DV], far_saved, far_parts, far_done),
        (edges, data, saved, parts, done),
        sems,
    )
    here = place[0]
    taps = head_taps(conv, columns, place[1])
    count = states.shape[0]
    total = jnp.zeros((SENT, 2 * DV), f32)
    for b in range(count):
        total = total + states[b].astype(f32) * (b > here).astype(f32)
    state = unpack_state(total)
    tile = states[jnp.minimum(here + 1, count - 1), FEAT // 2 : SENT].astype(f32)
    copies[0].wait()
    edge = edges[...]
    edge_v = wide_values(edge[2 * F :].astype(bf16))
    split_state = halves(state)
    column = jnp.concatenate(
        [
            tile[:, SPARE + 2 + 2 * j : SPARE + 3 + 2 * j]
            + tile[:, SPARE + 3 + 2 * j : SPARE + 4 + 2 * j]
            for j in range(DV // F + 1)
        ],
        0,
    )
    pair = jnp.sum(column * edge_v[: DV + F].astype(f32), 0, keepdims=True)
    lane = lax.broadcasted_iota(jnp.int32, (FEAT, 2 * DV), 1)
    g_feat = mm(split_state[0], edge_v, NN) + mm(split_state[1], edge_v, NN)
    g_feat = g_feat - jnp.where(lane == 1, features(edge[:F])[:, 0:1] * pair, 0.0)
    after = jnp.concatenate(
        [tile[:, SPARE : SPARE + 2], features_back(edge[F : 2 * F], g_feat)[:, 0:2]], 0
    ) * (here + 1 < count).astype(f32)
    for copy in copies[1:]:
        copy.wait()
    for c in reversed(range(H // WIDE)):
        k = saved[c, 2 * F : 3 * F]
        v = wide_values(rows_of(data, c, 0, DV))
        k_feat = features(k).astype(bf16)
        held = state.astype(bf16)
        g_key = saved[c, F : 2 * F] + features_back(k, mm(held, v, NN))
        g_value = (saved[c, 3 * F :] + mm(held, k_feat, TN)[:DV]).astype(bf16)
        state = state + parts[c].astype(f32)
        now = jnp.concatenate([saved[c, 0:F], g_key], 0)
        total = (
            taps[:, 0:1] * now
            + taps[:, 1:2] * jnp.concatenate([now[:, 1:], after[:, 0:1]], 1)
            + taps[:, 2:3] * jnp.concatenate([now[:, 2:], after], 1)
        ).astype(bf16)
        after = now[:, 0:2]
        for i in range(WIDE):
            cols = slice(TOK * i, TOK * (i + 1))
            b = WIDE * c + i
            out[b, FIRST : FIRST + DV] = done[b]
            out[b, FIRST + DV : FIRST + 2 * DV] = g_value[:, cols]
            for dest in range(H):
                out[dest, 2 * F * b : 2 * F * (b + 1)] = total[:, cols]

def stacked(grads, block):
    return jnp.concatenate(
        [
            grads[h, pl.ds(2 * F * block + at, F)]
            for at in (0, F)
            for h in range(H)
        ],
        0,
    )


def weight_kernel(place, grads, far, out, own, data, sem):
    copy = pltpu.make_async_copy(far.at[:, 0:HID], data, sem)
    copy.start()
    own[...] = stacked(grads, place[1])
    total = jnp.concatenate([stacked(grads, b) for b in range(H)], 1).T
    count, rows = out.shape[:2]
    parts = count * rows // TOK
    copy.wait()
    for i in range(parts):
        at = TOK * i
        tokens = jnp.concatenate([data[b, at : at + TOK] for b in range(H)], 0)
        result = mm(tokens, total, TN).astype(bf16)
        for j in range(count // parts):
            out[i * (count // parts) + j] = result[rows * j : rows * (j + 1)]


def join_kernel(place, part, *refs, flip):
    out, sems = refs[-2:]
    at = (place[1] + flip) % 2
    copies = fetch(
        [part.at[h] for h in range(H // 2)],
        [out.at[2 * h + at] for h in range(H // 2)],
        sems,
    )
    for copy in copies:
        copy.wait()


def hidden_kernel(own, weight, out):
    out[...] = mm(own[...].T, weight[...], NT).astype(bf16)


def unpack_kernel(data, gate, cot, output, g_gate, g_value):
    attended, values = (
        jnp.concatenate([data[h, at : at + DV] for h in range(H)], 0).T
        for at in (FIRST, FIRST + DV)
    )
    g = gate[...].astype(f32)
    sig = jax.nn.sigmoid(g)
    attended = attended.astype(f32)
    output[...] = (attended * (g * sig)).astype(bf16)
    g_gate[...] = (
        cot[...].astype(f32) * attended * sig * (1.0 + g * (1.0 - sig))
    ).astype(bf16)
    g_value[...] = values


def near(x):
    return pltpu.with_memory_space_constraint(x, pltpu.VMEM)


def call(kernel, name, out_shape, *args, scalars=0, lazy=0, far=False, results=pltpu.VMEM, scratch=(), alias={}):
    whole = pl.BlockSpec(memory_space=pltpu.VMEM)
    specs = [pl.BlockSpec(memory_space=pltpu.SMEM)] * scalars
    specs += [whole] * (len(args) - scalars - lazy)
    specs += [pl.BlockSpec(memory_space=pl.ANY)] * lazy
    if isinstance(results, tuple):
        outs = tuple(pl.BlockSpec(memory_space=r) for r in results)
    else:
        outs = jax.tree.map(lambda s: pl.BlockSpec(memory_space=results), out_shape)
    if not far:
        out_shape = jax.tree.map(lambda s: pltpu.VMEM(s.shape, s.dtype), out_shape)
    return pl.pallas_call(
        kernel,
        name=name,
        out_shape=out_shape,
        in_specs=specs,
        out_specs=outs,
        scratch_shapes=scratch,
        input_output_aliases=alias,
    )(*args)


def window(size):
    return pltpu.VMEM((H, size, TOK), bf16), pltpu.SemaphoreType.DMA(())


def shape(dims, kind):
    return jax.ShapeDtypeStruct(dims, kind)


def swap(x, axis):
    return near(lax.all_to_all(x, axis, 0, 0, tiled=True))


def body(hidden_in, qk_weight, conv_weight, values, gate_in, cotangent):
    tokens = hidden_in[0]
    supers = lax.axis_size(SUPER)
    others = lax.axis_size(OTHER)
    model = tokens.shape[1]
    chunks, width = H // WIDE, TOK * WIDE
    place = jnp.stack([lax.axis_index(SUPER), lax.axis_index(GROUP)]).astype(jnp.int32)
    taps = (pltpu.VMEM((2 * H * F, 8), f32),)
    packed = call(
        pack_kernel,
        "pack",
        shape((H, ROWS, TOK), bf16),
        tokens,
        qk_weight,
        values[0],
        gate_in[0],
        cotangent[0],
        lazy=5,
        scratch=(
            *(pltpu.VMEM((TOK, H * DV), bf16),) * 3,
            pltpu.VMEM(qk_weight.shape, bf16),
            pltpu.VMEM(tokens.shape, bf16),
            pltpu.SemaphoreType.DMA((5,)),
        ),
    )
    data = lax.all_to_all(packed, GROUP, 0, 0, tiled=True)
    own = call(
        state_kernel,
        "state",
        shape((supers, SENT, 2 * DV), bf16),
        place,
        near(data),
        conv_weight,
        scalars=1,
        scratch=taps,
    )
    done, saved, parts, edges, sent = call(
        main_kernel,
        "main",
        (
            shape((H, DV, TOK), bf16),
            shape((chunks, 3 * F + DV, width), f32),
            shape((chunks, FEAT, 2 * DV), bf16),
            shape((2 * F + DV, 2 * DV), f32),
            pltpu.VMEM((supers, SENT, 2 * DV), bf16),
        ),
        place,
        near(data),
        swap(own, SUPER),
        conv_weight,
        scalars=1,
        far=True,
        results=(pl.ANY,) * 4 + (pltpu.VMEM,),
        scratch=taps
        + (
            pltpu.VMEM((H, DV, TOK), bf16),
            pltpu.VMEM((chunks, 3 * F + DV, width), f32),
            pltpu.VMEM((chunks, FEAT, 2 * DV), bf16),
            pltpu.VMEM((2 * F + DV, 2 * DV), f32),
            pltpu.SemaphoreType.DMA((1 + 3 * chunks,)),
        ),
    )
    back = call(
        back_kernel,
        "back",
        shape((H, FIRST + 2 * DV, TOK), bf16),
        place,
        swap(sent, SUPER),
        conv_weight,
        done,
        saved,
        parts,
        edges,
        data,
        scalars=1,
        lazy=5,
        scratch=taps
        + (
            pltpu.VMEM((2 * F + DV, 2 * DV), f32),
            pltpu.VMEM((H, DV, TOK), bf16),
            pltpu.VMEM((H, DV, TOK), bf16),
            pltpu.VMEM((chunks, 3 * F + DV, width), f32),
            pltpu.VMEM((chunks, FEAT, 2 * DV), bf16),
            pltpu.SemaphoreType.DMA((5,)),
        ),
    )
    back = swap(back, GROUP)
    partial, own_grad = call(
        weight_kernel,
        "weight",
        (
            shape((others, model // H // others, 2 * H * F), bf16),
            shape((2 * H * F, TOK), bf16),
        ),
        place,
        back,
        data,
        scalars=1,
        lazy=1,
        scratch=window(HID),
    )
    deep = model // H // others
    some = swap(partial, OTHER)
    summed = call(
        sum_kernel, "sum_a", shape((lax.axis_size("z"), deep, 2 * H * F), bf16), some
    )
    summed = call(
        sum_kernel, "sum_b", shape((H // 2 * others, deep, 2 * H * F), bf16), swap(summed, "z")
    )
    mine = lax.all_to_all(summed, ("h",) + OTHER, 0, 0, tiled=True)
    mine = mine.reshape(H // 2, model // H, 2 * H * F)
    output, grad_gate, grad_values = call(
        unpack_kernel,
        "unpack",
        (shape((TOK, H * DV), bf16),) * 3,
        back,
        gate_in[0],
        cotangent[0],
        far=True,
    )
    grad_hidden = call(
        hidden_kernel,
        "hidden",
        shape((TOK, model), bf16),
        near(own_grad),
        qk_weight,
        far=True,
    )
    mine, output, grad_hidden = lax.optimization_barrier((mine, output, grad_hidden))
    theirs = lax.ppermute(mine, "core", [(0, 1), (1, 0)])
    joined = ()
    for flip, part in enumerate((mine, theirs)):
        joined = (
            call(
                functools.partial(join_kernel, flip=flip),
                f"join_{flip}",
                shape((H, model // H, 2 * H * F), bf16),
                place,
                near(part),
                *joined,
                scalars=1,
                lazy=1 + flip,
                far=True,
                results=pl.ANY,
                scratch=(pltpu.SemaphoreType.DMA((H // 2,)),),
                alias={2: 0} if flip else {},
            ),
        )
    grad_qk_weight = joined[0].reshape(model, 2 * H * F)
    return output[None], grad_hidden[None], grad_values[None], grad_gate[None], grad_qk_weight


def solution(mesh):
    pairs, blocks = mesh.devices.shape
    y = 4 if blocks // H % 4 == 0 else 1
    fine = Mesh(
        mesh.devices.reshape(pairs, y, blocks // H // y, H // 2, 2),
        ("dp", "y", "z", "h", "core"),
    )
    split = P("dp", SUPER + GROUP, None)
    return jax.shard_map(
        body,
        mesh=fine,
        in_specs=(split, P(), P(), split, split, split),
        out_specs=(split, split, split, split, P()),
        check_vma=False,
    )
```

```python
import functools
import math

import jax
import jax.numpy as jnp
from jax import lax
from jax.experimental import pallas as pl
from jax.experimental.pallas import tpu as pltpu
from jax.sharding import Mesh, PartitionSpec as P

H = 8
F = 16
DV = 64
KCONV = 3
SUPER = ("y", "z")
OTHER = ("dp", "y")
GROUP = ("h", "core")
TOK = 128
HID = 256
AT_V, AT_G, AT_P = HID, HID + DV, HID + 2 * DV
ROWS = AT_P + 2 * F
FEAT = 160
SENT = FEAT // 2 + 16
WIDE = 2
FIRST = 2 * F * H
SPARE = 32
f32 = jnp.float32
bf16 = jnp.bfloat16
NN = ((1,), (0,))
NT = ((1,), (1,))
TN = ((0,), (0,))


def mm(a, b, dims):
    return lax.dot_general(a, b, (dims, ((), ())), preferred_element_type=f32)


def halves(x):
    high = x.astype(bf16)
    return high, (x - high.astype(f32)).astype(bf16)


def feature_scale(d):
    return F**-0.5 * (math.sqrt(0.5) if d == 0 else 1.0)


def up(x, d):
    return x if d == 0 else jnp.concatenate([x[d:], x[:d]], 0)


def features(x):
    rows = [x * F**-0.25]
    for d in range(F // 2):
        rows.append(x * up(x, d) * feature_scale(d))
    half = F // 2
    rows.append(x[:half] * x[half:] * feature_scale(half))
    row = lax.broadcasted_iota(jnp.int32, (8, x.shape[1]), 0)
    rows.append(jnp.where(row == 0, 1.0, 0.0))
    return jnp.concatenate(rows, 0)


def features_back(x, grads):
    total = grads[:F] * F**-0.25
    half = F // 2
    for d in range(half):
        part = grads[F * (d + 1) : F * (d + 2)] * feature_scale(d)
        total = total + part * up(x, d) + up(part * x, (F - d) % F)
    part = grads[F * (half + 1) : F * (half + 1) + half] * feature_scale(half)
    return total + jnp.concatenate([part * x[half:], part * x[:half]], 0)


def pack_state(state, extra):
    half = FEAT // 2
    lane = lax.broadcasted_iota(jnp.int32, (half, 2 * DV), 1)
    main = jnp.where(lane < DV, state[:half], pltpu.roll(state[half:], DV, 1))
    high, low = halves(state)
    high, low = high.astype(f32), low.astype(f32)
    small = lane[:16]
    sums = jnp.zeros((16, 2 * DV), f32)
    for i in range(FEAT // 16):
        sums = jnp.where(small == i, high[16 * i : 16 * i + 16, DV : DV + 1], sums)
        sums = jnp.where(small == i + 16, low[16 * i : 16 * i + 16, DV : DV + 1], sums)
    for i, column in enumerate(extra):
        sums = jnp.where(small == SPARE + i, column.astype(f32), sums)
    return jnp.concatenate([main, sums], 0).astype(bf16)


def unpack_state(total):
    half = FEAT // 2
    main = total[:half]
    main = jnp.concatenate([main, pltpu.roll(main, DV, 1)], 0)
    sums = total[half:]
    sums = sums + pltpu.roll(sums, 2 * DV - 16, 1)
    column = jnp.concatenate([sums[:, i : i + 1] for i in range(FEAT // 16)], 0)
    lane = lax.broadcasted_iota(jnp.int32, (FEAT, 2 * DV), 1)
    return jnp.where(lane < DV, main, jnp.where(lane == DV, column, 0.0))


def repeat_into(out, value):
    for i in range(out.shape[0]):
        out[i] = value


def wide_values(values):
    row = lax.broadcasted_iota(jnp.int32, (DV, values.shape[1]), 0)
    return jnp.concatenate([values, jnp.where(row == 0, 1.0, 0.0).astype(bf16)], 0)


def rows_of(ref, chunk, start, size):
    return jnp.concatenate(
        [ref[WIDE * chunk + i, start : start + size] for i in range(WIDE)], 1
    )


def head_taps(conv, columns, head):
    padded = jnp.concatenate([conv[...], jnp.zeros((8 - KCONV, 2 * H * F), f32)], 0)
    columns[...] = padded.T
    at = pl.multiple_of(F * head, F)
    return jnp.concatenate([columns[pl.ds(at, F)], columns[pl.ds(H * F + at, F)]], 0)


def convolve(now, before, taps):
    return (
        taps[:, 0:1] * now
        + taps[:, 1:2] * jnp.concatenate([before[:, 1:2], now[:, :-1]], 1)
        + taps[:, 2:3] * jnp.concatenate([before, now[:, :-2]], 1)
    )


def first_tokens(states, taps):
    rows, lanes = F, 2 * DV
    lane = lax.broadcasted_iota(jnp.int32, (rows, lanes), 1)
    raw, vals = jnp.zeros((rows, lanes), f32), jnp.zeros((rows, lanes), f32)
    for b in range(states.shape[0]):
        tile = states[b, FEAT // 2 : SENT].astype(f32)
        here = (lane >= 8 * b) & (lane < 8 * (b + 1))
        raw = jnp.where(here, pltpu.roll(tile, (8 * b - SPARE) % lanes, 1), raw)
        vals = jnp.where(here, pltpu.roll(tile, (8 * b - SPARE - 8) % lanes, 1), vals)
    prev = jnp.where(lane < 8, 0.0, pltpu.roll(raw, 8, 1))
    one = jnp.where(
        lane % 4 == 0, pltpu.roll(prev, lanes - 3, 1), pltpu.roll(raw, 1, 1)
    )
    two = pltpu.roll(prev, lanes - 2, 1)
    q, k = (
        t[:, 0:1] * raw + t[:, 1:2] * one + t[:, 2:3] * two for t in (taps[:F], taps[F:])
    )
    v = jnp.concatenate(
        [vals if j == 0 else pltpu.roll(vals, lanes - 2 * j, 1) for j in range(DV // F)], 0
    )
    return q, k, v


def sum_kernel(data, out):
    total = data[0].astype(f32)
    for i in range(1, data.shape[0]):
        total = total + data[i].astype(f32)
    repeat_into(out, total.astype(bf16))


def fetch(sources, targets, sems):
    copies = [
        pltpu.make_async_copy(source, target, sems.at[i])
        for i, (source, target) in enumerate(zip(sources, targets))
    ]
    for copy in copies:
        copy.start()
    return copies


def pack_kernel(*refs):
    out, gate, cot, values, weight, tokens, sems = refs[5:]
    far_tokens, far_weight, far_values, far_gate, far_cot = refs[:5]
    w_rows, t_rows = (
        [pl.ds(n // 4 * i, n // 4) for i in range(4)] for n in (weight.shape[0], TOK)
    )
    copies = fetch(
        [far_gate, far_cot, far_values]
        + [far_weight.at[r] for r in w_rows]
        + [far_tokens.at[r] for r in t_rows],
        [gate, cot, values]
        + [weight.at[r] for r in w_rows]
        + [tokens.at[r] for r in t_rows],
        sems,
    )
    for copy in copies[:3]:
        copy.wait()
    g = gate[...].astype(f32)
    v = values[...].T
    up = (cot[...].astype(f32) * (g * jax.nn.sigmoid(g))).astype(bf16).T
    for h in range(H):
        cols = slice(DV * h, DV * (h + 1))
        out[h, AT_V : AT_V + DV] = v[cols]
        out[h, AT_G : AT_G + DV] = up[cols]
    for copy in copies[3:]:
        copy.wait()
    x = tokens[...]
    projected = mm(x, weight[...], NN).T.astype(bf16)
    width = H * F
    for h in range(H):
        out[h, AT_P : AT_P + F] = projected[F * h : F * (h + 1)]
        out[h, AT_P + F : ROWS] = projected[width + F * h : width + F * (h + 1)]
        for i in range(x.shape[1] // H // TOK):
            start = x.shape[1] // H * h + TOK * i
            out[h, TOK * i : TOK * (i + 1)] = x[:, start : start + TOK]


def state_kernel(place, data, conv, out, columns):
    taps = head_taps(conv, columns, place[1])[F:]
    total = jnp.zeros((FEAT, 2 * DV), f32)
    before = jnp.zeros((F, 2), f32)
    for c in range(H // WIDE):
        raw = rows_of(data, c, AT_P + F, F).astype(f32)
        feat = features(convolve(raw, before, taps))
        if c == 0:
            token = lax.broadcasted_iota(jnp.int32, feat.shape, 1)
            feat = jnp.where(token < KCONV - 1, 0.0, feat)
        before = raw[:, -2:]
        high, low = halves(feat)
        v = wide_values(rows_of(data, c, AT_V, DV))
        total = total + (mm(high, v, NT) + mm(low, v, NT))
    first, last = data[0, AT_P:ROWS], data[H - 1, AT_P:ROWS]
    begin = data[0, AT_V : AT_V + DV]
    extra = []
    for start in (F, 0):
        rows = slice(start, start + F)
        extra += [first[rows, 0:1], first[rows, 1:2]]
        extra += [last[rows, TOK - 2 : TOK - 1], last[rows, TOK - 1 : TOK]]
    for j in range(DV // F):
        rows = slice(F * j, F * (j + 1))
        extra += [begin[rows, 0:1], begin[rows, 1:2]]
    repeat_into(out, pack_state(total, extra))


def main_kernel(
    place, data, states, conv, far_out, far_saved, far_parts, far_edges, sent,
    columns, out, saved, parts, edges, sems,
):
    here = place[0]
    copies = []
    taps = head_taps(conv, columns, place[1])
    length = TOK * WIDE
    total = jnp.zeros((SENT, 2 * DV), f32)
    for b in range(states.shape[0]):
        total = total + states[b].astype(f32) * (b < here).astype(f32)
    first_q, first_k, first_v = first_tokens(states, taps)
    lane = lax.broadcasted_iota(jnp.int32, (FEAT, 2 * DV), 1)
    earlier = (lane % 8 < KCONV - 1) & (lane < 8 * here)
    feat = halves(jnp.where(earlier, features(first_k), 0.0))
    first_values = wide_values(first_v.astype(bf16))
    state = (
        unpack_state(total) + mm(feat[0], first_values, NT) + mm(feat[1], first_values, NT)
    )
    shift = 2 * DV * 2 - 8 * (here + 1)
    edges[0:F] = pltpu.roll(first_q, shift - 4, 1)
    edges[F : 2 * F] = pltpu.roll(first_k, shift, 1)
    edges[2 * F :] = pltpu.roll(first_v, shift, 1)
    copies += fetch((edges,), (far_edges,), sems.at[pl.ds(0, 1)])
    tile = states[jnp.maximum(here - 1, 0), FEAT // 2 : SENT].astype(f32)
    tile = tile * (here > 0).astype(f32)
    before = jnp.concatenate(
        [tile[:, SPARE + 6 : SPARE + 8], tile[:, SPARE + 2 : SPARE + 4]], 0
    )
    k_at = lax.broadcasted_iota(jnp.int32, (length, length), 0)
    q_at = lax.broadcasted_iota(jnp.int32, (length, length), 1)
    causal = k_at <= q_at
    whole = jnp.zeros((FEAT, 2 * DV), f32)
    for c in range(H // WIDE):
        raw = rows_of(data, c, AT_P, 2 * F).astype(f32)
        mixed = convolve(raw, before, taps)
        before = raw[:, -2:]
        q, k = mixed[:F], mixed[F:]
        (qh, ql), (kh, kl) = halves(q * F**-0.5), halves(k)
        saved[c, 2 * F : 3 * F] = k
        v = wide_values(rows_of(data, c, AT_V, DV))
        g_att = rows_of(data, c, AT_G, DV).astype(f32)
        near_one = 1.0 + mm(
            jnp.concatenate([kh, kh, kl], 0), jnp.concatenate([qh, ql, qh], 0), TN
        )
        weights = jnp.where(causal, 0.5 + 0.5 * near_one * near_one, 0.0).astype(bf16)
        q_feat, k_feat = features(q).astype(bf16), features(k).astype(bf16)
        held = state.astype(bf16)
        numer = mm(v, weights, NN) + mm(held, q_feat, TN)
        inverse = 1.0 / numer[DV : DV + 1]
        attended = numer[:DV] * inverse
        result = attended.astype(bf16)
        g_num = g_att * inverse
        g_den = -jnp.sum(g_att * attended, 0, keepdims=True) * inverse
        row = lax.broadcasted_iota(jnp.int32, (DV, length), 0)
        wide = jnp.concatenate([g_num, jnp.where(row == 0, g_den, 0.0)], 0)
        grads = halves(wide)
        g_weights = mm(v, grads[0], TN) + mm(v, grads[1], TN)
        g_scores = jnp.where(causal, g_weights * near_one, 0.0).astype(bf16)
        g_local = (mm(kh, g_scores, NN) + mm(kl, g_scores, NN)) * F**-0.5
        g_query = g_local + features_back(q, mm(held, grads[0], NN))
        if c == 0:
            extra = [g_query[:, 0:1], g_query[:, 1:2]]
            for j in range(DV // F + 1):
                column = wide[F * j : F * (j + 1), 0:1]
                high = column.astype(bf16)
                extra += [high, column - high.astype(f32)]
        g_key = mm(qh, g_scores, NT) + mm(ql, g_scores, NT)
        g_value = mm(grads[0][:DV], weights, NT) + mm(grads[1][:DV], weights, NT)
        part = mm(q_feat, grads[0], NT)
        whole = whole + part
        parts[c] = part.astype(bf16)
        state = state + mm(k_feat, v, NT)
        for i in range(WIDE):
            cols = slice(TOK * i, TOK * (i + 1))
            out[WIDE * c + i] = result[:, cols]
        saved[c, 0:F] = g_query
        saved[c, F : 2 * F] = g_key
        saved[c, 3 * F :] = g_value
        some = slice(WIDE * c, WIDE * (c + 1))
        copies += fetch(
            (out.at[some], saved.at[c], parts.at[c]),
            (far_out.at[some], far_saved.at[c], far_parts.at[c]),
            sems.at[pl.ds(1 + 3 * c, 3)],
        )
    repeat_into(sent, pack_state(whole, extra))
    for copy in copies:
        copy.wait()


def back_kernel(
    place, states, conv, far_done, far_saved, far_parts, far_edges, far, out,
    columns, edges, data, done, saved, parts, sems,
):
    copies = fetch(
        (far_edges, far.at[:, AT_V : AT_V + DV], far_saved, far_parts, far_done),
        (edges, data, saved, parts, done),
        sems,
    )
    here = place[0]
    taps = head_taps(conv, columns, place[1])
    count = states.shape[0]
    total = jnp.zeros((SENT, 2 * DV), f32)
    for b in range(count):
        total = total + states[b].astype(f32) * (b > here).astype(f32)
    state = unpack_state(total)
    tile = states[jnp.minimum(here + 1, count - 1), FEAT // 2 : SENT].astype(f32)
    copies[0].wait()
    edge = edges[...]
    edge_v = wide_values(edge[2 * F :].astype(bf16))
    split_state = halves(state)
    column = jnp.concatenate(
        [
            tile[:, SPARE + 2 + 2 * j : SPARE + 3 + 2 * j]
            + tile[:, SPARE + 3 + 2 * j : SPARE + 4 + 2 * j]
            for j in range(DV // F + 1)
        ],
        0,
    )
    pair = jnp.sum(column * edge_v[: DV + F].astype(f32), 0, keepdims=True)
    lane = lax.broadcasted_iota(jnp.int32, (FEAT, 2 * DV), 1)
    g_feat = mm(split_state[0], edge_v, NN) + mm(split_state[1], edge_v, NN)
    g_feat = g_feat - jnp.where(lane == 1, features(edge[:F])[:, 0:1] * pair, 0.0)
    after = jnp.concatenate(
        [tile[:, SPARE : SPARE + 2], features_back(edge[F : 2 * F], g_feat)[:, 0:2]], 0
    ) * (here + 1 < count).astype(f32)
    for copy in copies[1:]:
        copy.wait()
    for c in reversed(range(H // WIDE)):
        k = saved[c, 2 * F : 3 * F]
        v = wide_values(rows_of(data, c, 0, DV))
        k_feat = features(k).astype(bf16)
        held = state.astype(bf16)
        g_key = saved[c, F : 2 * F] + features_back(k, mm(held, v, NN))
        g_value = (saved[c, 3 * F :] + mm(held, k_feat, TN)[:DV]).astype(bf16)
        state = state + parts[c].astype(f32)
        now = jnp.concatenate([saved[c, 0:F], g_key], 0)
        total = (
            taps[:, 0:1] * now
            + taps[:, 1:2] * jnp.concatenate([now[:, 1:], after[:, 0:1]], 1)
            + taps[:, 2:3] * jnp.concatenate([now[:, 2:], after], 1)
        ).astype(bf16)
        after = now[:, 0:2]
        for i in range(WIDE):
            cols = slice(TOK * i, TOK * (i + 1))
            b = WIDE * c + i
            out[b, FIRST : FIRST + DV] = done[b]
            out[b, FIRST + DV : FIRST + 2 * DV] = g_value[:, cols]
            for dest in range(H):
                out[dest, 2 * F * b : 2 * F * (b + 1)] = total[:, cols]

def stacked(grads, block):
    return jnp.concatenate(
        [
            grads[h, pl.ds(2 * F * block + at, F)]
            for at in (0, F)
            for h in range(H)
        ],
        0,
    )


def weight_kernel(place, grads, far, out, own, data, sem):
    copies = fetch(
        [far.at[b, 0:HID] for b in range(H)], [data.at[b] for b in range(H)], sem
    )
    own[...] = stacked(grads, place[1])
    total = jnp.concatenate([stacked(grads, b) for b in range(H)], 1).T
    count, rows = out.shape[:2]
    parts = count * rows // TOK
    for copy in copies:
        copy.wait()
    for i in range(parts):
        at = TOK * i
        tokens = jnp.concatenate([data[b, at : at + TOK] for b in range(H)], 0)
        result = mm(tokens, total, TN).astype(bf16)
        for j in range(count // parts):
            out[i * (count // parts) + j] = result[rows * j : rows * (j + 1)]


def join_kernel(place, part, *refs, flip):
    out, sems = refs[-2:]
    at = (place[1] + flip) % 2
    size = part.shape[1] // 4
    pieces = [(h, pl.ds(size * i, size)) for h in range(H // 2) for i in range(4)]
    copies = fetch(
        [part.at[h, r] for h, r in pieces],
        [out.at[2 * h + at, r] for h, r in pieces],
        sems,
    )
    for copy in copies:
        copy.wait()


def hidden_kernel(own, weight, out):
    out[...] = mm(own[...].T, weight[...], NT).astype(bf16)


def unpack_kernel(data, gate, cot, output, g_gate, g_value):
    attended, values = (
        jnp.concatenate([data[h, at : at + DV] for h in range(H)], 0).T
        for at in (FIRST, FIRST + DV)
    )
    g = gate[...].astype(f32)
    sig = jax.nn.sigmoid(g)
    attended = attended.astype(f32)
    output[...] = (attended * (g * sig)).astype(bf16)
    g_gate[...] = (
        cot[...].astype(f32) * attended * sig * (1.0 + g * (1.0 - sig))
    ).astype(bf16)
    g_value[...] = values


def near(x):
    return pltpu.with_memory_space_constraint(x, pltpu.VMEM)


def call(kernel, name, out_shape, *args, scalars=0, lazy=0, far=False, results=pltpu.VMEM, scratch=(), alias={}):
    whole = pl.BlockSpec(memory_space=pltpu.VMEM)
    specs = [pl.BlockSpec(memory_space=pltpu.SMEM)] * scalars
    specs += [whole] * (len(args) - scalars - lazy)
    specs += [pl.BlockSpec(memory_space=pl.ANY)] * lazy
    if isinstance(results, tuple):
        outs = tuple(pl.BlockSpec(memory_space=r) for r in results)
    else:
        outs = jax.tree.map(lambda s: pl.BlockSpec(memory_space=results), out_shape)
    if not far:
        out_shape = jax.tree.map(lambda s: pltpu.VMEM(s.shape, s.dtype), out_shape)
    return pl.pallas_call(
        kernel,
        name=name,
        out_shape=out_shape,
        in_specs=specs,
        out_specs=outs,
        scratch_shapes=scratch,
        input_output_aliases=alias,
    )(*args)


def window(size):
    return pltpu.VMEM((H, size, TOK), bf16), pltpu.SemaphoreType.DMA((H,))


def shape(dims, kind):
    return jax.ShapeDtypeStruct(dims, kind)


def swap(x, axis):
    return near(lax.all_to_all(x, axis, 0, 0, tiled=True))


def body(hidden_in, qk_weight, conv_weight, values, gate_in, cotangent):
    tokens = hidden_in[0]
    supers = lax.axis_size(SUPER)
    others = lax.axis_size(OTHER)
    model = tokens.shape[1]
    chunks, width = H // WIDE, TOK * WIDE
    place = jnp.stack([lax.axis_index(SUPER), lax.axis_index(GROUP)]).astype(jnp.int32)
    taps = (pltpu.VMEM((2 * H * F, 8), f32),)
    packed = call(
        pack_kernel,
        "pack",
        shape((H, ROWS, TOK), bf16),
        tokens,
        qk_weight,
        values[0],
        gate_in[0],
        cotangent[0],
        lazy=5,
        scratch=(
            *(pltpu.VMEM((TOK, H * DV), bf16),) * 3,
            pltpu.VMEM(qk_weight.shape, bf16),
            pltpu.VMEM(tokens.shape, bf16),
            pltpu.SemaphoreType.DMA((11,)),
        ),
    )
    data = lax.all_to_all(packed, GROUP, 0, 0, tiled=True)
    own = call(
        state_kernel,
        "state",
        shape((supers, SENT, 2 * DV), bf16),
        place,
        near(data),
        conv_weight,
        scalars=1,
        scratch=taps,
    )
    done, saved, parts, edges, sent = call(
        main_kernel,
        "main",
        (
            shape((H, DV, TOK), bf16),
            shape((chunks, 3 * F + DV, width), f32),
            shape((chunks, FEAT, 2 * DV), bf16),
            shape((2 * F + DV, 2 * DV), f32),
            pltpu.VMEM((supers, SENT, 2 * DV), bf16),
        ),
        place,
        near(data),
        swap(own, SUPER),
        conv_weight,
        scalars=1,
        far=True,
        results=(pl.ANY,) * 4 + (pltpu.VMEM,),
        scratch=taps
        + (
            pltpu.VMEM((H, DV, TOK), bf16),
            pltpu.VMEM((chunks, 3 * F + DV, width), f32),
            pltpu.VMEM((chunks, FEAT, 2 * DV), bf16),
            pltpu.VMEM((2 * F + DV, 2 * DV), f32),
            pltpu.SemaphoreType.DMA((1 + 3 * chunks,)),
        ),
    )
    back = call(
        back_kernel,
        "back",
        shape((H, FIRST + 2 * DV, TOK), bf16),
        place,
        swap(sent, SUPER),
        conv_weight,
        done,
        saved,
        parts,
        edges,
        data,
        scalars=1,
        lazy=5,
        scratch=taps
        + (
            pltpu.VMEM((2 * F + DV, 2 * DV), f32),
            pltpu.VMEM((H, DV, TOK), bf16),
            pltpu.VMEM((H, DV, TOK), bf16),
            pltpu.VMEM((chunks, 3 * F + DV, width), f32),
            pltpu.VMEM((chunks, FEAT, 2 * DV), bf16),
            pltpu.SemaphoreType.DMA((5,)),
        ),
    )
    back = swap(back, GROUP)
    partial, own_grad = call(
        weight_kernel,
        "weight",
        (
            shape((others, model // H // others, 2 * H * F), bf16),
            shape((2 * H * F, TOK), bf16),
        ),
        place,
        back,
        data,
        scalars=1,
        lazy=1,
        scratch=window(HID),
    )
    deep = model // H // others
    some = swap(partial, OTHER)
    summed = call(
        sum_kernel, "sum_a", shape((lax.axis_size("z"), deep, 2 * H * F), bf16), some
    )
    summed = call(
        sum_kernel, "sum_b", shape((H // 2 * others, deep, 2 * H * F), bf16), swap(summed, "z")
    )
    mine = lax.all_to_all(summed, ("h",) + OTHER, 0, 0, tiled=True)
    mine = mine.reshape(H // 2, model // H, 2 * H * F)
    output, grad_gate, grad_values = call(
        unpack_kernel,
        "unpack",
        (shape((TOK, H * DV), bf16),) * 3,
        back,
        gate_in[0],
        cotangent[0],
        far=True,
    )
    grad_hidden = call(
        hidden_kernel,
        "hidden",
        shape((TOK, model), bf16),
        near(own_grad),
        qk_weight,
        far=True,
    )
    mine, output, grad_hidden = lax.optimization_barrier((mine, output, grad_hidden))
    theirs = lax.ppermute(mine, "core", [(0, 1), (1, 0)])
    joined = ()
    for flip, part in enumerate((mine, theirs)):
        joined = (
            call(
                functools.partial(join_kernel, flip=flip),
                f"join_{flip}",
                shape((H, model // H, 2 * H * F), bf16),
                place,
                near(part),
                *joined,
                scalars=1,
                lazy=1 + flip,
                far=True,
                results=pl.ANY,
                scratch=(pltpu.SemaphoreType.DMA((2 * H,)),),
                alias={2: 0} if flip else {},
            ),
        )
    grad_qk_weight = joined[0].reshape(model, 2 * H * F)
    return output[None], grad_hidden[None], grad_values[None], grad_gate[None], grad_qk_weight


def solution(mesh):
    pairs, blocks = mesh.devices.shape
    y = 4 if blocks // H % 4 == 0 else 1
    fine = Mesh(
        mesh.devices.reshape(pairs, y, blocks // H // y, H // 2, 2),
        ("dp", "y", "z", "h", "core"),
    )
    split = P("dp", SUPER + GROUP, None)
    return jax.shard_map(
        body,
        mesh=fine,
        in_specs=(split, P(), P(), split, split, split),
        out_specs=(split, split, split, split, P()),
        check_vma=False,
    )
```

```python
import functools
import math

import jax
import jax.numpy as jnp
from jax import lax
from jax.experimental import pallas as pl
from jax.experimental.pallas import tpu as pltpu
from jax.sharding import Mesh, PartitionSpec as P

H = 8
F = 16
DV = 64
KCONV = 3
SUPER = ("y", "z")
OTHER = ("dp", "y")
GROUP = ("h", "core")
TOK = 128
HID = 256
AT_V, AT_G, AT_P = HID, HID + DV, HID + 2 * DV
ROWS = AT_P + 2 * F
FEAT = 160
SENT = FEAT // 2 + 16
WIDE = 2
FIRST = 2 * F * H
SPARE = 32
f32 = jnp.float32
bf16 = jnp.bfloat16
NN = ((1,), (0,))
NT = ((1,), (1,))
TN = ((0,), (0,))


def mm(a, b, dims):
    return lax.dot_general(a, b, (dims, ((), ())), preferred_element_type=f32)


def halves(x):
    high = x.astype(bf16)
    return high, (x - high.astype(f32)).astype(bf16)


def feature_scale(d):
    return F**-0.5 * (math.sqrt(0.5) if d == 0 else 1.0)


def up(x, d):
    return x if d == 0 else jnp.concatenate([x[d:], x[:d]], 0)


def features(x):
    rows = [x * F**-0.25]
    for d in range(F // 2):
        rows.append(x * up(x, d) * feature_scale(d))
    half = F // 2
    rows.append(x[:half] * x[half:] * feature_scale(half))
    row = lax.broadcasted_iota(jnp.int32, (8, x.shape[1]), 0)
    rows.append(jnp.where(row == 0, 1.0, 0.0))
    return jnp.concatenate(rows, 0)


def features_back(x, grads):
    total = grads[:F] * F**-0.25
    half = F // 2
    for d in range(half):
        part = grads[F * (d + 1) : F * (d + 2)] * feature_scale(d)
        total = total + part * up(x, d) + up(part * x, (F - d) % F)
    part = grads[F * (half + 1) : F * (half + 1) + half] * feature_scale(half)
    return total + jnp.concatenate([part * x[half:], part * x[:half]], 0)


def pack_state(state, extra):
    half = FEAT // 2
    lane = lax.broadcasted_iota(jnp.int32, (half, 2 * DV), 1)
    main = jnp.where(lane < DV, state[:half], pltpu.roll(state[half:], DV, 1))
    high, low = halves(state)
    high, low = high.astype(f32), low.astype(f32)
    small = lane[:16]
    sums = jnp.zeros((16, 2 * DV), f32)
    for i in range(FEAT // 16):
        sums = jnp.where(small == i, high[16 * i : 16 * i + 16, DV : DV + 1], sums)
        sums = jnp.where(small == i + 16, low[16 * i : 16 * i + 16, DV : DV + 1], sums)
    for i, column in enumerate(extra):
        sums = jnp.where(small == SPARE + i, column.astype(f32), sums)
    return jnp.concatenate([main, sums], 0).astype(bf16)


def unpack_state(total):
    half = FEAT // 2
    main = total[:half]
    main = jnp.concatenate([main, pltpu.roll(main, DV, 1)], 0)
    sums = total[half:]
    sums = sums + pltpu.roll(sums, 2 * DV - 16, 1)
    column = jnp.concatenate([sums[:, i : i + 1] for i in range(FEAT // 16)], 0)
    lane = lax.broadcasted_iota(jnp.int32, (FEAT, 2 * DV), 1)
    return jnp.where(lane < DV, main, jnp.where(lane == DV, column, 0.0))


def repeat_into(out, value):
    for i in range(out.shape[0]):
        out[i] = value


def wide_values(values):
    row = lax.broadcasted_iota(jnp.int32, (DV, values.shape[1]), 0)
    return jnp.concatenate([values, jnp.where(row == 0, 1.0, 0.0).astype(bf16)], 0)


def rows_of(ref, chunk, start, size):
    return jnp.concatenate(
        [ref[WIDE * chunk + i, start : start + size] for i in range(WIDE)], 1
    )


def head_taps(conv, columns, head):
    padded = jnp.concatenate([conv[...], jnp.zeros((8 - KCONV, 2 * H * F), f32)], 0)
    columns[...] = padded.T
    at = pl.multiple_of(F * head, F)
    return jnp.concatenate([columns[pl.ds(at, F)], columns[pl.ds(H * F + at, F)]], 0)


def convolve(now, before, taps):
    return (
        taps[:, 0:1] * now
        + taps[:, 1:2] * jnp.concatenate([before[:, 1:2], now[:, :-1]], 1)
        + taps[:, 2:3] * jnp.concatenate([before, now[:, :-2]], 1)
    )


def first_tokens(states, taps):
    rows, lanes = F, 2 * DV
    lane = lax.broadcasted_iota(jnp.int32, (rows, lanes), 1)
    raw, vals = jnp.zeros((rows, lanes), f32), jnp.zeros((rows, lanes), f32)
    for b in range(states.shape[0]):
        tile = states[b, FEAT // 2 : SENT].astype(f32)
        here = (lane >= 8 * b) & (lane < 8 * (b + 1))
        raw = jnp.where(here, pltpu.roll(tile, (8 * b - SPARE) % lanes, 1), raw)
        vals = jnp.where(here, pltpu.roll(tile, (8 * b - SPARE - 8) % lanes, 1), vals)
    prev = jnp.where(lane < 8, 0.0, pltpu.roll(raw, 8, 1))
    one = jnp.where(
        lane % 4 == 0, pltpu.roll(prev, lanes - 3, 1), pltpu.roll(raw, 1, 1)
    )
    two = pltpu.roll(prev, lanes - 2, 1)
    q, k = (
        t[:, 0:1] * raw + t[:, 1:2] * one + t[:, 2:3] * two for t in (taps[:F], taps[F:])
    )
    v = jnp.concatenate(
        [vals if j == 0 else pltpu.roll(vals, lanes - 2 * j, 1) for j in range(DV // F)], 0
    )
    return q, k, v


def sum_kernel(data, out):
    total = data[0].astype(f32)
    for i in range(1, data.shape[0]):
        total = total + data[i].astype(f32)
    repeat_into(out, total.astype(bf16))


def fetch(sources, targets, sems):
    copies = [
        pltpu.make_async_copy(source, target, sems.at[i])
        for i, (source, target) in enumerate(zip(sources, targets))
    ]
    for copy in copies:
        copy.start()
    return copies


def pack_kernel(*refs):
    out, gate, cot, values, weight, tokens, sems = refs[5:]
    far_tokens, far_weight, far_values, far_gate, far_cot = refs[:5]
    copies = fetch(
        (far_gate, far_cot, far_values, far_weight, far_tokens),
        (gate, cot, values, weight, tokens),
        sems,
    )
    for copy in copies[:3]:
        copy.wait()
    g = gate[...].astype(f32)
    v = values[...].T
    up = (cot[...].astype(f32) * (g * jax.nn.sigmoid(g))).astype(bf16).T
    for h in range(H):
        cols = slice(DV * h, DV * (h + 1))
        out[h, AT_V : AT_V + DV] = v[cols]
        out[h, AT_G : AT_G + DV] = up[cols]
    for copy in copies[3:]:
        copy.wait()
    x = tokens[...]
    projected = mm(x, weight[...], NN).T.astype(bf16)
    width = H * F
    for h in range(H):
        out[h, AT_P : AT_P + F] = projected[F * h : F * (h + 1)]
        out[h, AT_P + F : ROWS] = projected[width + F * h : width + F * (h + 1)]
        for i in range(x.shape[1] // H // TOK):
            start = x.shape[1] // H * h + TOK * i
            out[h, TOK * i : TOK * (i + 1)] = x[:, start : start + TOK]


def state_kernel(place, data, conv, out, columns):
    taps = head_taps(conv, columns, place[1])[F:]
    total = jnp.zeros((FEAT, 2 * DV), f32)
    before = jnp.zeros((F, 2), f32)
    for c in range(H // WIDE):
        raw = rows_of(data, c, AT_P + F, F).astype(f32)
        feat = features(convolve(raw, before, taps))
        if c == 0:
            token = lax.broadcasted_iota(jnp.int32, feat.shape, 1)
            feat = jnp.where(token < KCONV - 1, 0.0, feat)
        before = raw[:, -2:]
        feat = feat.astype(bf16)
        v = wide_values(rows_of(data, c, AT_V, DV))
        total = total + mm(feat, v, NT)
    first, last = data[0, AT_P:ROWS], data[H - 1, AT_P:ROWS]
    begin = data[0, AT_V : AT_V + DV]
    extra = []
    for start in (F, 0):
        rows = slice(start, start + F)
        extra += [first[rows, 0:1], first[rows, 1:2]]
        extra += [last[rows, TOK - 2 : TOK - 1], last[rows, TOK - 1 : TOK]]
    for j in range(DV // F):
        rows = slice(F * j, F * (j + 1))
        extra += [begin[rows, 0:1], begin[rows, 1:2]]
    repeat_into(out, pack_state(total, extra))


def main_kernel(
    place, data, states, conv, far_out, far_saved, far_parts, far_edges, sent,
    columns, out, saved, parts, edges, sems,
):
    here = place[0]
    copies = []
    taps = head_taps(conv, columns, place[1])
    length = TOK * WIDE
    total = jnp.zeros((SENT, 2 * DV), f32)
    for b in range(states.shape[0]):
        total = total + states[b].astype(f32) * (b < here).astype(f32)
    first_q, first_k, first_v = first_tokens(states, taps)
    lane = lax.broadcasted_iota(jnp.int32, (FEAT, 2 * DV), 1)
    earlier = (lane % 8 < KCONV - 1) & (lane < 8 * here)
    feat = halves(jnp.where(earlier, features(first_k), 0.0))
    first_values = wide_values(first_v.astype(bf16))
    state = (
        unpack_state(total) + mm(feat[0], first_values, NT) + mm(feat[1], first_values, NT)
    )
    shift = 2 * DV * 2 - 8 * (here + 1)
    edges[0:F] = pltpu.roll(first_q, shift - 4, 1)
    edges[F : 2 * F] = pltpu.roll(first_k, shift, 1)
    edges[2 * F :] = pltpu.roll(first_v, shift, 1)
    copies += fetch((edges,), (far_edges,), sems.at[pl.ds(0, 1)])
    tile = states[jnp.maximum(here - 1, 0), FEAT // 2 : SENT].astype(f32)
    tile = tile * (here > 0).astype(f32)
    before = jnp.concatenate(
        [tile[:, SPARE + 6 : SPARE + 8], tile[:, SPARE + 2 : SPARE + 4]], 0
    )
    k_at = lax.broadcasted_iota(jnp.int32, (length, length), 0)
    q_at = lax.broadcasted_iota(jnp.int32, (length, length), 1)
    causal = k_at <= q_at
    whole = jnp.zeros((FEAT, 2 * DV), f32)
    for c in range(H // WIDE):
        raw = rows_of(data, c, AT_P, 2 * F).astype(f32)
        mixed = convolve(raw, before, taps)
        before = raw[:, -2:]
        q, k = mixed[:F], mixed[F:]
        (qh, ql), (kh, kl) = halves(q * F**-0.5), halves(k)
        saved[c, 2 * F : 3 * F] = k
        v = wide_values(rows_of(data, c, AT_V, DV))
        g_att = rows_of(data, c, AT_G, DV).astype(f32)
        near_one = 1.0 + mm(
            jnp.concatenate([kh, kh, kl], 0), jnp.concatenate([qh, ql, qh], 0), TN
        )
        weights = jnp.where(causal, 0.5 + 0.5 * near_one * near_one, 0.0).astype(bf16)
        q_feat, k_feat = features(q).astype(bf16), features(k).astype(bf16)
        held = state.astype(bf16)
        numer = mm(v, weights, NN) + mm(held, q_feat, TN)
        inverse = 1.0 / numer[DV : DV + 1]
        attended = numer[:DV] * inverse
        result = attended.astype(bf16)
        g_num = g_att * inverse
        g_den = -jnp.sum(g_att * attended, 0, keepdims=True) * inverse
        row = lax.broadcasted_iota(jnp.int32, (DV, length), 0)
        wide = jnp.concatenate([g_num, jnp.where(row == 0, g_den, 0.0)], 0)
        grads = halves(wide)
        g_weights = mm(v, grads[0], TN) + mm(v, grads[1], TN)
        g_scores = jnp.where(causal, g_weights * near_one, 0.0).astype(bf16)
        g_local = mm(kh, g_scores, NN) * F**-0.5
        g_query = g_local + features_back(q, mm(held, grads[0], NN))
        if c == 0:
            extra = [g_query[:, 0:1], g_query[:, 1:2]]
            for j in range(DV // F + 1):
                column = wide[F * j : F * (j + 1), 0:1]
                high = column.astype(bf16)
                extra += [high, column - high.astype(f32)]
        g_key = mm(qh, g_scores, NT)
        g_value = mm(grads[0][:DV], weights, NT)
        part = mm(q_feat, grads[0], NT)
        whole = whole + part
        parts[c] = part.astype(bf16)
        state = state + mm(k_feat, v, NT)
        for i in range(WIDE):
            cols = slice(TOK * i, TOK * (i + 1))
            out[WIDE * c + i] = result[:, cols]
        saved[c, 0:F] = g_query
        saved[c, F : 2 * F] = g_key
        saved[c, 3 * F :] = g_value
        some = slice(WIDE * c, WIDE * (c + 1))
        copies += fetch(
            (out.at[some], saved.at[c], parts.at[c]),
            (far_out.at[some], far_saved.at[c], far_parts.at[c]),
            sems.at[pl.ds(1 + 3 * c, 3)],
        )
    repeat_into(sent, pack_state(whole, extra))
    for copy in copies:
        copy.wait()


def back_kernel(
    place, states, conv, far_done, far_saved, far_parts, far_edges, far, out,
    columns, edges, data, done, saved, parts, sems,
):
    copies = fetch(
        (far_edges, far.at[:, AT_V : AT_V + DV], far_saved, far_parts, far_done),
        (edges, data, saved, parts, done),
        sems,
    )
    here = place[0]
    taps = head_taps(conv, columns, place[1])
    count = states.shape[0]
    total = jnp.zeros((SENT, 2 * DV), f32)
    for b in range(count):
        total = total + states[b].astype(f32) * (b > here).astype(f32)
    state = unpack_state(total)
    tile = states[jnp.minimum(here + 1, count - 1), FEAT // 2 : SENT].astype(f32)
    copies[0].wait()
    edge = edges[...]
    edge_v = wide_values(edge[2 * F :].astype(bf16))
    split_state = halves(state)
    column = jnp.concatenate(
        [
            tile[:, SPARE + 2 + 2 * j : SPARE + 3 + 2 * j]
            + tile[:, SPARE + 3 + 2 * j : SPARE + 4 + 2 * j]
            for j in range(DV // F + 1)
        ],
        0,
    )
    pair = jnp.sum(column * edge_v[: DV + F].astype(f32), 0, keepdims=True)
    lane = lax.broadcasted_iota(jnp.int32, (FEAT, 2 * DV), 1)
    g_feat = mm(split_state[0], edge_v, NN) + mm(split_state[1], edge_v, NN)
    g_feat = g_feat - jnp.where(lane == 1, features(edge[:F])[:, 0:1] * pair, 0.0)
    after = jnp.concatenate(
        [tile[:, SPARE : SPARE + 2], features_back(edge[F : 2 * F], g_feat)[:, 0:2]], 0
    ) * (here + 1 < count).astype(f32)
    for copy in copies[1:]:
        copy.wait()
    for c in reversed(range(H // WIDE)):
        k = saved[c, 2 * F : 3 * F]
        v = wide_values(rows_of(data, c, 0, DV))
        k_feat = features(k).astype(bf16)
        held = state.astype(bf16)
        g_key = saved[c, F : 2 * F] + features_back(k, mm(held, v, NN))
        g_value = (saved[c, 3 * F :] + mm(held, k_feat, TN)[:DV]).astype(bf16)
        state = state + parts[c].astype(f32)
        now = jnp.concatenate([saved[c, 0:F], g_key], 0)
        total = (
            taps[:, 0:1] * now
            + taps[:, 1:2] * jnp.concatenate([now[:, 1:], after[:, 0:1]], 1)
            + taps[:, 2:3] * jnp.concatenate([now[:, 2:], after], 1)
        ).astype(bf16)
        after = now[:, 0:2]
        for i in range(WIDE):
            cols = slice(TOK * i, TOK * (i + 1))
            b = WIDE * c + i
            out[b, FIRST : FIRST + DV] = done[b]
            out[b, FIRST + DV : FIRST + 2 * DV] = g_value[:, cols]
            for dest in range(H):
                out[dest, 2 * F * b : 2 * F * (b + 1)] = total[:, cols]

def stacked(grads, block):
    return jnp.concatenate(
        [
            grads[h, pl.ds(2 * F * block + at, F)]
            for at in (0, F)
            for h in range(H)
        ],
        0,
    )


def weight_kernel(place, grads, far, out, own, data, sem):
    copy = pltpu.make_async_copy(far.at[:, 0:HID], data, sem)
    copy.start()
    own[...] = stacked(grads, place[1])
    total = jnp.concatenate([stacked(grads, b) for b in range(H)], 1).T
    count, rows = out.shape[:2]
    parts = count * rows // TOK
    copy.wait()
    for i in range(parts):
        at = TOK * i
        tokens = jnp.concatenate([data[b, at : at + TOK] for b in range(H)], 0)
        result = mm(tokens, total, TN).astype(bf16)
        for j in range(count // parts):
            out[i * (count // parts) + j] = result[rows * j : rows * (j + 1)]


def join_kernel(place, part, *refs, flip):
    out, sems = refs[-2:]
    at = (place[1] + flip) % 2
    copies = fetch(
        [part.at[h] for h in range(H // 2)],
        [out.at[2 * h + at] for h in range(H // 2)],
        sems,
    )
    for copy in copies:
        copy.wait()


def hidden_kernel(own, weight, out):
    out[...] = mm(own[...].T, weight[...], NT).astype(bf16)


def unpack_kernel(data, gate, cot, output, g_gate, g_value):
    attended, values = (
        jnp.concatenate([data[h, at : at + DV] for h in range(H)], 0).T
        for at in (FIRST, FIRST + DV)
    )
    g = gate[...].astype(f32)
    sig = jax.nn.sigmoid(g)
    attended = attended.astype(f32)
    output[...] = (attended * (g * sig)).astype(bf16)
    g_gate[...] = (
        cot[...].astype(f32) * attended * sig * (1.0 + g * (1.0 - sig))
    ).astype(bf16)
    g_value[...] = values


def near(x):
    return pltpu.with_memory_space_constraint(x, pltpu.VMEM)


def call(kernel, name, out_shape, *args, scalars=0, lazy=0, far=False, results=pltpu.VMEM, scratch=(), alias={}):
    whole = pl.BlockSpec(memory_space=pltpu.VMEM)
    specs = [pl.BlockSpec(memory_space=pltpu.SMEM)] * scalars
    specs += [whole] * (len(args) - scalars - lazy)
    specs += [pl.BlockSpec(memory_space=pl.ANY)] * lazy
    if isinstance(results, tuple):
        outs = tuple(pl.BlockSpec(memory_space=r) for r in results)
    else:
        outs = jax.tree.map(lambda s: pl.BlockSpec(memory_space=results), out_shape)
    if not far:
        out_shape = jax.tree.map(lambda s: pltpu.VMEM(s.shape, s.dtype), out_shape)
    return pl.pallas_call(
        kernel,
        name=name,
        out_shape=out_shape,
        in_specs=specs,
        out_specs=outs,
        scratch_shapes=scratch,
        input_output_aliases=alias,
    )(*args)


def window(size):
    return pltpu.VMEM((H, size, TOK), bf16), pltpu.SemaphoreType.DMA(())


def shape(dims, kind):
    return jax.ShapeDtypeStruct(dims, kind)


def swap(x, axis):
    return near(lax.all_to_all(x, axis, 0, 0, tiled=True))


def body(hidden_in, qk_weight, conv_weight, values, gate_in, cotangent):
    tokens = hidden_in[0]
    supers = lax.axis_size(SUPER)
    others = lax.axis_size(OTHER)
    model = tokens.shape[1]
    chunks, width = H // WIDE, TOK * WIDE
    place = jnp.stack([lax.axis_index(SUPER), lax.axis_index(GROUP)]).astype(jnp.int32)
    taps = (pltpu.VMEM((2 * H * F, 8), f32),)
    packed = call(
        pack_kernel,
        "pack",
        shape((H, ROWS, TOK), bf16),
        tokens,
        qk_weight,
        values[0],
        gate_in[0],
        cotangent[0],
        lazy=5,
        scratch=(
            *(pltpu.VMEM((TOK, H * DV), bf16),) * 3,
            pltpu.VMEM(qk_weight.shape, bf16),
            pltpu.VMEM(tokens.shape, bf16),
            pltpu.SemaphoreType.DMA((5,)),
        ),
    )
    data = lax.all_to_all(packed, GROUP, 0, 0, tiled=True)
    own = call(
        state_kernel,
        "state",
        shape((supers, SENT, 2 * DV), bf16),
        place,
        near(data),
        conv_weight,
        scalars=1,
        scratch=taps,
    )
    done, saved, parts, edges, sent = call(
        main_kernel,
        "main",
        (
            shape((H, DV, TOK), bf16),
            shape((chunks, 3 * F + DV, width), f32),
            shape((chunks, FEAT, 2 * DV), bf16),
            shape((2 * F + DV, 2 * DV), f32),
            pltpu.VMEM((supers, SENT, 2 * DV), bf16),
        ),
        place,
        near(data),
        swap(own, SUPER),
        conv_weight,
        scalars=1,
        far=True,
        results=(pl.ANY,) * 4 + (pltpu.VMEM,),
        scratch=taps
        + (
            pltpu.VMEM((H, DV, TOK), bf16),
            pltpu.VMEM((chunks, 3 * F + DV, width), f32),
            pltpu.VMEM((chunks, FEAT, 2 * DV), bf16),
            pltpu.VMEM((2 * F + DV, 2 * DV), f32),
            pltpu.SemaphoreType.DMA((1 + 3 * chunks,)),
        ),
    )
    back = call(
        back_kernel,
        "back",
        shape((H, FIRST + 2 * DV, TOK), bf16),
        place,
        swap(sent, SUPER),
        conv_weight,
        done,
        saved,
        parts,
        edges,
        data,
        scalars=1,
        lazy=5,
        scratch=taps
        + (
            pltpu.VMEM((2 * F + DV, 2 * DV), f32),
            pltpu.VMEM((H, DV, TOK), bf16),
            pltpu.VMEM((H, DV, TOK), bf16),
            pltpu.VMEM((chunks, 3 * F + DV, width), f32),
            pltpu.VMEM((chunks, FEAT, 2 * DV), bf16),
            pltpu.SemaphoreType.DMA((5,)),
        ),
    )
    back = swap(back, GROUP)
    partial, own_grad = call(
        weight_kernel,
        "weight",
        (
            shape((others, model // H // others, 2 * H * F), bf16),
            shape((2 * H * F, TOK), bf16),
        ),
        place,
        back,
        data,
        scalars=1,
        lazy=1,
        scratch=window(HID),
    )
    deep = model // H // others
    some = swap(partial, OTHER)
    summed = call(
        sum_kernel, "sum_a", shape((lax.axis_size("z"), deep, 2 * H * F), bf16), some
    )
    summed = call(
        sum_kernel, "sum_b", shape((H // 2 * others, deep, 2 * H * F), bf16), swap(summed, "z")
    )
    mine = lax.all_to_all(summed, ("h",) + OTHER, 0, 0, tiled=True)
    mine = mine.reshape(H // 2, model // H, 2 * H * F)
    output, grad_gate, grad_values = call(
        unpack_kernel,
        "unpack",
        (shape((TOK, H * DV), bf16),) * 3,
        back,
        gate_in[0],
        cotangent[0],
        far=True,
    )
    grad_hidden = call(
        hidden_kernel,
        "hidden",
        shape((TOK, model), bf16),
        near(own_grad),
        qk_weight,
        far=True,
    )
    mine, output, grad_hidden = lax.optimization_barrier((mine, output, grad_hidden))
    theirs = lax.ppermute(mine, "core", [(0, 1), (1, 0)])
    joined = ()
    for flip, part in enumerate((mine, theirs)):
        joined = (
            call(
                functools.partial(join_kernel, flip=flip),
                f"join_{flip}",
                shape((H, model // H, 2 * H * F), bf16),
                place,
                near(part),
                *joined,
                scalars=1,
                lazy=1 + flip,
                far=True,
                results=pl.ANY,
                scratch=(pltpu.SemaphoreType.DMA((H // 2,)),),
                alias={2: 0} if flip else {},
            ),
        )
    grad_qk_weight = joined[0].reshape(model, 2 * H * F)
    return output[None], grad_hidden[None], grad_values[None], grad_gate[None], grad_qk_weight


def solution(mesh):
    pairs, blocks = mesh.devices.shape
    y = 4 if blocks // H % 4 == 0 else 1
    fine = Mesh(
        mesh.devices.reshape(pairs, y, blocks // H // y, H // 2, 2),
        ("dp", "y", "z", "h", "core"),
    )
    split = P("dp", SUPER + GROUP, None)
    return jax.shard_map(
        body,
        mesh=fine,
        in_specs=(split, P(), P(), split, split, split),
        out_specs=(split, split, split, split, P()),
        check_vma=False,
    )
```
